256 devices in a mesh: tm: 8 (over z), chan: 32 (over x, y, core).
Axes of the slice: x: 4, y: 4, z: 8, core: 2. Of those that a mesh axis runs over, the one named last changes fastest.
Arguments:
- signal: float32 [256, 16384], P('chan', 'tm'), may hold values from -6 to 6
- band: float32 [2, 16, 256], replicated, may hold values from -4 to 4
- response: float32 [2, 8, 16, 2048], P(None, 'tm', None, 'chan'), may hold values from -6 to 6
- offsets: int32 [8, 2048], P('tm', 'chan'), may hold values from 0 to 255, as said below
Outputs:
- smoothed: float32 [256, 16384], P('chan', 'tm')
The draws below stay inside these ranges and needn't reach their ends.
Inputs may be any that keep to these rules, and one draw needn't show every extreme that they name: Row c of bin k's gain holds the columns c + offsets + j, wrapping around the 256 channels; every offset lies within 8 of 0 modulo 256, and entry [p, q] is the same for all p and for all q in one run of 64 consecutive q.
All inputs are finite; a program needn't handle non-finite values.
Results may differ from the reference program's by a relative error of at most 0.0003.
Values sent between devices are 32-bit elements; how exact they have to be, the bound alone decides.
No kernel may reach another device: no remote copies, remote signals or barrier semaphores. Data moves between devices by JAX's collectives and lax.ppermute only.
A program may use at most 64 MiB of HBM per device.

```python
import jax
import jax.numpy as jnp
from jax import lax

CHANNELS = 256
BAND = 16
T_DEV = 2048
PHASES = 8
SECTIONS = 3
SAMPLES = 16384


def draw_offsets(key, part):
    run_count = 32
    drift = jax.random.randint(key, (run_count,), -(BAND // 2), BAND // 2 + 1)
    run_ids = jnp.arange(run_count, dtype=jnp.int32)
    drift = jnp.where(run_ids == 0, BAND // 2, drift)
    drift = jnp.where(run_ids == 1, -(BAND // 2), drift)
    drift = jnp.where(run_ids == 2, -1, drift)
    drift = jnp.where(run_ids == 3, 0, drift)
    value = drift % CHANNELS
    row_vals = jnp.repeat(value, T_DEV // run_count)
    return jnp.broadcast_to(row_vals[None, :], (PHASES, T_DEV)).astype(jnp.int32)


def block_levels(key, dims, cuts, least, largest):
    def one(axis_at, shards_of):
        heights = jax.random.uniform(jax.random.fold_in(jax.random.fold_in(key, 6), axis_at), (shards_of,), jnp.float32, least / len(cuts), largest / len(cuts))
        return jnp.repeat(jnp.exp(heights), dims[axis_at] // shards_of).reshape((-1,) + (1,) * (len(dims) - axis_at - 1))

    factor_of = one(*cuts[0])
    for cut in cuts[1:]:
        factor_of = factor_of * one(*cut)
    return factor_of


def bell_draw(stream_key, extent, width, limit, split=(), held_as=jnp.bfloat16):
    gain = block_levels(stream_key, extent, split, -0.22, 0.18) if split else 1.0
    values = jax.random.normal(stream_key, extent, jnp.float32) * width * gain
    return jnp.minimum(jnp.maximum(values, -limit), limit).astype(held_as)


def setup_inputs(seed: int = 0) -> dict:
    splits = jax.random.split(jax.random.key(seed), 5)
    return {
        "signal": bell_draw(splits[0], (CHANNELS, SAMPLES), 1.0, 6.0, ((0, 32), (1, 8)), jnp.float32),
        "band": bell_draw(splits[1], (2, BAND, CHANNELS), 0.3, 4.0, (), jnp.float32),
        "response": bell_draw(splits[2], (2, PHASES, BAND, T_DEV), 0.7, 6.0, ((1, 8), (3, 32)), jnp.float32),
        "offsets": draw_offsets(jax.random.fold_in(splits[4], 71), 0),
    }


def reverse_index(value, bit_count):
    result = 0
    for bit_index in range(bit_count):
        result = result + ((value >> bit_index) & 1) * (1 << (bit_count - 1 - bit_index))
    return result


def reference(signal, band, response, offsets):
    total_len = SAMPLES
    reorder = jnp.array([reverse_index(p, SECTIONS) for p in range(PHASES)], dtype=jnp.int32)
    resp_nat = response[:, reorder]
    resp_nat = jnp.transpose(resp_nat, (0, 2, 3, 1)).reshape(2, BAND, total_len)
    offset_nat = jnp.transpose(offsets[reorder], (1, 0)).reshape(total_len)
    spectrum = jnp.fft.fft(signal, axis=1)
    coefficient = band[0] + 1j * band[1]
    block_count = PHASES
    spec_blocks = jnp.transpose(spectrum.reshape(CHANNELS, block_count, T_DEV), (1, 0, 2))
    resp_blocks = jnp.transpose((resp_nat[0] + 1j * resp_nat[1]).reshape(BAND, block_count, T_DEV), (1, 0, 2))
    offset_blocks = offset_nat.reshape(block_count, T_DEV)

    def mix_block(packed):
        spec_part, resp_part, offset_row = packed
        gather_idx = (jnp.arange(CHANNELS, dtype=jnp.int32)[:, None] + offset_row[None, :]) % CHANNELS
        moved = jnp.take_along_axis(spec_part, gather_idx, axis=0)
        extended = jnp.concatenate([moved, moved[:BAND - 1]], axis=0)
        accumulated = jnp.zeros_like(spec_part)
        for lag_step in range(BAND):
            accumulated = accumulated + coefficient[lag_step][:, None] * resp_part[lag_step][None, :] * extended[lag_step:lag_step + CHANNELS]
        return accumulated

    mixed = lax.map(mix_block, (spec_blocks, resp_blocks, offset_blocks))
    mixed = jnp.transpose(mixed, (1, 0, 2)).reshape(CHANNELS, total_len)
    return jnp.real(jnp.fft.ifft(mixed, axis=1)).astype(jnp.float32)
```

```python
import math

import jax
import jax.numpy as jnp
from jax import lax
from jax.sharding import PartitionSpec as P

PRECISE = lax.Precision.HIGHEST


def from_partner(block, axis, stride):
    count = lax.axis_size(axis)
    route = []
    for low in range(count):
        high = low | 1 << stride
        if high != low and high < count:
            route += [(low, high), (high, low)]
    return lax.ppermute(block, axis, route)


def twiddle(numer, length):
    angle = -2.0 * math.pi / length * numer.astype(jnp.float32)
    return (jnp.cos(angle), jnp.sin(angle))


def dft_table(length):
    steps = lax.iota(jnp.int32, length)
    return twiddle(steps[:, None] * steps[None, :] % length, length)


def reverse_bits(value, bit_count):
    result = value * 0
    for bit_index in range(bit_count):
        result = result + value // (1 << bit_index) % 2 * (1 << bit_count - 1 - bit_index)
    return result


def complex_einsum(form, left_real, left_imag, right_real, right_imag):
    out_real = jnp.einsum(form, left_real, right_real, precision=PRECISE) - jnp.einsum(
        form, left_imag, right_imag, precision=PRECISE
    )
    out_imag = jnp.einsum(form, left_real, right_imag, precision=PRECISE) + jnp.einsum(
        form, left_imag, right_real, precision=PRECISE
    )
    return (out_real, out_imag)


def forward_local(real_part, imag_part, phase_bin, total_len, inner_len):
    channel_count, length = real_part.shape
    outer_len = length // inner_len
    sample_pos = lax.iota(jnp.int32, length)
    cosine, sine_part = twiddle(sample_pos * phase_bin % total_len, total_len)
    real_part, imag_part = (
        real_part * cosine - imag_part * sine_part,
        real_part * sine_part + imag_part * cosine,
    )
    real_part = real_part.reshape(channel_count, inner_len, outer_len)
    imag_part = imag_part.reshape(channel_count, inner_len, outer_len)
    table_real, table_imag = dft_table(inner_len)
    real_part, imag_part = complex_einsum(
        "cab,ak->cbk", real_part, imag_part, table_real, table_imag
    )
    outer_ids = lax.iota(jnp.int32, outer_len)[:, None]
    inner_ids = lax.iota(jnp.int32, inner_len)[None, :]
    cosine, sine_part = twiddle(outer_ids * inner_ids, length)
    real_part, imag_part = (
        real_part * cosine - imag_part * sine_part,
        real_part * sine_part + imag_part * cosine,
    )
    table_real, table_imag = dft_table(outer_len)
    return complex_einsum("cbk,bm->mck", real_part, imag_part, table_real, table_imag)


def inverse_local(spec_real, spec_imag, phase_bin, total_len):
    outer_len, channel_count, inner_len = spec_real.shape
    length = outer_len * inner_len
    table_real, table_imag = dft_table(outer_len)
    real_part, imag_part = complex_einsum(
        "mck,mb->cbk", spec_real, spec_imag, table_real, -table_imag
    )
    outer_ids = lax.iota(jnp.int32, outer_len)[:, None]
    inner_ids = lax.iota(jnp.int32, inner_len)[None, :]
    cosine, sine_part = twiddle(outer_ids * inner_ids, length)
    sine_part = -sine_part
    real_part, imag_part = (
        real_part * cosine - imag_part * sine_part,
        real_part * sine_part + imag_part * cosine,
    )
    table_real, table_imag = dft_table(inner_len)
    real_part, imag_part = complex_einsum(
        "cbk,ka->cab", real_part, imag_part, table_real, -table_imag
    )
    real_part = real_part.reshape(channel_count, length)
    imag_part = imag_part.reshape(channel_count, length)
    sample_pos = lax.iota(jnp.int32, length)
    cosine, sine_part = twiddle(sample_pos * phase_bin % total_len, total_len)
    sine_part = -sine_part
    return (real_part * cosine - imag_part * sine_part, real_part * sine_part + imag_part * cosine)


def mix_bins(spread, band, response, offsets):
    fine_len, channel_all, inner_len = (spread.shape[1], spread.shape[2], spread.shape[3])
    band_width = band.shape[1]
    half_width = band_width // 2
    shift_cols = offsets.reshape(1, fine_len, 1, inner_len)
    centered = (shift_cols + half_width) % channel_all - half_width
    moved = jnp.zeros_like(spread)
    for shift_amount in range(-half_width, half_width + 1):
        rolled = jnp.roll(spread, -shift_amount, axis=2)
        moved = jnp.where(centered == shift_amount, rolled, moved)
    moved_real = moved[0]
    moved_imag = moved[1]
    wide_real = jnp.concatenate([moved_real, moved_real[:, : band_width - 1]], axis=1)
    wide_imag = jnp.concatenate([moved_imag, moved_imag[:, : band_width - 1]], axis=1)
    responses = response.reshape(2, band_width, fine_len, 1, inner_len)
    acc_real = jnp.zeros_like(moved_real)
    acc_imag = jnp.zeros_like(moved_imag)
    for lag_index in range(band_width):
        value_real = wide_real[:, lag_index : lag_index + channel_all]
        value_imag = wide_imag[:, lag_index : lag_index + channel_all]
        gain_real = band[0, lag_index][None, :, None]
        gain_imag = band[1, lag_index][None, :, None]
        coef_real = gain_real * responses[0, lag_index] - gain_imag * responses[1, lag_index]
        coef_imag = gain_real * responses[1, lag_index] + gain_imag * responses[0, lag_index]
        acc_real = acc_real + coef_real * value_real - coef_imag * value_imag
        acc_imag = acc_imag + coef_real * value_imag + coef_imag * value_real
    return (acc_real, acc_imag)


def per_device(signal, band, response, offsets):
    blocks = lax.axis_size("tm")
    levels = blocks.bit_length() - 1
    device_pos = lax.axis_index("tm")
    phase_bin = reverse_bits(device_pos, levels)
    channel_count, length = signal.shape
    total_len = length * blocks
    inner_len = math.gcd(128, length // lax.axis_size("chan"))
    piece = length // blocks
    block_ids = lax.iota(jnp.int32, blocks)
    residues = reverse_bits(block_ids, levels)
    pieces = signal.reshape(channel_count, blocks, piece).transpose(1, 0, 2)
    gathered = lax.all_to_all(pieces, "tm", 0, 0, tiled=True)
    cosine, sine_part = twiddle(residues[:, None] * block_ids[None, :] % blocks, blocks)
    part_real = jnp.einsum("rb,bcs->rcs", cosine, gathered, precision=PRECISE)
    part_imag = jnp.einsum("rb,bcs->rcs", sine_part, gathered, precision=PRECISE)
    sent = jnp.stack([part_real, part_imag], axis=1)
    spread_time = lax.all_to_all(sent, "tm", 0, 0, tiled=True)
    real_part = spread_time[:, 0].transpose(1, 0, 2).reshape(channel_count, length)
    imag_part = spread_time[:, 1].transpose(1, 0, 2).reshape(channel_count, length)
    spec_real, spec_imag = forward_local(real_part, imag_part, phase_bin, total_len, inner_len)
    spread = lax.all_to_all(
        jnp.stack([spec_real, spec_imag]), "chan", split_axis=1, concat_axis=2, tiled=True
    )
    mixed_real, mixed_imag = mix_bins(spread, band, response, offsets)
    returned = lax.all_to_all(
        jnp.stack([mixed_real, mixed_imag]), "chan", split_axis=2, concat_axis=1, tiled=True
    )
    real_part, imag_part = inverse_local(returned[0], returned[1], phase_bin, total_len)
    back = jnp.stack(
        [
            real_part.reshape(channel_count, blocks, piece).transpose(1, 0, 2),
            imag_part.reshape(channel_count, blocks, piece).transpose(1, 0, 2),
        ],
        axis=1,
    )
    by_residue = lax.all_to_all(back, "tm", 0, 0, tiled=True)
    cosine, sine_part = twiddle(block_ids[:, None] * residues[None, :] % blocks, blocks)
    combined = jnp.einsum(
        "br,rcs->bcs", cosine, by_residue[:, 0], precision=PRECISE
    ) + jnp.einsum("br,rcs->bcs", sine_part, by_residue[:, 1], precision=PRECISE)
    returned_time = lax.all_to_all(combined, "tm", 0, 0, tiled=True)
    smoothed = returned_time.transpose(1, 0, 2).reshape(channel_count, length)
    return smoothed / total_len


def solution(mesh):
    in_specs = (P("chan", "tm"), P(), P(None, "tm", None, "chan"), P("tm", "chan"))
    out_specs = P("chan", "tm")
    return jax.shard_map(
        per_device, mesh=mesh, in_specs=in_specs, out_specs=out_specs, check_vma=False
    )
```

```python
import math

import jax
import jax.numpy as jnp
from jax import lax
from jax.sharding import PartitionSpec as P

PRECISE = lax.Precision.HIGHEST


def from_partner(block, axis, stride):
    count = lax.axis_size(axis)
    route = []
    for low in range(count):
        high = low | 1 << stride
        if high != low and high < count:
            route += [(low, high), (high, low)]
    return lax.ppermute(block, axis, route)


def twiddle(numer, length):
    angle = -2.0 * math.pi / length * numer.astype(jnp.float32)
    return (jnp.cos(angle), jnp.sin(angle))


def dft_table(length):
    steps = lax.iota(jnp.int32, length)
    return twiddle(steps[:, None] * steps[None, :] % length, length)


def reverse_bits(value, bit_count):
    result = value * 0
    for bit_index in range(bit_count):
        result = result + value // (1 << bit_index) % 2 * (1 << bit_count - 1 - bit_index)
    return result


def complex_einsum(form, left_real, left_imag, right_real, right_imag):
    out_real = jnp.einsum(form, left_real, right_real, precision=PRECISE) - jnp.einsum(
        form, left_imag, right_imag, precision=PRECISE
    )
    out_imag = jnp.einsum(form, left_real, right_imag, precision=PRECISE) + jnp.einsum(
        form, left_imag, right_real, precision=PRECISE
    )
    return (out_real, out_imag)


def forward_local(real_part, imag_part, phase_bin, total_len, inner_len):
    channel_count, length = real_part.shape
    outer_len = length // inner_len
    sample_pos = lax.iota(jnp.int32, length)
    cosine, sine_part = twiddle(sample_pos * phase_bin % total_len, total_len)
    real_part, imag_part = (
        real_part * cosine - imag_part * sine_part,
        real_part * sine_part + imag_part * cosine,
    )
    real_part = real_part.reshape(channel_count, inner_len, outer_len)
    imag_part = imag_part.reshape(channel_count, inner_len, outer_len)
    table_real, table_imag = dft_table(inner_len)
    real_part, imag_part = complex_einsum(
        "cab,ak->cbk", real_part, imag_part, table_real, table_imag
    )
    outer_ids = lax.iota(jnp.int32, outer_len)[:, None]
    inner_ids = lax.iota(jnp.int32, inner_len)[None, :]
    cosine, sine_part = twiddle(outer_ids * inner_ids, length)
    real_part, imag_part = (
        real_part * cosine - imag_part * sine_part,
        real_part * sine_part + imag_part * cosine,
    )
    table_real, table_imag = dft_table(outer_len)
    return complex_einsum("cbk,bm->mck", real_part, imag_part, table_real, table_imag)


def inverse_local(spec_real, spec_imag, phase_bin, total_len):
    outer_len, channel_count, inner_len = spec_real.shape
    length = outer_len * inner_len
    table_real, table_imag = dft_table(outer_len)
    real_part, imag_part = complex_einsum(
        "mck,mb->cbk", spec_real, spec_imag, table_real, -table_imag
    )
    outer_ids = lax.iota(jnp.int32, outer_len)[:, None]
    inner_ids = lax.iota(jnp.int32, inner_len)[None, :]
    cosine, sine_part = twiddle(outer_ids * inner_ids, length)
    sine_part = -sine_part
    real_part, imag_part = (
        real_part * cosine - imag_part * sine_part,
        real_part * sine_part + imag_part * cosine,
    )
    table_real, table_imag = dft_table(inner_len)
    real_part, imag_part = complex_einsum(
        "cbk,ka->cab", real_part, imag_part, table_real, -table_imag
    )
    real_part = real_part.reshape(channel_count, length)
    imag_part = imag_part.reshape(channel_count, length)
    sample_pos = lax.iota(jnp.int32, length)
    cosine, sine_part = twiddle(sample_pos * phase_bin % total_len, total_len)
    sine_part = -sine_part
    return (real_part * cosine - imag_part * sine_part, real_part * sine_part + imag_part * cosine)


def from_offset(block, axis, delta):
    count = lax.axis_size(axis)
    return lax.ppermute(block, axis, [((i + delta) % count, i) for i in range(count)])


def mix_halo(window, band_rows, table, halo_below, channel_all):
    _, outer_len, _, inner_len = window.shape
    band_width = band_rows.shape[1]
    half_width = band_width // 2
    own = band_rows.shape[2]
    span = own + band_width - 1
    if table.shape[0] != outer_len:
        rows = table.shape[1]
        table = table.transpose(1, 0, 2).reshape(rows, outer_len, inner_len).transpose(1, 0, 2)
    responses = table[:, : 2 * band_width].reshape(outer_len, 2, band_width, inner_len)
    shift = table[:, 2 * band_width].astype(jnp.int32)
    centered = (shift + half_width) % channel_all - half_width
    moved = jnp.zeros(window.shape[:2] + (span, inner_len), window.dtype)
    for shift_amount in range(-half_width, half_width + 1):
        lo = halo_below + shift_amount
        piece = window[:, :, lo : lo + span]
        moved = jnp.where((centered == shift_amount)[None, :, None, :], piece, moved)
    acc_real = jnp.zeros((outer_len, own, inner_len), window.dtype)
    acc_imag = jnp.zeros((outer_len, own, inner_len), window.dtype)
    for lag_index in range(band_width):
        value_real = moved[0, :, lag_index : lag_index + own]
        value_imag = moved[1, :, lag_index : lag_index + own]
        gain_real = band_rows[0, lag_index][None, :, None]
        gain_imag = band_rows[1, lag_index][None, :, None]
        resp_real = responses[:, 0, lag_index][:, None, :]
        resp_imag = responses[:, 1, lag_index][:, None, :]
        coef_real = gain_real * resp_real - gain_imag * resp_imag
        coef_imag = gain_real * resp_imag + gain_imag * resp_real
        acc_real = acc_real + coef_real * value_real - coef_imag * value_imag
        acc_imag = acc_imag + coef_real * value_imag + coef_imag * value_real
    return (acc_real, acc_imag)


def per_device(signal, band, response, offsets):
    blocks = lax.axis_size("tm")
    levels = blocks.bit_length() - 1
    device_pos = lax.axis_index("tm")
    phase_bin = reverse_bits(device_pos, levels)
    channel_count, length = signal.shape
    total_len = length * blocks
    inner_len = math.gcd(128, length // lax.axis_size("chan"))
    real_part = signal
    imag_part = jnp.zeros_like(signal)
    for bit_index in range(levels - 1, -1, -1):
        half_span = 1 << bit_index
        partner = from_partner(jnp.stack([real_part, imag_part]), "tm", bit_index)
        upper_half = device_pos // half_span % 2 == 1
        cosine, sine_part = twiddle(device_pos % half_span, 2 * half_span)
        diff_real = partner[0] - real_part
        diff_imag = partner[1] - imag_part
        new_real = jnp.where(
            upper_half, diff_real * cosine - diff_imag * sine_part, real_part + partner[0]
        )
        new_imag = jnp.where(
            upper_half, diff_real * sine_part + diff_imag * cosine, imag_part + partner[1]
        )
        real_part, imag_part = (new_real, new_imag)
    spec_real, spec_imag = forward_local(real_part, imag_part, phase_bin, total_len, inner_len)
    own = channel_count
    band_width = band.shape[1]
    chan_pos = lax.axis_index("chan")
    band_rows = lax.dynamic_slice_in_dim(band, chan_pos * own, own, axis=2)
    packed = jnp.concatenate(
        [response.reshape(2 * band_width, -1), offsets.reshape(1, -1).astype(jnp.float32)], axis=0
    )
    table = lax.all_gather(packed, "chan")
    spectra = jnp.stack([spec_real, spec_imag])
    neighbours = [from_offset(spectra, "chan", delta) for delta in (-1, 1, 2, 3)]
    window = jnp.concatenate([neighbours[0], spectra] + neighbours[1:], axis=2)
    mixed_real, mixed_imag = mix_halo(window, band_rows, table, own, band.shape[2])
    real_part, imag_part = inverse_local(mixed_real, mixed_imag, phase_bin, total_len)
    for bit_index in range(levels):
        half_span = 1 << bit_index
        partner = from_partner(jnp.stack([real_part, imag_part]), "tm", bit_index)
        upper_half = device_pos // half_span % 2 == 1
        cosine, sine_part = twiddle(device_pos % half_span, 2 * half_span)
        sine_part = -sine_part
        base_real = jnp.where(upper_half, partner[0], real_part)
        base_imag = jnp.where(upper_half, partner[1], imag_part)
        scaled_real = jnp.where(upper_half, real_part, partner[0])
        scaled_imag = jnp.where(upper_half, imag_part, partner[1])
        prod_real = scaled_real * cosine - scaled_imag * sine_part
        prod_imag = scaled_real * sine_part + scaled_imag * cosine
        real_part = jnp.where(upper_half, base_real - prod_real, base_real + prod_real)
        imag_part = jnp.where(upper_half, base_imag - prod_imag, base_imag + prod_imag)
    smoothed = real_part / total_len
    return smoothed


def solution(mesh):
    in_specs = (P("chan", "tm"), P(), P(None, "tm", None, "chan"), P("tm", "chan"))
    out_specs = P("chan", "tm")
    return jax.shard_map(
        per_device, mesh=mesh, in_specs=in_specs, out_specs=out_specs, check_vma=False
    )
```

```python
import math

import jax
import jax.numpy as jnp
from jax import lax
from jax.sharding import PartitionSpec as P

PRECISE = lax.Precision.HIGHEST


def from_partner(block, axis, stride):
    count = lax.axis_size(axis)
    route = []
    for low in range(count):
        high = low | 1 << stride
        if high != low and high < count:
            route += [(low, high), (high, low)]
    return lax.ppermute(block, axis, route)


def twiddle(numer, length):
    angle = -2.0 * math.pi / length * numer.astype(jnp.float32)
    return (jnp.cos(angle), jnp.sin(angle))


def dft_table(length):
    steps = lax.iota(jnp.int32, length)
    return twiddle(steps[:, None] * steps[None, :] % length, length)


def reverse_bits(value, bit_count):
    result = value * 0
    for bit_index in range(bit_count):
        result = result + value // (1 << bit_index) % 2 * (1 << bit_count - 1 - bit_index)
    return result


def complex_einsum(form, left_real, left_imag, right_real, right_imag):
    out_real = jnp.einsum(form, left_real, right_real, precision=PRECISE) - jnp.einsum(
        form, left_imag, right_imag, precision=PRECISE
    )
    out_imag = jnp.einsum(form, left_real, right_imag, precision=PRECISE) + jnp.einsum(
        form, left_imag, right_real, precision=PRECISE
    )
    return (out_real, out_imag)


def forward_local(real_part, imag_part, phase_bin, total_len, inner_len):
    channel_count, length = real_part.shape
    outer_len = length // inner_len
    sample_pos = lax.iota(jnp.int32, length)
    cosine, sine_part = twiddle(sample_pos * phase_bin % total_len, total_len)
    real_part, imag_part = (
        real_part * cosine - imag_part * sine_part,
        real_part * sine_part + imag_part * cosine,
    )
    real_part = real_part.reshape(channel_count, inner_len, outer_len)
    imag_part = imag_part.reshape(channel_count, inner_len, outer_len)
    table_real, table_imag = dft_table(inner_len)
    real_part, imag_part = complex_einsum(
        "cab,ak->cbk", real_part, imag_part, table_real, table_imag
    )
    outer_ids = lax.iota(jnp.int32, outer_len)[:, None]
    inner_ids = lax.iota(jnp.int32, inner_len)[None, :]
    cosine, sine_part = twiddle(outer_ids * inner_ids, length)
    real_part, imag_part = (
        real_part * cosine - imag_part * sine_part,
        real_part * sine_part + imag_part * cosine,
    )
    table_real, table_imag = dft_table(outer_len)
    return complex_einsum("cbk,bm->mck", real_part, imag_part, table_real, table_imag)


def inverse_local(spec_real, spec_imag, phase_bin, total_len):
    outer_len, channel_count, inner_len = spec_real.shape
    length = outer_len * inner_len
    table_real, table_imag = dft_table(outer_len)
    real_part, imag_part = complex_einsum(
        "mck,mb->cbk", spec_real, spec_imag, table_real, -table_imag
    )
    outer_ids = lax.iota(jnp.int32, outer_len)[:, None]
    inner_ids = lax.iota(jnp.int32, inner_len)[None, :]
    cosine, sine_part = twiddle(outer_ids * inner_ids, length)
    sine_part = -sine_part
    real_part, imag_part = (
        real_part * cosine - imag_part * sine_part,
        real_part * sine_part + imag_part * cosine,
    )
    table_real, table_imag = dft_table(inner_len)
    real_part, imag_part = complex_einsum(
        "cbk,ka->cab", real_part, imag_part, table_real, -table_imag
    )
    real_part = real_part.reshape(channel_count, length)
    imag_part = imag_part.reshape(channel_count, length)
    sample_pos = lax.iota(jnp.int32, length)
    cosine, sine_part = twiddle(sample_pos * phase_bin % total_len, total_len)
    sine_part = -sine_part
    return (real_part * cosine - imag_part * sine_part, real_part * sine_part + imag_part * cosine)


def from_offset(block, axis, delta):
    count = lax.axis_size(axis)
    return lax.ppermute(block, axis, [((i + delta) % count, i) for i in range(count)])


def gather_doubling(block, axis):
    count = lax.axis_size(axis)
    me = lax.axis_index(axis)
    stride = 1
    while stride < count:
        partner = from_partner(block, axis, stride.bit_length() - 1)
        upper = me // stride % 2 == 1
        block = jnp.where(upper, jnp.concatenate([partner, block]), jnp.concatenate([block, partner]))
        stride *= 2
    return block


def mix_halo(window, band_rows, table, halo_below, channel_all):
    _, outer_len, _, inner_len = window.shape
    band_width = band_rows.shape[1]
    half_width = band_width // 2
    own = band_rows.shape[2]
    span = own + band_width - 1
    if table.shape[0] != outer_len:
        rows = table.shape[1]
        table = table.transpose(1, 0, 2).reshape(rows, outer_len, inner_len).transpose(1, 0, 2)
    responses = table[:, : 2 * band_width].reshape(outer_len, 2, band_width, inner_len)
    shift = table[:, 2 * band_width].astype(jnp.int32)
    centered = (shift + half_width) % channel_all - half_width
    moved = jnp.zeros(window.shape[:2] + (span, inner_len), window.dtype)
    for shift_amount in range(-half_width, half_width + 1):
        lo = halo_below + shift_amount
        piece = window[:, :, lo : lo + span]
        moved = jnp.where((centered == shift_amount)[None, :, None, :], piece, moved)
    acc_real = jnp.zeros((outer_len, own, inner_len), window.dtype)
    acc_imag = jnp.zeros((outer_len, own, inner_len), window.dtype)
    for lag_index in range(band_width):
        value_real = moved[0, :, lag_index : lag_index + own]
        value_imag = moved[1, :, lag_index : lag_index + own]
        gain_real = band_rows[0, lag_index][None, :, None]
        gain_imag = band_rows[1, lag_index][None, :, None]
        resp_real = responses[:, 0, lag_index][:, None, :]
        resp_imag = responses[:, 1, lag_index][:, None, :]
        coef_real = gain_real * resp_real - gain_imag * resp_imag
        coef_imag = gain_real * resp_imag + gain_imag * resp_real
        acc_real = acc_real + coef_real * value_real - coef_imag * value_imag
        acc_imag = acc_imag + coef_real * value_imag + coef_imag * value_real
    return (acc_real, acc_imag)


def per_device(signal, band, response, offsets):
    blocks = lax.axis_size("tm")
    levels = blocks.bit_length() - 1
    device_pos = lax.axis_index("tm")
    phase_bin = reverse_bits(device_pos, levels)
    channel_count, length = signal.shape
    total_len = length * blocks
    inner_len = math.gcd(128, length // lax.axis_size("chan"))
    real_part = signal
    imag_part = jnp.zeros_like(signal)
    for bit_index in range(levels - 1, -1, -1):
        half_span = 1 << bit_index
        partner = from_partner(jnp.stack([real_part, imag_part]), "tm", bit_index)
        upper_half = device_pos // half_span % 2 == 1
        cosine, sine_part = twiddle(device_pos % half_span, 2 * half_span)
        diff_real = partner[0] - real_part
        diff_imag = partner[1] - imag_part
        new_real = jnp.where(
            upper_half, diff_real * cosine - diff_imag * sine_part, real_part + partner[0]
        )
        new_imag = jnp.where(
            upper_half, diff_real * sine_part + diff_imag * cosine, imag_part + partner[1]
        )
        real_part, imag_part = (new_real, new_imag)
    spec_real, spec_imag = forward_local(real_part, imag_part, phase_bin, total_len, inner_len)
    own = channel_count
    band_width = band.shape[1]
    chan_pos = lax.axis_index("chan")
    band_rows = lax.dynamic_slice_in_dim(band, chan_pos * own, own, axis=2)
    packed = jnp.concatenate(
        [response.reshape(2 * band_width, -1), offsets.reshape(1, -1).astype(jnp.float32)], axis=0
    )
    table = gather_doubling(packed[None], "chan")
    spectra = jnp.stack([spec_real, spec_imag])
    neighbours = [from_offset(spectra, "chan", delta) for delta in (-1, 1, 2, 3)]
    window = jnp.concatenate([neighbours[0], spectra] + neighbours[1:], axis=2)
    mixed_real, mixed_imag = mix_halo(window, band_rows, table, own, band.shape[2])
    real_part, imag_part = inverse_local(mixed_real, mixed_imag, phase_bin, total_len)
    for bit_index in range(levels):
        half_span = 1 << bit_index
        partner = from_partner(jnp.stack([real_part, imag_part]), "tm", bit_index)
        upper_half = device_pos // half_span % 2 == 1
        cosine, sine_part = twiddle(device_pos % half_span, 2 * half_span)
        sine_part = -sine_part
        base_real = jnp.where(upper_half, partner[0], real_part)
        base_imag = jnp.where(upper_half, partner[1], imag_part)
        scaled_real = jnp.where(upper_half, real_part, partner[0])
        scaled_imag = jnp.where(upper_half, imag_part, partner[1])
        prod_real = scaled_real * cosine - scaled_imag * sine_part
        prod_imag = scaled_real * sine_part + scaled_imag * cosine
        real_part = jnp.where(upper_half, base_real - prod_real, base_real + prod_real)
        imag_part = jnp.where(upper_half, base_imag - prod_imag, base_imag + prod_imag)
    smoothed = real_part / total_len
    return smoothed


def solution(mesh):
    in_specs = (P("chan", "tm"), P(), P(None, "tm", None, "chan"), P("tm", "chan"))
    out_specs = P("chan", "tm")
    return jax.shard_map(
        per_device, mesh=mesh, in_specs=in_specs, out_specs=out_specs, check_vma=False
    )
```

```python
import math

import jax
import jax.numpy as jnp
from jax import lax
from jax.experimental import pallas as pl
from jax.experimental.pallas import tpu as pltpu
from jax.sharding import PartitionSpec as P

PRECISE = lax.Precision.HIGHEST


def from_partner(block, axis, stride):
    count = lax.axis_size(axis)
    route = []
    for low in range(count):
        high = low | 1 << stride
        if high != low and high < count:
            route += [(low, high), (high, low)]
    return lax.ppermute(block, axis, route)


def twiddle(numer, length):
    angle = -2.0 * math.pi / length * numer.astype(jnp.float32)
    return (jnp.cos(angle), jnp.sin(angle))


def dft_table(length):
    steps = lax.iota(jnp.int32, length)
    return twiddle(steps[:, None] * steps[None, :] % length, length)


def reverse_bits(value, bit_count):
    result = value * 0
    for bit_index in range(bit_count):
        result = result + value // (1 << bit_index) % 2 * (1 << bit_count - 1 - bit_index)
    return result


def complex_einsum(form, left_real, left_imag, right_real, right_imag):
    out_real = jnp.einsum(form, left_real, right_real, precision=PRECISE) - jnp.einsum(
        form, left_imag, right_imag, precision=PRECISE
    )
    out_imag = jnp.einsum(form, left_real, right_imag, precision=PRECISE) + jnp.einsum(
        form, left_imag, right_real, precision=PRECISE
    )
    return (out_real, out_imag)


def forward_local(real_part, imag_part, phase_bin, total_len, inner_len):
    channel_count, length = real_part.shape
    outer_len = length // inner_len
    sample_pos = lax.iota(jnp.int32, length)
    cosine, sine_part = twiddle(sample_pos * phase_bin % total_len, total_len)
    real_part, imag_part = (
        real_part * cosine - imag_part * sine_part,
        real_part * sine_part + imag_part * cosine,
    )
    real_part = real_part.reshape(channel_count, inner_len, outer_len)
    imag_part = imag_part.reshape(channel_count, inner_len, outer_len)
    table_real, table_imag = dft_table(inner_len)
    real_part, imag_part = complex_einsum(
        "cab,ak->cbk", real_part, imag_part, table_real, table_imag
    )
    outer_ids = lax.iota(jnp.int32, outer_len)[:, None]
    inner_ids = lax.iota(jnp.int32, inner_len)[None, :]
    cosine, sine_part = twiddle(outer_ids * inner_ids, length)
    real_part, imag_part = (
        real_part * cosine - imag_part * sine_part,
        real_part * sine_part + imag_part * cosine,
    )
    table_real, table_imag = dft_table(outer_len)
    return complex_einsum("cbk,bm->mck", real_part, imag_part, table_real, table_imag)


def inverse_local(spec_real, spec_imag, phase_bin, total_len):
    outer_len, channel_count, inner_len = spec_real.shape
    length = outer_len * inner_len
    table_real, table_imag = dft_table(outer_len)
    real_part, imag_part = complex_einsum(
        "mck,mb->cbk", spec_real, spec_imag, table_real, -table_imag
    )
    outer_ids = lax.iota(jnp.int32, outer_len)[:, None]
    inner_ids = lax.iota(jnp.int32, inner_len)[None, :]
    cosine, sine_part = twiddle(outer_ids * inner_ids, length)
    sine_part = -sine_part
    real_part, imag_part = (
        real_part * cosine - imag_part * sine_part,
        real_part * sine_part + imag_part * cosine,
    )
    table_real, table_imag = dft_table(inner_len)
    real_part, imag_part = complex_einsum(
        "cbk,ka->cab", real_part, imag_part, table_real, -table_imag
    )
    real_part = real_part.reshape(channel_count, length)
    imag_part = imag_part.reshape(channel_count, length)
    sample_pos = lax.iota(jnp.int32, length)
    cosine, sine_part = twiddle(sample_pos * phase_bin % total_len, total_len)
    sine_part = -sine_part
    return (real_part * cosine - imag_part * sine_part, real_part * sine_part + imag_part * cosine)


LANES = 128


def cdot(left_real, left_imag, right_real, right_imag):
    def dot(a, b):
        return jnp.dot(a, b, precision=PRECISE, preferred_element_type=jnp.float32)

    return (
        dot(left_real, right_real) - dot(left_imag, right_imag),
        dot(left_real, right_imag) + dot(left_imag, right_real),
    )


def forward_kernel(xr_ref, xi_ref, twr_ref, twi_ref, kr_ref, ki_ref, t2r_ref, t2i_ref, wr_ref, wi_ref, yr_ref, yi_ref):
    own, outer, inner = xr_ref.shape
    xr = xr_ref[...]
    xi = xi_ref[...]
    twr = twr_ref[...][None]
    twi = twi_ref[...][None]
    ur = (xr * twr - xi * twi).reshape(own * outer, inner)
    ui = (xr * twi + xi * twr).reshape(own * outer, inner)
    zr, zi = cdot(kr_ref[...], ki_ref[...], ur, ui)
    t2r = t2r_ref[...]
    t2i = t2i_ref[...]
    zr, zi = (zr * t2r - zi * t2i, zr * t2i + zi * t2r)
    yr, yi = cdot(zr, zi, wr_ref[...], wi_ref[...])
    yr_ref[...] = yr.reshape(own, outer, inner)
    yi_ref[...] = yi.reshape(own, outer, inner)


def inverse_kernel(win_ref, shift_ref, resp_ref, band_ref, twr_ref, twi_ref, kr_ref, ki_ref, t2r_ref, t2i_ref, wr_ref, wi_ref, xr_ref, xi_ref):
    own, outer, inner = xr_ref.shape
    band_width = resp_ref.shape[1]
    half_width = band_width // 2
    span = own + band_width - 1
    shift = shift_ref[...]
    masks = [shift == amount for amount in range(-half_width, half_width + 1)]
    moved = []
    for row in range(span):
        mr = jnp.zeros((outer, inner), jnp.float32)
        mi = jnp.zeros((outer, inner), jnp.float32)
        for index, amount in enumerate(range(-half_width, half_width + 1)):
            source = own + amount + row
            mr = jnp.where(masks[index], win_ref[0, source], mr)
            mi = jnp.where(masks[index], win_ref[1, source], mi)
        moved.append((mr, mi))
    rows_real = []
    rows_imag = []
    for channel in range(own):
        acc_r = jnp.zeros((outer, inner), jnp.float32)
        acc_i = jnp.zeros((outer, inner), jnp.float32)
        for lag in range(band_width):
            br = band_ref[lag * own + channel]
            bi = band_ref[(band_width + lag) * own + channel]
            rr = resp_ref[0, lag]
            ri = resp_ref[1, lag]
            cr = br * rr - bi * ri
            ci = br * ri + bi * rr
            vr, vi = moved[channel + lag]
            acc_r = acc_r + cr * vr - ci * vi
            acc_i = acc_i + cr * vi + ci * vr
        rows_real.append(acc_r)
        rows_imag.append(acc_i)
    mr = jnp.concatenate(rows_real, axis=0)
    mi = jnp.concatenate(rows_imag, axis=0)
    yr, yi = cdot(mr, mi, wr_ref[...], -wi_ref[...])
    t2r = t2r_ref[...]
    t2i = -t2i_ref[...]
    yr, yi = (yr * t2r - yi * t2i, yr * t2i + yi * t2r)
    xr, xi = cdot(kr_ref[...], -ki_ref[...], yr, yi)
    xr = xr.reshape(own, outer, inner)
    xi = xi.reshape(own, outer, inner)
    twr = twr_ref[...][None]
    twi = -twi_ref[...][None]
    xr_ref[...] = xr * twr - xi * twi
    xi_ref[...] = xr * twi + xi * twr


def local_tables(own, outer, inner, phase_bin, total_len):
    length = outer * inner
    rows = lax.iota(jnp.int32, outer)[:, None]
    cols = lax.iota(jnp.int32, inner)[None, :]
    twr, twi = twiddle((rows * inner + cols) * phase_bin % total_len, total_len)
    small_r, small_i = dft_table(outer)
    eye = jnp.eye(own, dtype=jnp.float32)
    kr = jnp.kron(eye, small_r)
    ki = jnp.kron(eye, small_i)
    t2r, t2i = twiddle(rows * cols % length, length)
    t2r = jnp.tile(t2r, (own, 1))
    t2i = jnp.tile(t2i, (own, 1))
    wr, wi = dft_table(inner)
    return (twr, twi, kr, ki, t2r, t2i, wr, wi)


def vmem_specs(count):
    return [pl.BlockSpec(memory_space=pltpu.VMEM)] * count


def forward_call(xr, xi, tables):
    shape = jax.ShapeDtypeStruct(xr.shape, jnp.float32)
    return pl.pallas_call(
        forward_kernel,
        out_shape=(shape, shape),
        in_specs=vmem_specs(2 + len(tables)),
        out_specs=tuple(vmem_specs(2)),
    )(xr, xi, *tables)


def inverse_call(window, shift, responses, band_flat, tables, own):
    shape = jax.ShapeDtypeStruct((own,) + window.shape[2:], jnp.float32)
    specs = vmem_specs(3) + [pl.BlockSpec(memory_space=pltpu.SMEM)] + vmem_specs(len(tables))
    return pl.pallas_call(
        inverse_kernel,
        out_shape=(shape, shape),
        in_specs=specs,
        out_specs=tuple(vmem_specs(2)),
    )(window, shift, responses, band_flat, *tables)


def from_offset(block, axis, delta):
    count = lax.axis_size(axis)
    return lax.ppermute(block, axis, [((i + delta) % count, i) for i in range(count)])


def gather_doubling(block, axis):
    count = lax.axis_size(axis)
    me = lax.axis_index(axis)
    stride = 1
    while stride < count:
        partner = from_partner(block, axis, stride.bit_length() - 1)
        upper = me // stride % 2 == 1
        block = jnp.where(upper, jnp.concatenate([partner, block]), jnp.concatenate([block, partner]))
        stride *= 2
    return block


def per_device(signal, band, response, offsets):
    blocks = lax.axis_size("tm")
    levels = blocks.bit_length() - 1
    device_pos = lax.axis_index("tm")
    phase_bin = reverse_bits(device_pos, levels)
    channel_count, length = signal.shape
    total_len = length * blocks
    inner_len = math.gcd(128, length // lax.axis_size("chan"))
    real_part = signal
    imag_part = jnp.zeros_like(signal)
    for bit_index in range(levels - 1, -1, -1):
        half_span = 1 << bit_index
        partner = from_partner(jnp.stack([real_part, imag_part]), "tm", bit_index)
        upper_half = device_pos // half_span % 2 == 1
        cosine, sine_part = twiddle(device_pos % half_span, 2 * half_span)
        diff_real = partner[0] - real_part
        diff_imag = partner[1] - imag_part
        new_real = jnp.where(
            upper_half, diff_real * cosine - diff_imag * sine_part, real_part + partner[0]
        )
        new_imag = jnp.where(
            upper_half, diff_real * sine_part + diff_imag * cosine, imag_part + partner[1]
        )
        real_part, imag_part = (new_real, new_imag)
    inner = LANES
    outer = length // inner
    own = channel_count
    band_width = band.shape[1]
    half_width = band_width // 2
    channel_all = band.shape[2]
    tables = local_tables(own, outer, inner, phase_bin, total_len)
    spec_real, spec_imag = forward_call(
        real_part.reshape(own, outer, inner), imag_part.reshape(own, outer, inner), tables
    )
    chan_pos = lax.axis_index("chan")
    band_rows = lax.dynamic_slice_in_dim(band, chan_pos * own, own, axis=2)
    packed = jnp.concatenate(
        [response.reshape(2 * band_width, -1), offsets.reshape(1, -1).astype(jnp.float32)], axis=0
    )
    table = gather_doubling(packed[None], "chan")
    entries = table.shape[1]
    table = table.transpose(1, 0, 2).reshape(entries, inner, outer).transpose(0, 2, 1)
    responses = table[: 2 * band_width].reshape(2, band_width, outer, inner)
    shift = (table[2 * band_width].astype(jnp.int32) + half_width) % channel_all - half_width
    spectra = jnp.stack([spec_real, spec_imag])
    neighbours = [from_offset(spectra, "chan", delta) for delta in (-1, 1, 2, 3)]
    window = jnp.concatenate([neighbours[0], spectra] + neighbours[1:], axis=1)
    real_part, imag_part = inverse_call(window, shift, responses, band_rows.reshape(-1), tables, own)
    real_part = real_part.reshape(own, length)
    imag_part = imag_part.reshape(own, length)
    for bit_index in range(levels):
        half_span = 1 << bit_index
        partner = from_partner(jnp.stack([real_part, imag_part]), "tm", bit_index)
        upper_half = device_pos // half_span % 2 == 1
        cosine, sine_part = twiddle(device_pos % half_span, 2 * half_span)
        sine_part = -sine_part
        base_real = jnp.where(upper_half, partner[0], real_part)
        base_imag = jnp.where(upper_half, partner[1], imag_part)
        scaled_real = jnp.where(upper_half, real_part, partner[0])
        scaled_imag = jnp.where(upper_half, imag_part, partner[1])
        prod_real = scaled_real * cosine - scaled_imag * sine_part
        prod_imag = scaled_real * sine_part + scaled_imag * cosine
        real_part = jnp.where(upper_half, base_real - prod_real, base_real + prod_real)
        imag_part = jnp.where(upper_half, base_imag - prod_imag, base_imag + prod_imag)
    smoothed = real_part / total_len
    return smoothed


def solution(mesh):
    in_specs = (P("chan", "tm"), P(), P(None, "tm", None, "chan"), P("tm", "chan"))
    out_specs = P("chan", "tm")
    return jax.shard_map(
        per_device, mesh=mesh, in_specs=in_specs, out_specs=out_specs, check_vma=False
    )
```

```python
import math

import numpy as np

import jax
import jax.numpy as jnp
from jax import lax
from jax.experimental import pallas as pl
from jax.experimental.pallas import tpu as pltpu
from jax.sharding import PartitionSpec as P

PRECISE = lax.Precision.HIGHEST


def from_partner(block, axis, stride):
    count = lax.axis_size(axis)
    route = []
    for low in range(count):
        high = low | 1 << stride
        if high != low and high < count:
            route += [(low, high), (high, low)]
    return lax.ppermute(block, axis, route)


def twiddle(numer, length):
    angle = -2.0 * math.pi / length * numer.astype(jnp.float32)
    return (jnp.cos(angle), jnp.sin(angle))


def dft_table(length):
    steps = lax.iota(jnp.int32, length)
    return twiddle(steps[:, None] * steps[None, :] % length, length)


def reverse_bits(value, bit_count):
    result = value * 0
    for bit_index in range(bit_count):
        result = result + value // (1 << bit_index) % 2 * (1 << bit_count - 1 - bit_index)
    return result


def complex_einsum(form, left_real, left_imag, right_real, right_imag):
    out_real = jnp.einsum(form, left_real, right_real, precision=PRECISE) - jnp.einsum(
        form, left_imag, right_imag, precision=PRECISE
    )
    out_imag = jnp.einsum(form, left_real, right_imag, precision=PRECISE) + jnp.einsum(
        form, left_imag, right_real, precision=PRECISE
    )
    return (out_real, out_imag)


def forward_local(real_part, imag_part, phase_bin, total_len, inner_len):
    channel_count, length = real_part.shape
    outer_len = length // inner_len
    sample_pos = lax.iota(jnp.int32, length)
    cosine, sine_part = twiddle(sample_pos * phase_bin % total_len, total_len)
    real_part, imag_part = (
        real_part * cosine - imag_part * sine_part,
        real_part * sine_part + imag_part * cosine,
    )
    real_part = real_part.reshape(channel_count, inner_len, outer_len)
    imag_part = imag_part.reshape(channel_count, inner_len, outer_len)
    table_real, table_imag = dft_table(inner_len)
    real_part, imag_part = complex_einsum(
        "cab,ak->cbk", real_part, imag_part, table_real, table_imag
    )
    outer_ids = lax.iota(jnp.int32, outer_len)[:, None]
    inner_ids = lax.iota(jnp.int32, inner_len)[None, :]
    cosine, sine_part = twiddle(outer_ids * inner_ids, length)
    real_part, imag_part = (
        real_part * cosine - imag_part * sine_part,
        real_part * sine_part + imag_part * cosine,
    )
    table_real, table_imag = dft_table(outer_len)
    return complex_einsum("cbk,bm->mck", real_part, imag_part, table_real, table_imag)


def inverse_local(spec_real, spec_imag, phase_bin, total_len):
    outer_len, channel_count, inner_len = spec_real.shape
    length = outer_len * inner_len
    table_real, table_imag = dft_table(outer_len)
    real_part, imag_part = complex_einsum(
        "mck,mb->cbk", spec_real, spec_imag, table_real, -table_imag
    )
    outer_ids = lax.iota(jnp.int32, outer_len)[:, None]
    inner_ids = lax.iota(jnp.int32, inner_len)[None, :]
    cosine, sine_part = twiddle(outer_ids * inner_ids, length)
    sine_part = -sine_part
    real_part, imag_part = (
        real_part * cosine - imag_part * sine_part,
        real_part * sine_part + imag_part * cosine,
    )
    table_real, table_imag = dft_table(inner_len)
    real_part, imag_part = complex_einsum(
        "cbk,ka->cab", real_part, imag_part, table_real, -table_imag
    )
    real_part = real_part.reshape(channel_count, length)
    imag_part = imag_part.reshape(channel_count, length)
    sample_pos = lax.iota(jnp.int32, length)
    cosine, sine_part = twiddle(sample_pos * phase_bin % total_len, total_len)
    sine_part = -sine_part
    return (real_part * cosine - imag_part * sine_part, real_part * sine_part + imag_part * cosine)


LANES = 128


def cdot(left_real, left_imag, right_real, right_imag):
    def dot(a, b):
        return jnp.dot(a, b, precision=PRECISE, preferred_element_type=jnp.float32)

    return (
        dot(left_real, right_real) - dot(left_imag, right_imag),
        dot(left_real, right_imag) + dot(left_imag, right_real),
    )


def forward_kernel(xr_ref, xi_ref, twr_ref, twi_ref, kr_ref, ki_ref, t2r_ref, t2i_ref, wr_ref, wi_ref, yr_ref, yi_ref):
    own, outer, inner = xr_ref.shape
    xr = xr_ref[...]
    xi = xi_ref[...]
    position = lax.axis_index("tm")
    twr = twr_ref[position][None]
    twi = twi_ref[position][None]
    ur = (xr * twr - xi * twi).reshape(own * outer, inner)
    ui = (xr * twi + xi * twr).reshape(own * outer, inner)
    zr, zi = cdot(kr_ref[...], ki_ref[...], ur, ui)
    t2r = t2r_ref[...]
    t2i = t2i_ref[...]
    zr, zi = (zr * t2r - zi * t2i, zr * t2i + zi * t2r)
    yr, yi = cdot(zr, zi, wr_ref[...], wi_ref[...])
    yr_ref[...] = yr.reshape(own, outer, inner)
    yi_ref[...] = yi.reshape(own, outer, inner)


def inverse_kernel(win_ref, shift_ref, resp_ref, band_ref, twr_ref, twi_ref, kr_ref, ki_ref, t2r_ref, t2i_ref, wr_ref, wi_ref, xr_ref, xi_ref):
    own, outer, inner = xr_ref.shape
    band_width = resp_ref.shape[1]
    half_width = band_width // 2
    span = own + band_width - 1
    shift = shift_ref[...]
    masks = [shift == amount for amount in range(-half_width, half_width + 1)]
    moved = []
    for row in range(span):
        mr = jnp.zeros((outer, inner), jnp.float32)
        mi = jnp.zeros((outer, inner), jnp.float32)
        for index, amount in enumerate(range(-half_width, half_width + 1)):
            source = own + amount + row
            mr = jnp.where(masks[index], win_ref[0, source], mr)
            mi = jnp.where(masks[index], win_ref[1, source], mi)
        moved.append((mr, mi))
    rows_real = []
    rows_imag = []
    channel_all = band_ref.shape[0] // (2 * band_width)
    first = lax.axis_index("chan") * own
    for channel in range(own):
        acc_r = jnp.zeros((outer, inner), jnp.float32)
        acc_i = jnp.zeros((outer, inner), jnp.float32)
        for lag in range(band_width):
            br = band_ref[lag * channel_all + first + channel]
            bi = band_ref[(band_width + lag) * channel_all + first + channel]
            rr = resp_ref[0, lag]
            ri = resp_ref[1, lag]
            cr = br * rr - bi * ri
            ci = br * ri + bi * rr
            vr, vi = moved[channel + lag]
            acc_r = acc_r + cr * vr - ci * vi
            acc_i = acc_i + cr * vi + ci * vr
        rows_real.append(acc_r)
        rows_imag.append(acc_i)
    mr = jnp.concatenate(rows_real, axis=0)
    mi = jnp.concatenate(rows_imag, axis=0)
    yr, yi = cdot(mr, mi, wr_ref[...], -wi_ref[...])
    t2r = t2r_ref[...]
    t2i = -t2i_ref[...]
    yr, yi = (yr * t2r - yi * t2i, yr * t2i + yi * t2r)
    xr, xi = cdot(kr_ref[...], -ki_ref[...], yr, yi)
    xr = xr.reshape(own, outer, inner)
    xi = xi.reshape(own, outer, inner)
    position = lax.axis_index("tm")
    twr = twr_ref[position][None]
    twi = -twi_ref[position][None]
    xr_ref[...] = xr * twr - xi * twi
    xi_ref[...] = xr * twi + xi * twr


def dft_constant(length, numer):
    angle = -2.0 * np.pi / length * (numer % length)
    return (np.cos(angle).astype(np.float32), np.sin(angle).astype(np.float32))


def local_tables(own, outer, inner, blocks, levels):
    length = outer * inner
    total_len = length * blocks
    rows = np.arange(outer)[:, None]
    cols = np.arange(inner)[None, :]
    residues = [reverse_bits(position, levels) for position in range(blocks)]
    phase = np.stack([(rows * inner + cols) * residue for residue in residues])
    twr, twi = dft_constant(total_len, phase)
    small_r, small_i = dft_constant(outer, rows * np.arange(outer)[None, :])
    eye = np.eye(own, dtype=np.float32)
    kr = np.kron(eye, small_r)
    ki = np.kron(eye, small_i)
    t2r, t2i = dft_constant(length, rows * cols)
    t2r = np.tile(t2r, (own, 1))
    t2i = np.tile(t2i, (own, 1))
    wr, wi = dft_constant(inner, np.arange(inner)[:, None] * cols)
    return tuple(jnp.asarray(table) for table in (twr, twi, kr, ki, t2r, t2i, wr, wi))


def vmem_specs(count):
    return [pl.BlockSpec(memory_space=pltpu.VMEM)] * count


def forward_call(xr, xi, tables):
    shape = jax.ShapeDtypeStruct(xr.shape, jnp.float32)
    return pl.pallas_call(
        forward_kernel,
        out_shape=(shape, shape),
        in_specs=vmem_specs(2 + len(tables)),
        out_specs=tuple(vmem_specs(2)),
    )(xr, xi, *tables)


def inverse_call(window, shift, responses, band_flat, tables, own):
    shape = jax.ShapeDtypeStruct((own,) + window.shape[2:], jnp.float32)
    specs = vmem_specs(3) + [pl.BlockSpec(memory_space=pltpu.SMEM)] + vmem_specs(len(tables))
    return pl.pallas_call(
        inverse_kernel,
        out_shape=(shape, shape),
        in_specs=specs,
        out_specs=tuple(vmem_specs(2)),
    )(window, shift, responses, band_flat, *tables)


def from_offset(block, axis, delta):
    count = lax.axis_size(axis)
    return lax.ppermute(block, axis, [((i + delta) % count, i) for i in range(count)])


def gather_doubling(block, axis):
    count = lax.axis_size(axis)
    me = lax.axis_index(axis)
    stride = 1
    while stride < count:
        partner = from_partner(block, axis, stride.bit_length() - 1)
        upper = me // stride % 2 == 1
        block = jnp.where(upper, jnp.concatenate([partner, block]), jnp.concatenate([block, partner]))
        stride *= 2
    return block


def per_device(signal, band, response, offsets):
    blocks = lax.axis_size("tm")
    levels = blocks.bit_length() - 1
    device_pos = lax.axis_index("tm")
    phase_bin = reverse_bits(device_pos, levels)
    channel_count, length = signal.shape
    total_len = length * blocks
    inner_len = math.gcd(128, length // lax.axis_size("chan"))
    real_part = signal
    imag_part = jnp.zeros_like(signal)
    for bit_index in range(levels - 1, -1, -1):
        half_span = 1 << bit_index
        partner = from_partner(jnp.stack([real_part, imag_part]), "tm", bit_index)
        upper_half = device_pos // half_span % 2 == 1
        cosine, sine_part = twiddle(device_pos % half_span, 2 * half_span)
        diff_real = partner[0] - real_part
        diff_imag = partner[1] - imag_part
        new_real = jnp.where(
            upper_half, diff_real * cosine - diff_imag * sine_part, real_part + partner[0]
        )
        new_imag = jnp.where(
            upper_half, diff_real * sine_part + diff_imag * cosine, imag_part + partner[1]
        )
        real_part, imag_part = (new_real, new_imag)
    inner = LANES
    outer = length // inner
    own = channel_count
    band_width = band.shape[1]
    half_width = band_width // 2
    channel_all = band.shape[2]
    tables = local_tables(own, outer, inner, blocks, levels)
    spec_real, spec_imag = forward_call(
        real_part.reshape(own, outer, inner), imag_part.reshape(own, outer, inner), tables
    )
    packed = jnp.concatenate(
        [response.reshape(2 * band_width, -1), offsets.reshape(1, -1).astype(jnp.float32)], axis=0
    )
    packed, _ = lax.optimization_barrier((packed, real_part))
    table = gather_doubling(packed[None], "chan")
    entries = table.shape[1]
    table = table.transpose(1, 0, 2).reshape(entries, inner, outer).transpose(0, 2, 1)
    responses = table[: 2 * band_width].reshape(2, band_width, outer, inner)
    shift = (table[2 * band_width].astype(jnp.int32) + half_width) % channel_all - half_width
    spectra = jnp.stack([spec_real, spec_imag])
    neighbours = [from_offset(spectra, "chan", delta) for delta in (-1, 1, 2, 3)]
    window = jnp.concatenate([neighbours[0], spectra] + neighbours[1:], axis=1)
    real_part, imag_part = inverse_call(window, shift, responses, band.reshape(-1), tables, own)
    real_part = real_part.reshape(own, length)
    imag_part = imag_part.reshape(own, length)
    for bit_index in range(levels):
        half_span = 1 << bit_index
        partner = from_partner(jnp.stack([real_part, imag_part]), "tm", bit_index)
        upper_half = device_pos // half_span % 2 == 1
        cosine, sine_part = twiddle(device_pos % half_span, 2 * half_span)
        sine_part = -sine_part
        base_real = jnp.where(upper_half, partner[0], real_part)
        base_imag = jnp.where(upper_half, partner[1], imag_part)
        scaled_real = jnp.where(upper_half, real_part, partner[0])
        scaled_imag = jnp.where(upper_half, imag_part, partner[1])
        prod_real = scaled_real * cosine - scaled_imag * sine_part
        prod_imag = scaled_real * sine_part + scaled_imag * cosine
        real_part = jnp.where(upper_half, base_real - prod_real, base_real + prod_real)
        imag_part = jnp.where(upper_half, base_imag - prod_imag, base_imag + prod_imag)
    smoothed = real_part / total_len
    return smoothed


def solution(mesh):
    in_specs = (P("chan", "tm"), P(), P(None, "tm", None, "chan"), P("tm", "chan"))
    out_specs = P("chan", "tm")
    return jax.shard_map(
        per_device, mesh=mesh, in_specs=in_specs, out_specs=out_specs, check_vma=False
    )
```

```python
import math

import numpy as np

import jax
import jax.numpy as jnp
from jax import lax
from jax.experimental import pallas as pl
from jax.experimental.pallas import tpu as pltpu
from jax.sharding import PartitionSpec as P

PRECISE = lax.Precision.HIGHEST


def from_partner(block, axis, stride):
    count = lax.axis_size(axis)
    route = []
    for low in range(count):
        high = low | 1 << stride
        if high != low and high < count:
            route += [(low, high), (high, low)]
    return lax.ppermute(block, axis, route)


def twiddle(numer, length):
    angle = -2.0 * math.pi / length * numer.astype(jnp.float32)
    return (jnp.cos(angle), jnp.sin(angle))


def dft_table(length):
    steps = lax.iota(jnp.int32, length)
    return twiddle(steps[:, None] * steps[None, :] % length, length)


def reverse_bits(value, bit_count):
    result = value * 0
    for bit_index in range(bit_count):
        result = result + value // (1 << bit_index) % 2 * (1 << bit_count - 1 - bit_index)
    return result


def complex_einsum(form, left_real, left_imag, right_real, right_imag):
    out_real = jnp.einsum(form, left_real, right_real, precision=PRECISE) - jnp.einsum(
        form, left_imag, right_imag, precision=PRECISE
    )
    out_imag = jnp.einsum(form, left_real, right_imag, precision=PRECISE) + jnp.einsum(
        form, left_imag, right_real, precision=PRECISE
    )
    return (out_real, out_imag)


def forward_local(real_part, imag_part, phase_bin, total_len, inner_len):
    channel_count, length = real_part.shape
    outer_len = length // inner_len
    sample_pos = lax.iota(jnp.int32, length)
    cosine, sine_part = twiddle(sample_pos * phase_bin % total_len, total_len)
    real_part, imag_part = (
        real_part * cosine - imag_part * sine_part,
        real_part * sine_part + imag_part * cosine,
    )
    real_part = real_part.reshape(channel_count, inner_len, outer_len)
    imag_part = imag_part.reshape(channel_count, inner_len, outer_len)
    table_real, table_imag = dft_table(inner_len)
    real_part, imag_part = complex_einsum(
        "cab,ak->cbk", real_part, imag_part, table_real, table_imag
    )
    outer_ids = lax.iota(jnp.int32, outer_len)[:, None]
    inner_ids = lax.iota(jnp.int32, inner_len)[None, :]
    cosine, sine_part = twiddle(outer_ids * inner_ids, length)
    real_part, imag_part = (
        real_part * cosine - imag_part * sine_part,
        real_part * sine_part + imag_part * cosine,
    )
    table_real, table_imag = dft_table(outer_len)
    return complex_einsum("cbk,bm->mck", real_part, imag_part, table_real, table_imag)


def inverse_local(spec_real, spec_imag, phase_bin, total_len):
    outer_len, channel_count, inner_len = spec_real.shape
    length = outer_len * inner_len
    table_real, table_imag = dft_table(outer_len)
    real_part, imag_part = complex_einsum(
        "mck,mb->cbk", spec_real, spec_imag, table_real, -table_imag
    )
    outer_ids = lax.iota(jnp.int32, outer_len)[:, None]
    inner_ids = lax.iota(jnp.int32, inner_len)[None, :]
    cosine, sine_part = twiddle(outer_ids * inner_ids, length)
    sine_part = -sine_part
    real_part, imag_part = (
        real_part * cosine - imag_part * sine_part,
        real_part * sine_part + imag_part * cosine,
    )
    table_real, table_imag = dft_table(inner_len)
    real_part, imag_part = complex_einsum(
        "cbk,ka->cab", real_part, imag_part, table_real, -table_imag
    )
    real_part = real_part.reshape(channel_count, length)
    imag_part = imag_part.reshape(channel_count, length)
    sample_pos = lax.iota(jnp.int32, length)
    cosine, sine_part = twiddle(sample_pos * phase_bin % total_len, total_len)
    sine_part = -sine_part
    return (real_part * cosine - imag_part * sine_part, real_part * sine_part + imag_part * cosine)


LANES = 128


def cdot(left_real, left_imag, right_real, right_imag):
    def dot(a, b):
        return jnp.dot(a, b, precision=PRECISE, preferred_element_type=jnp.float32)

    return (
        dot(left_real, right_real) - dot(left_imag, right_imag),
        dot(left_real, right_imag) + dot(left_imag, right_real),
    )


def forward_kernel(xr_ref, xi_ref, twr_ref, twi_ref, kr_ref, ki_ref, t2r_ref, t2i_ref, wr_ref, wi_ref, yr_ref, yi_ref):
    own, outer, inner = xr_ref.shape
    xr = xr_ref[...]
    xi = xi_ref[...]
    position = lax.axis_index("tm")
    twr = twr_ref[position][None]
    twi = twi_ref[position][None]
    ur = (xr * twr - xi * twi).reshape(own * outer, inner)
    ui = (xr * twi + xi * twr).reshape(own * outer, inner)
    zr, zi = cdot(kr_ref[...], ki_ref[...], ur, ui)
    t2r = t2r_ref[...]
    t2i = t2i_ref[...]
    zr, zi = (zr * t2r - zi * t2i, zr * t2i + zi * t2r)
    yr, yi = cdot(zr, zi, wr_ref[...], wi_ref[...])
    yr_ref[...] = yr.reshape(own, outer, inner)
    yi_ref[...] = yi.reshape(own, outer, inner)


def inverse_kernel(win_ref, shift_ref, resp_ref, band_ref, twr_ref, twi_ref, kr_ref, ki_ref, t2r_ref, t2i_ref, wr_ref, wi_ref, xr_ref, xi_ref):
    own, outer, inner = xr_ref.shape
    band_width = resp_ref.shape[1]
    half_width = band_width // 2
    span = own + band_width - 1
    shift = shift_ref[...]
    masks = [shift == amount for amount in range(-half_width, half_width + 1)]
    moved = []
    for row in range(span):
        mr = jnp.zeros((outer, inner), jnp.float32)
        mi = jnp.zeros((outer, inner), jnp.float32)
        for index, amount in enumerate(range(-half_width, half_width + 1)):
            source = own + amount + row
            mr = jnp.where(masks[index], win_ref[0, source], mr)
            mi = jnp.where(masks[index], win_ref[1, source], mi)
        moved.append((mr, mi))
    rows_real = []
    rows_imag = []
    channel_all = band_ref.shape[0] // (2 * band_width)
    first = lax.axis_index("chan") * own
    for channel in range(own):
        acc_r = jnp.zeros((outer, inner), jnp.float32)
        acc_i = jnp.zeros((outer, inner), jnp.float32)
        for lag in range(band_width):
            br = band_ref[lag * channel_all + first + channel]
            bi = band_ref[(band_width + lag) * channel_all + first + channel]
            rr = resp_ref[0, lag]
            ri = resp_ref[1, lag]
            cr = br * rr - bi * ri
            ci = br * ri + bi * rr
            vr, vi = moved[channel + lag]
            acc_r = acc_r + cr * vr - ci * vi
            acc_i = acc_i + cr * vi + ci * vr
        rows_real.append(acc_r)
        rows_imag.append(acc_i)
    mr = jnp.concatenate(rows_real, axis=0)
    mi = jnp.concatenate(rows_imag, axis=0)
    yr, yi = cdot(mr, mi, wr_ref[...], -wi_ref[...])
    t2r = t2r_ref[...]
    t2i = -t2i_ref[...]
    yr, yi = (yr * t2r - yi * t2i, yr * t2i + yi * t2r)
    xr, xi = cdot(kr_ref[...], -ki_ref[...], yr, yi)
    xr = xr.reshape(own, outer, inner)
    xi = xi.reshape(own, outer, inner)
    position = lax.axis_index("tm")
    twr = twr_ref[position][None]
    twi = -twi_ref[position][None]
    xr_ref[...] = xr * twr - xi * twi
    xi_ref[...] = xr * twi + xi * twr


def dft_constant(length, numer):
    angle = -2.0 * np.pi / length * (numer % length)
    return (np.cos(angle).astype(np.float32), np.sin(angle).astype(np.float32))


def local_tables(own, outer, inner, blocks, levels):
    length = outer * inner
    total_len = length * blocks
    rows = np.arange(outer)[:, None]
    cols = np.arange(inner)[None, :]
    residues = [reverse_bits(position, levels) for position in range(blocks)]
    phase = np.stack([(rows * inner + cols) * residue for residue in residues])
    twr, twi = dft_constant(total_len, phase)
    small_r, small_i = dft_constant(outer, rows * np.arange(outer)[None, :])
    eye = np.eye(own, dtype=np.float32)
    kr = np.kron(eye, small_r)
    ki = np.kron(eye, small_i)
    t2r, t2i = dft_constant(length, rows * cols)
    t2r = np.tile(t2r, (own, 1))
    t2i = np.tile(t2i, (own, 1))
    wr, wi = dft_constant(inner, np.arange(inner)[:, None] * cols)
    return tuple(jnp.asarray(table) for table in (twr, twi, kr, ki, t2r, t2i, wr, wi))


def vmem_specs(count):
    return [pl.BlockSpec(memory_space=pltpu.VMEM)] * count


def forward_call(xr, xi, tables):
    shape = jax.ShapeDtypeStruct(xr.shape, jnp.float32)
    return pl.pallas_call(
        forward_kernel,
        out_shape=(shape, shape),
        in_specs=vmem_specs(2 + len(tables)),
        out_specs=tuple(vmem_specs(2)),
    )(xr, xi, *tables)


def inverse_call(window, shift, responses, band_flat, tables, own):
    shape = jax.ShapeDtypeStruct((own,) + window.shape[2:], jnp.float32)
    specs = vmem_specs(3) + [pl.BlockSpec(memory_space=pltpu.SMEM)] + vmem_specs(len(tables))
    return pl.pallas_call(
        inverse_kernel,
        out_shape=(shape, shape),
        in_specs=specs,
        out_specs=tuple(vmem_specs(2)),
    )(window, shift, responses, band_flat, *tables)


def from_offset(block, axis, delta):
    count = lax.axis_size(axis)
    return lax.ppermute(block, axis, [((i + delta) % count, i) for i in range(count)])


def gather_doubling(block, axis):
    count = lax.axis_size(axis)
    me = lax.axis_index(axis)
    stride = 1
    while stride < count:
        partner = from_partner(block, axis, stride.bit_length() - 1)
        upper = me // stride % 2 == 1
        block = jnp.where(upper, jnp.concatenate([partner, block]), jnp.concatenate([block, partner]))
        stride *= 2
    return block


def per_device(signal, band, response, offsets):
    blocks = lax.axis_size("tm")
    levels = blocks.bit_length() - 1
    device_pos = lax.axis_index("tm")
    phase_bin = reverse_bits(device_pos, levels)
    channel_count, length = signal.shape
    total_len = length * blocks
    inner_len = math.gcd(128, length // lax.axis_size("chan"))
    real_part = signal
    imag_part = jnp.zeros_like(signal)
    for bit_index in range(levels - 1, -1, -1):
        half_span = 1 << bit_index
        partner = from_partner(jnp.stack([real_part, imag_part]), "tm", bit_index)
        upper_half = device_pos // half_span % 2 == 1
        cosine, sine_part = twiddle(device_pos % half_span, 2 * half_span)
        diff_real = partner[0] - real_part
        diff_imag = partner[1] - imag_part
        new_real = jnp.where(
            upper_half, diff_real * cosine - diff_imag * sine_part, real_part + partner[0]
        )
        new_imag = jnp.where(
            upper_half, diff_real * sine_part + diff_imag * cosine, imag_part + partner[1]
        )
        real_part, imag_part = (new_real, new_imag)
    inner = LANES
    outer = length // inner
    own = channel_count
    band_width = band.shape[1]
    half_width = band_width // 2
    channel_all = band.shape[2]
    tables = local_tables(own, outer, inner, blocks, levels)
    spec_real, spec_imag = forward_call(
        real_part.reshape(own, outer, inner), imag_part.reshape(own, outer, inner), tables
    )
    packed = jnp.concatenate(
        [response.reshape(2 * band_width, -1), offsets.reshape(1, -1).astype(jnp.float32)], axis=0
    )
    slots = jnp.zeros((lax.axis_size("chan"),) + packed.shape, packed.dtype)
    table = lax.psum(lax.dynamic_update_index_in_dim(slots, packed, lax.axis_index("chan"), 0), "chan")
    entries = table.shape[1]
    table = table.transpose(1, 0, 2).reshape(entries, inner, outer).transpose(0, 2, 1)
    responses = table[: 2 * band_width].reshape(2, band_width, outer, inner)
    shift = (table[2 * band_width].astype(jnp.int32) + half_width) % channel_all - half_width
    spectra = jnp.stack([spec_real, spec_imag])
    neighbours = [from_offset(spectra, "chan", delta) for delta in (-1, 1, 2, 3)]
    window = jnp.concatenate([neighbours[0], spectra] + neighbours[1:], axis=1)
    real_part, imag_part = inverse_call(window, shift, responses, band.reshape(-1), tables, own)
    real_part = real_part.reshape(own, length)
    imag_part = imag_part.reshape(own, length)
    for bit_index in range(levels):
        half_span = 1 << bit_index
        partner = from_partner(jnp.stack([real_part, imag_part]), "tm", bit_index)
        upper_half = device_pos // half_span % 2 == 1
        cosine, sine_part = twiddle(device_pos % half_span, 2 * half_span)
        sine_part = -sine_part
        base_real = jnp.where(upper_half, partner[0], real_part)
        base_imag = jnp.where(upper_half, partner[1], imag_part)
        scaled_real = jnp.where(upper_half, real_part, partner[0])
        scaled_imag = jnp.where(upper_half, imag_part, partner[1])
        prod_real = scaled_real * cosine - scaled_imag * sine_part
        prod_imag = scaled_real * sine_part + scaled_imag * cosine
        real_part = jnp.where(upper_half, base_real - prod_real, base_real + prod_real)
        imag_part = jnp.where(upper_half, base_imag - prod_imag, base_imag + prod_imag)
    smoothed = real_part / total_len
    return smoothed


def solution(mesh):
    in_specs = (P("chan", "tm"), P(), P(None, "tm", None, "chan"), P("tm", "chan"))
    out_specs = P("chan", "tm")
    return jax.shard_map(
        per_device, mesh=mesh, in_specs=in_specs, out_specs=out_specs, check_vma=False
    )
```

```python
import math

import numpy as np

import jax
import jax.numpy as jnp
from jax import lax
from jax.experimental import pallas as pl
from jax.experimental.pallas import tpu as pltpu
from jax.sharding import PartitionSpec as P

PRECISE = lax.Precision.HIGHEST


def from_partner(block, axis, stride):
    count = lax.axis_size(axis)
    route = []
    for low in range(count):
        high = low | 1 << stride
        if high != low and high < count:
            route += [(low, high), (high, low)]
    return lax.ppermute(block, axis, route)


def twiddle(numer, length):
    angle = -2.0 * math.pi / length * numer.astype(jnp.float32)
    return (jnp.cos(angle), jnp.sin(angle))


def dft_table(length):
    steps = lax.iota(jnp.int32, length)
    return twiddle(steps[:, None] * steps[None, :] % length, length)


def reverse_bits(value, bit_count):
    result = value * 0
    for bit_index in range(bit_count):
        result = result + value // (1 << bit_index) % 2 * (1 << bit_count - 1 - bit_index)
    return result


def complex_einsum(form, left_real, left_imag, right_real, right_imag):
    out_real = jnp.einsum(form, left_real, right_real, precision=PRECISE) - jnp.einsum(
        form, left_imag, right_imag, precision=PRECISE
    )
    out_imag = jnp.einsum(form, left_real, right_imag, precision=PRECISE) + jnp.einsum(
        form, left_imag, right_real, precision=PRECISE
    )
    return (out_real, out_imag)


def forward_local(real_part, imag_part, phase_bin, total_len, inner_len):
    channel_count, length = real_part.shape
    outer_len = length // inner_len
    sample_pos = lax.iota(jnp.int32, length)
    cosine, sine_part = twiddle(sample_pos * phase_bin % total_len, total_len)
    real_part, imag_part = (
        real_part * cosine - imag_part * sine_part,
        real_part * sine_part + imag_part * cosine,
    )
    real_part = real_part.reshape(channel_count, inner_len, outer_len)
    imag_part = imag_part.reshape(channel_count, inner_len, outer_len)
    table_real, table_imag = dft_table(inner_len)
    real_part, imag_part = complex_einsum(
        "cab,ak->cbk", real_part, imag_part, table_real, table_imag
    )
    outer_ids = lax.iota(jnp.int32, outer_len)[:, None]
    inner_ids = lax.iota(jnp.int32, inner_len)[None, :]
    cosine, sine_part = twiddle(outer_ids * inner_ids, length)
    real_part, imag_part = (
        real_part * cosine - imag_part * sine_part,
        real_part * sine_part + imag_part * cosine,
    )
    table_real, table_imag = dft_table(outer_len)
    return complex_einsum("cbk,bm->mck", real_part, imag_part, table_real, table_imag)


def inverse_local(spec_real, spec_imag, phase_bin, total_len):
    outer_len, channel_count, inner_len = spec_real.shape
    length = outer_len * inner_len
    table_real, table_imag = dft_table(outer_len)
    real_part, imag_part = complex_einsum(
        "mck,mb->cbk", spec_real, spec_imag, table_real, -table_imag
    )
    outer_ids = lax.iota(jnp.int32, outer_len)[:, None]
    inner_ids = lax.iota(jnp.int32, inner_len)[None, :]
    cosine, sine_part = twiddle(outer_ids * inner_ids, length)
    sine_part = -sine_part
    real_part, imag_part = (
        real_part * cosine - imag_part * sine_part,
        real_part * sine_part + imag_part * cosine,
    )
    table_real, table_imag = dft_table(inner_len)
    real_part, imag_part = complex_einsum(
        "cbk,ka->cab", real_part, imag_part, table_real, -table_imag
    )
    real_part = real_part.reshape(channel_count, length)
    imag_part = imag_part.reshape(channel_count, length)
    sample_pos = lax.iota(jnp.int32, length)
    cosine, sine_part = twiddle(sample_pos * phase_bin % total_len, total_len)
    sine_part = -sine_part
    return (real_part * cosine - imag_part * sine_part, real_part * sine_part + imag_part * cosine)


LANES = 128


def cdot(left_real, left_imag, right_real, right_imag):
    def dot(a, b):
        return jnp.dot(a, b, precision=PRECISE, preferred_element_type=jnp.float32)

    return (
        dot(left_real, right_real) - dot(left_imag, right_imag),
        dot(left_real, right_imag) + dot(left_imag, right_real),
    )


def forward_kernel(xr_ref, xi_ref, twr_ref, twi_ref, kr_ref, ki_ref, t2r_ref, t2i_ref, wr_ref, wi_ref, yr_ref, yi_ref):
    own, outer, inner = xr_ref.shape
    xr = xr_ref[...]
    xi = xi_ref[...]
    position = lax.axis_index("tm")
    twr = twr_ref[position][None]
    twi = twi_ref[position][None]
    ur = (xr * twr - xi * twi).reshape(own * outer, inner)
    ui = (xr * twi + xi * twr).reshape(own * outer, inner)
    zr, zi = cdot(kr_ref[...], ki_ref[...], ur, ui)
    t2r = t2r_ref[...]
    t2i = t2i_ref[...]
    zr, zi = (zr * t2r - zi * t2i, zr * t2i + zi * t2r)
    yr, yi = cdot(zr, zi, wr_ref[...], wi_ref[...])
    yr_ref[...] = yr.reshape(own, outer, inner)
    yi_ref[...] = yi.reshape(own, outer, inner)


def inverse_kernel(win_ref, shift_ref, resp_ref, band_ref, twr_ref, twi_ref, kr_ref, ki_ref, t2r_ref, t2i_ref, wr_ref, wi_ref, xr_ref, xi_ref):
    own, outer, inner = xr_ref.shape
    band_width = resp_ref.shape[1]
    half_width = band_width // 2
    span = own + band_width - 1
    shift = shift_ref[...]
    masks = [shift == amount for amount in range(-half_width, half_width + 1)]
    moved = []
    for row in range(span):
        mr = jnp.zeros((outer, inner), jnp.float32)
        mi = jnp.zeros((outer, inner), jnp.float32)
        for index, amount in enumerate(range(-half_width, half_width + 1)):
            source = own + amount + row
            mr = jnp.where(masks[index], win_ref[0, source], mr)
            mi = jnp.where(masks[index], win_ref[1, source], mi)
        moved.append((mr, mi))
    rows_real = []
    rows_imag = []
    channel_all = band_ref.shape[0] // (2 * band_width)
    first = lax.axis_index("chan") * own
    for channel in range(own):
        acc_r = jnp.zeros((outer, inner), jnp.float32)
        acc_i = jnp.zeros((outer, inner), jnp.float32)
        for lag in range(band_width):
            br = band_ref[lag * channel_all + first + channel]
            bi = band_ref[(band_width + lag) * channel_all + first + channel]
            rr = resp_ref[0, lag]
            ri = resp_ref[1, lag]
            cr = br * rr - bi * ri
            ci = br * ri + bi * rr
            vr, vi = moved[channel + lag]
            acc_r = acc_r + cr * vr - ci * vi
            acc_i = acc_i + cr * vi + ci * vr
        rows_real.append(acc_r)
        rows_imag.append(acc_i)
    mr = jnp.concatenate(rows_real, axis=0)
    mi = jnp.concatenate(rows_imag, axis=0)
    yr, yi = cdot(mr, mi, wr_ref[...], -wi_ref[...])
    t2r = t2r_ref[...]
    t2i = -t2i_ref[...]
    yr, yi = (yr * t2r - yi * t2i, yr * t2i + yi * t2r)
    xr, xi = cdot(kr_ref[...], -ki_ref[...], yr, yi)
    xr = xr.reshape(own, outer, inner)
    xi = xi.reshape(own, outer, inner)
    position = lax.axis_index("tm")
    twr = twr_ref[position][None]
    twi = -twi_ref[position][None]
    xr_ref[...] = xr * twr - xi * twi
    xi_ref[...] = xr * twi + xi * twr


def dft_constant(length, numer):
    angle = -2.0 * np.pi / length * (numer % length)
    return (np.cos(angle).astype(np.float32), np.sin(angle).astype(np.float32))


def local_tables(own, outer, inner, blocks, levels):
    length = outer * inner
    total_len = length * blocks
    rows = np.arange(outer)[:, None]
    cols = np.arange(inner)[None, :]
    residues = [reverse_bits(position, levels) for position in range(blocks)]
    phase = np.stack([(rows * inner + cols) * residue for residue in residues])
    twr, twi = dft_constant(total_len, phase)
    small_r, small_i = dft_constant(outer, rows * np.arange(outer)[None, :])
    eye = np.eye(own, dtype=np.float32)
    kr = np.kron(eye, small_r)
    ki = np.kron(eye, small_i)
    t2r, t2i = dft_constant(length, rows * cols)
    t2r = np.tile(t2r, (own, 1))
    t2i = np.tile(t2i, (own, 1))
    wr, wi = dft_constant(inner, np.arange(inner)[:, None] * cols)
    return tuple(jnp.asarray(table) for table in (twr, twi, kr, ki, t2r, t2i, wr, wi))


def vmem_specs(count):
    return [pl.BlockSpec(memory_space=pltpu.VMEM)] * count


def forward_call(xr, xi, tables):
    shape = jax.ShapeDtypeStruct(xr.shape, jnp.float32)
    return pl.pallas_call(
        forward_kernel,
        out_shape=(shape, shape),
        in_specs=vmem_specs(2 + len(tables)),
        out_specs=tuple(vmem_specs(2)),
    )(xr, xi, *tables)


def inverse_call(window, shift, responses, band_flat, tables, own):
    shape = jax.ShapeDtypeStruct((own,) + window.shape[2:], jnp.float32)
    specs = vmem_specs(3) + [pl.BlockSpec(memory_space=pltpu.SMEM)] + vmem_specs(len(tables))
    return pl.pallas_call(
        inverse_kernel,
        out_shape=(shape, shape),
        in_specs=specs,
        out_specs=tuple(vmem_specs(2)),
    )(window, shift, responses, band_flat, *tables)


def from_offset(block, axis, delta):
    count = lax.axis_size(axis)
    return lax.ppermute(block, axis, [((i + delta) % count, i) for i in range(count)])


def digit_radices(count):
    radices = []
    for radix in (2, 4, 4):
        if count % radix == 0 and count > 1:
            radices.append(radix)
            count //= radix
    while count > 1:
        radices.append(2)
        count //= 2
    return radices


def gather_radix(block, axis):
    count = lax.axis_size(axis)
    me = lax.axis_index(axis)
    stride = 1
    for radix in digit_radices(count):
        digit = me // stride % radix
        pieces = [block]
        for delta in range(1, radix):
            route = []
            for index in range(count):
                own_digit = index // stride % radix
                source = index + ((own_digit + delta) % radix - own_digit) * stride
                route.append((source, index))
            pieces.append(lax.ppermute(block, axis, route))
        stacked = jnp.roll(jnp.stack(pieces), digit, axis=0)
        block = stacked.reshape((radix * block.shape[0],) + block.shape[1:])
        stride *= radix
    return block


def gather_doubling(block, axis):
    count = lax.axis_size(axis)
    me = lax.axis_index(axis)
    stride = 1
    while stride < count:
        partner = from_partner(block, axis, stride.bit_length() - 1)
        upper = me // stride % 2 == 1
        block = jnp.where(upper, jnp.concatenate([partner, block]), jnp.concatenate([block, partner]))
        stride *= 2
    return block


def per_device(signal, band, response, offsets):
    blocks = lax.axis_size("tm")
    levels = blocks.bit_length() - 1
    device_pos = lax.axis_index("tm")
    phase_bin = reverse_bits(device_pos, levels)
    channel_count, length = signal.shape
    total_len = length * blocks
    inner_len = math.gcd(128, length // lax.axis_size("chan"))
    real_part = signal
    imag_part = jnp.zeros_like(signal)
    for bit_index in range(levels - 1, -1, -1):
        half_span = 1 << bit_index
        upper_half = device_pos // half_span % 2 == 1
        cosine, sine_part = twiddle(device_pos % half_span, 2 * half_span)
        if bit_index == levels - 1:
            partner_real = from_partner(real_part, "tm", bit_index)
            diff_real = partner_real - real_part
            imag_part = jnp.where(upper_half, diff_real * sine_part, 0.0)
            real_part = jnp.where(upper_half, diff_real * cosine, real_part + partner_real)
            continue
        partner = from_partner(jnp.stack([real_part, imag_part]), "tm", bit_index)
        diff_real = partner[0] - real_part
        diff_imag = partner[1] - imag_part
        new_real = jnp.where(
            upper_half, diff_real * cosine - diff_imag * sine_part, real_part + partner[0]
        )
        new_imag = jnp.where(
            upper_half, diff_real * sine_part + diff_imag * cosine, imag_part + partner[1]
        )
        real_part, imag_part = (new_real, new_imag)
    inner = LANES
    outer = length // inner
    own = channel_count
    band_width = band.shape[1]
    half_width = band_width // 2
    channel_all = band.shape[2]
    tables = local_tables(own, outer, inner, blocks, levels)
    spec_real, spec_imag = forward_call(
        real_part.reshape(own, outer, inner), imag_part.reshape(own, outer, inner), tables
    )
    packed = jnp.concatenate(
        [response.reshape(2 * band_width, -1), offsets.reshape(1, -1).astype(jnp.float32)], axis=0
    )
    table = gather_radix(packed[None], "chan")
    entries = table.shape[1]
    table = table.transpose(1, 0, 2).reshape(entries, inner, outer).transpose(0, 2, 1)
    responses = table[: 2 * band_width].reshape(2, band_width, outer, inner)
    shift = (table[2 * band_width].astype(jnp.int32) + half_width) % channel_all - half_width
    spectra = jnp.stack([spec_real, spec_imag])
    neighbours = [from_offset(spectra, "chan", delta) for delta in (-1, 1, 2, 3)]
    window = jnp.concatenate([neighbours[0], spectra] + neighbours[1:], axis=1)
    real_part, imag_part = inverse_call(window, shift, responses, band.reshape(-1), tables, own)
    real_part = real_part.reshape(own, length)
    imag_part = imag_part.reshape(own, length)
    for bit_index in range(levels):
        half_span = 1 << bit_index
        upper_half = device_pos // half_span % 2 == 1
        cosine, sine_part = twiddle(device_pos % half_span, 2 * half_span)
        sine_part = -sine_part
        if bit_index == levels - 1:
            own_prod = real_part * cosine - imag_part * sine_part
            partner_real = from_partner(jnp.where(upper_half, own_prod, real_part), "tm", bit_index)
            real_part = jnp.where(upper_half, partner_real - own_prod, real_part + partner_real)
            break
        partner = from_partner(jnp.stack([real_part, imag_part]), "tm", bit_index)
        base_real = jnp.where(upper_half, partner[0], real_part)
        base_imag = jnp.where(upper_half, partner[1], imag_part)
        scaled_real = jnp.where(upper_half, real_part, partner[0])
        scaled_imag = jnp.where(upper_half, imag_part, partner[1])
        prod_real = scaled_real * cosine - scaled_imag * sine_part
        prod_imag = scaled_real * sine_part + scaled_imag * cosine
        real_part = jnp.where(upper_half, base_real - prod_real, base_real + prod_real)
        imag_part = jnp.where(upper_half, base_imag - prod_imag, base_imag + prod_imag)
    smoothed = real_part / total_len
    return smoothed


def solution(mesh):
    in_specs = (P("chan", "tm"), P(), P(None, "tm", None, "chan"), P("tm", "chan"))
    out_specs = P("chan", "tm")
    return jax.shard_map(
        per_device, mesh=mesh, in_specs=in_specs, out_specs=out_specs, check_vma=False
    )
```

```python
import math

import numpy as np

import jax
import jax.numpy as jnp
from jax import lax
from jax.experimental import pallas as pl
from jax.experimental.pallas import tpu as pltpu
from jax.sharding import PartitionSpec as P

PRECISE = lax.Precision.HIGHEST


def from_partner(block, axis, stride):
    count = lax.axis_size(axis)
    route = []
    for low in range(count):
        high = low | 1 << stride
        if high != low and high < count:
            route += [(low, high), (high, low)]
    return lax.ppermute(block, axis, route)


def twiddle(numer, length):
    angle = -2.0 * math.pi / length * numer.astype(jnp.float32)
    return (jnp.cos(angle), jnp.sin(angle))


def dft_table(length):
    steps = lax.iota(jnp.int32, length)
    return twiddle(steps[:, None] * steps[None, :] % length, length)


def reverse_bits(value, bit_count):
    result = value * 0
    for bit_index in range(bit_count):
        result = result + value // (1 << bit_index) % 2 * (1 << bit_count - 1 - bit_index)
    return result


def complex_einsum(form, left_real, left_imag, right_real, right_imag):
    out_real = jnp.einsum(form, left_real, right_real, precision=PRECISE) - jnp.einsum(
        form, left_imag, right_imag, precision=PRECISE
    )
    out_imag = jnp.einsum(form, left_real, right_imag, precision=PRECISE) + jnp.einsum(
        form, left_imag, right_real, precision=PRECISE
    )
    return (out_real, out_imag)


def forward_local(real_part, imag_part, phase_bin, total_len, inner_len):
    channel_count, length = real_part.shape
    outer_len = length // inner_len
    sample_pos = lax.iota(jnp.int32, length)
    cosine, sine_part = twiddle(sample_pos * phase_bin % total_len, total_len)
    real_part, imag_part = (
        real_part * cosine - imag_part * sine_part,
        real_part * sine_part + imag_part * cosine,
    )
    real_part = real_part.reshape(channel_count, inner_len, outer_len)
    imag_part = imag_part.reshape(channel_count, inner_len, outer_len)
    table_real, table_imag = dft_table(inner_len)
    real_part, imag_part = complex_einsum(
        "cab,ak->cbk", real_part, imag_part, table_real, table_imag
    )
    outer_ids = lax.iota(jnp.int32, outer_len)[:, None]
    inner_ids = lax.iota(jnp.int32, inner_len)[None, :]
    cosine, sine_part = twiddle(outer_ids * inner_ids, length)
    real_part, imag_part = (
        real_part * cosine - imag_part * sine_part,
        real_part * sine_part + imag_part * cosine,
    )
    table_real, table_imag = dft_table(outer_len)
    return complex_einsum("cbk,bm->mck", real_part, imag_part, table_real, table_imag)


def inverse_local(spec_real, spec_imag, phase_bin, total_len):
    outer_len, channel_count, inner_len = spec_real.shape
    length = outer_len * inner_len
    table_real, table_imag = dft_table(outer_len)
    real_part, imag_part = complex_einsum(
        "mck,mb->cbk", spec_real, spec_imag, table_real, -table_imag
    )
    outer_ids = lax.iota(jnp.int32, outer_len)[:, None]
    inner_ids = lax.iota(jnp.int32, inner_len)[None, :]
    cosine, sine_part = twiddle(outer_ids * inner_ids, length)
    sine_part = -sine_part
    real_part, imag_part = (
        real_part * cosine - imag_part * sine_part,
        real_part * sine_part + imag_part * cosine,
    )
    table_real, table_imag = dft_table(inner_len)
    real_part, imag_part = complex_einsum(
        "cbk,ka->cab", real_part, imag_part, table_real, -table_imag
    )
    real_part = real_part.reshape(channel_count, length)
    imag_part = imag_part.reshape(channel_count, length)
    sample_pos = lax.iota(jnp.int32, length)
    cosine, sine_part = twiddle(sample_pos * phase_bin % total_len, total_len)
    sine_part = -sine_part
    return (real_part * cosine - imag_part * sine_part, real_part * sine_part + imag_part * cosine)


LANES = 128


def cdot(left_real, left_imag, right_real, right_imag):
    def dot(a, b):
        return jnp.dot(a, b, precision=PRECISE, preferred_element_type=jnp.float32)

    return (
        dot(left_real, right_real) - dot(left_imag, right_imag),
        dot(left_real, right_imag) + dot(left_imag, right_real),
    )


def forward_kernel(xr_ref, xi_ref, twr_ref, twi_ref, kr_ref, ki_ref, t2r_ref, t2i_ref, wr_ref, wi_ref, yr_ref, yi_ref):
    own, outer, inner = xr_ref.shape
    xr = xr_ref[...]
    xi = xi_ref[...]
    position = lax.axis_index("tm")
    twr = twr_ref[position][None]
    twi = twi_ref[position][None]
    ur = (xr * twr - xi * twi).reshape(own * outer, inner)
    ui = (xr * twi + xi * twr).reshape(own * outer, inner)
    zr, zi = cdot(kr_ref[...], ki_ref[...], ur, ui)
    t2r = t2r_ref[...]
    t2i = t2i_ref[...]
    zr, zi = (zr * t2r - zi * t2i, zr * t2i + zi * t2r)
    yr, yi = cdot(zr, zi, wr_ref[...], wi_ref[...])
    yr_ref[...] = yr.reshape(own, outer, inner)
    yi_ref[...] = yi.reshape(own, outer, inner)


def inverse_kernel(win_ref, shift_ref, resp_ref, band_ref, twr_ref, twi_ref, kr_ref, ki_ref, t2r_ref, t2i_ref, wr_ref, wi_ref, xr_ref, xi_ref):
    own, outer, inner = xr_ref.shape
    band_width = resp_ref.shape[1]
    half_width = band_width // 2
    span = own + band_width - 1
    shift = shift_ref[...]
    masks = [shift == amount for amount in range(-half_width, half_width + 1)]
    moved = []
    for row in range(span):
        mr = jnp.zeros((outer, inner), jnp.float32)
        mi = jnp.zeros((outer, inner), jnp.float32)
        for index, amount in enumerate(range(-half_width, half_width + 1)):
            source = own + amount + row
            mr = jnp.where(masks[index], win_ref[0, source], mr)
            mi = jnp.where(masks[index], win_ref[1, source], mi)
        moved.append((mr, mi))
    rows_real = []
    rows_imag = []
    channel_all = band_ref.shape[0] // (2 * band_width)
    first = lax.axis_index("chan") * own
    for channel in range(own):
        acc_r = jnp.zeros((outer, inner), jnp.float32)
        acc_i = jnp.zeros((outer, inner), jnp.float32)
        for lag in range(band_width):
            br = band_ref[lag * channel_all + first + channel]
            bi = band_ref[(band_width + lag) * channel_all + first + channel]
            rr = resp_ref[0, lag]
            ri = resp_ref[1, lag]
            cr = br * rr - bi * ri
            ci = br * ri + bi * rr
            vr, vi = moved[channel + lag]
            acc_r = acc_r + cr * vr - ci * vi
            acc_i = acc_i + cr * vi + ci * vr
        rows_real.append(acc_r)
        rows_imag.append(acc_i)
    mr = jnp.concatenate(rows_real, axis=0)
    mi = jnp.concatenate(rows_imag, axis=0)
    yr, yi = cdot(mr, mi, wr_ref[...], -wi_ref[...])
    t2r = t2r_ref[...]
    t2i = -t2i_ref[...]
    yr, yi = (yr * t2r - yi * t2i, yr * t2i + yi * t2r)
    xr, xi = cdot(kr_ref[...], -ki_ref[...], yr, yi)
    xr = xr.reshape(own, outer, inner)
    xi = xi.reshape(own, outer, inner)
    position = lax.axis_index("tm")
    twr = twr_ref[position][None]
    twi = -twi_ref[position][None]
    xr_ref[...] = xr * twr - xi * twi
    xi_ref[...] = xr * twi + xi * twr


def dft_constant(length, numer):
    angle = -2.0 * np.pi / length * (numer % length)
    return (np.cos(angle).astype(np.float32), np.sin(angle).astype(np.float32))


def local_tables(own, outer, inner, blocks, levels):
    length = outer * inner
    total_len = length * blocks
    rows = np.arange(outer)[:, None]
    cols = np.arange(inner)[None, :]
    residues = [reverse_bits(position, levels) for position in range(blocks)]
    phase = np.stack([(rows * inner + cols) * residue for residue in residues])
    twr, twi = dft_constant(total_len, phase)
    small_r, small_i = dft_constant(outer, rows * np.arange(outer)[None, :])
    eye = np.eye(own, dtype=np.float32)
    kr = np.kron(eye, small_r)
    ki = np.kron(eye, small_i)
    t2r, t2i = dft_constant(length, rows * cols)
    t2r = np.tile(t2r, (own, 1))
    t2i = np.tile(t2i, (own, 1))
    wr, wi = dft_constant(inner, np.arange(inner)[:, None] * cols)
    return tuple(jnp.asarray(table) for table in (twr, twi, kr, ki, t2r, t2i, wr, wi))


def vmem_specs(count):
    return [pl.BlockSpec(memory_space=pltpu.VMEM)] * count


def forward_call(xr, xi, tables):
    shape = jax.ShapeDtypeStruct(xr.shape, jnp.float32)
    return pl.pallas_call(
        forward_kernel,
        out_shape=(shape, shape),
        in_specs=vmem_specs(2 + len(tables)),
        out_specs=tuple(vmem_specs(2)),
    )(xr, xi, *tables)


def inverse_call(window, shift, responses, band_flat, tables, own):
    shape = jax.ShapeDtypeStruct((own,) + window.shape[2:], jnp.float32)
    specs = vmem_specs(3) + [pl.BlockSpec(memory_space=pltpu.SMEM)] + vmem_specs(len(tables))
    return pl.pallas_call(
        inverse_kernel,
        out_shape=(shape, shape),
        in_specs=specs,
        out_specs=tuple(vmem_specs(2)),
    )(window, shift, responses, band_flat, *tables)


def from_offset(block, axis, delta):
    count = lax.axis_size(axis)
    return lax.ppermute(block, axis, [((i + delta) % count, i) for i in range(count)])


def digit_radices(count):
    radices = []
    for radix in (2, 4, 4):
        if count % radix == 0 and count > 1:
            radices.append(radix)
            count //= radix
    while count > 1:
        radices.append(2)
        count //= 2
    return radices


def gather_radix(block, axis):
    count = lax.axis_size(axis)
    me = lax.axis_index(axis)
    stride = 1
    for radix in digit_radices(count):
        digit = me // stride % radix
        pieces = [block]
        for delta in range(1, radix):
            route = []
            for index in range(count):
                own_digit = index // stride % radix
                source = index + ((own_digit + delta) % radix - own_digit) * stride
                route.append((source, index))
            pieces.append(lax.ppermute(block, axis, route))
        stacked = jnp.roll(jnp.stack(pieces), digit, axis=0)
        block = stacked.reshape((radix * block.shape[0],) + block.shape[1:])
        stride *= radix
    return block


def gather_doubling(block, axis):
    count = lax.axis_size(axis)
    me = lax.axis_index(axis)
    stride = 1
    while stride < count:
        partner = from_partner(block, axis, stride.bit_length() - 1)
        upper = me // stride % 2 == 1
        block = jnp.where(upper, jnp.concatenate([partner, block]), jnp.concatenate([block, partner]))
        stride *= 2
    return block


def per_device(signal, band, response, offsets):
    blocks = lax.axis_size("tm")
    levels = blocks.bit_length() - 1
    device_pos = lax.axis_index("tm")
    phase_bin = reverse_bits(device_pos, levels)
    channel_count, length = signal.shape
    total_len = length * blocks
    inner_len = math.gcd(128, length // lax.axis_size("chan"))
    real_part = signal
    imag_part = jnp.zeros_like(signal)
    for bit_index in range(levels - 1, -1, -1):
        half_span = 1 << bit_index
        upper_half = device_pos // half_span % 2 == 1
        cosine, sine_part = twiddle(device_pos % half_span, 2 * half_span)
        if bit_index == levels - 1:
            partner_real = from_partner(real_part, "tm", bit_index)
            diff_real = partner_real - real_part
            imag_part = jnp.where(upper_half, diff_real * sine_part, 0.0)
            real_part = jnp.where(upper_half, diff_real * cosine, real_part + partner_real)
            continue
        partner = from_partner(jnp.stack([real_part, imag_part]), "tm", bit_index)
        diff_real = partner[0] - real_part
        diff_imag = partner[1] - imag_part
        new_real = jnp.where(
            upper_half, diff_real * cosine - diff_imag * sine_part, real_part + partner[0]
        )
        new_imag = jnp.where(
            upper_half, diff_real * sine_part + diff_imag * cosine, imag_part + partner[1]
        )
        real_part, imag_part = (new_real, new_imag)
    inner = LANES
    outer = length // inner
    own = channel_count
    band_width = band.shape[1]
    half_width = band_width // 2
    channel_all = band.shape[2]
    tables = local_tables(own, outer, inner, blocks, levels)
    spec_real, spec_imag = forward_call(
        real_part.reshape(own, outer, inner), imag_part.reshape(own, outer, inner), tables
    )
    packed = jnp.concatenate(
        [response.reshape(2 * band_width, -1), offsets.reshape(1, -1).astype(jnp.float32)], axis=0
    )
    packed, _ = lax.optimization_barrier((packed, real_part))
    table = gather_radix(packed[None], "chan")
    entries = table.shape[1]
    table = table.transpose(1, 0, 2).reshape(entries, inner, outer).transpose(0, 2, 1)
    responses = table[: 2 * band_width].reshape(2, band_width, outer, inner)
    shift = (table[2 * band_width].astype(jnp.int32) + half_width) % channel_all - half_width
    spectra = jnp.stack([spec_real, spec_imag])
    neighbours = [from_offset(spectra, "chan", delta) for delta in (-1, 1, 2, 3)]
    window = jnp.concatenate([neighbours[0], spectra] + neighbours[1:], axis=1)
    real_part, imag_part = inverse_call(window, shift, responses, band.reshape(-1), tables, own)
    real_part = real_part.reshape(own, length)
    imag_part = imag_part.reshape(own, length)
    for bit_index in range(levels):
        half_span = 1 << bit_index
        upper_half = device_pos // half_span % 2 == 1
        cosine, sine_part = twiddle(device_pos % half_span, 2 * half_span)
        sine_part = -sine_part
        if bit_index == levels - 1:
            own_prod = real_part * cosine - imag_part * sine_part
            partner_real = from_partner(jnp.where(upper_half, own_prod, real_part), "tm", bit_index)
            real_part = jnp.where(upper_half, partner_real - own_prod, real_part + partner_real)
            break
        partner = from_partner(jnp.stack([real_part, imag_part]), "tm", bit_index)
        base_real = jnp.where(upper_half, partner[0], real_part)
        base_imag = jnp.where(upper_half, partner[1], imag_part)
        scaled_real = jnp.where(upper_half, real_part, partner[0])
        scaled_imag = jnp.where(upper_half, imag_part, partner[1])
        prod_real = scaled_real * cosine - scaled_imag * sine_part
        prod_imag = scaled_real * sine_part + scaled_imag * cosine
        real_part = jnp.where(upper_half, base_real - prod_real, base_real + prod_real)
        imag_part = jnp.where(upper_half, base_imag - prod_imag, base_imag + prod_imag)
    smoothed = real_part / total_len
    return smoothed


def solution(mesh):
    in_specs = (P("chan", "tm"), P(), P(None, "tm", None, "chan"), P("tm", "chan"))
    out_specs = P("chan", "tm")
    return jax.shard_map(
        per_device, mesh=mesh, in_specs=in_specs, out_specs=out_specs, check_vma=False
    )
```

```python
import math

import numpy as np

import jax
import jax.numpy as jnp
from jax import lax
from jax.experimental import pallas as pl
from jax.experimental.pallas import tpu as pltpu
from jax.sharding import PartitionSpec as P

PRECISE = lax.Precision.HIGHEST


def from_partner(block, axis, stride):
    count = lax.axis_size(axis)
    route = []
    for low in range(count):
        high = low | 1 << stride
        if high != low and high < count:
            route += [(low, high), (high, low)]
    return lax.ppermute(block, axis, route)


def twiddle(numer, length):
    angle = -2.0 * math.pi / length * numer.astype(jnp.float32)
    return (jnp.cos(angle), jnp.sin(angle))


def dft_table(length):
    steps = lax.iota(jnp.int32, length)
    return twiddle(steps[:, None] * steps[None, :] % length, length)


def reverse_bits(value, bit_count):
    result = value * 0
    for bit_index in range(bit_count):
        result = result + value // (1 << bit_index) % 2 * (1 << bit_count - 1 - bit_index)
    return result


def complex_einsum(form, left_real, left_imag, right_real, right_imag):
    out_real = jnp.einsum(form, left_real, right_real, precision=PRECISE) - jnp.einsum(
        form, left_imag, right_imag, precision=PRECISE
    )
    out_imag = jnp.einsum(form, left_real, right_imag, precision=PRECISE) + jnp.einsum(
        form, left_imag, right_real, precision=PRECISE
    )
    return (out_real, out_imag)


def forward_local(real_part, imag_part, phase_bin, total_len, inner_len):
    channel_count, length = real_part.shape
    outer_len = length // inner_len
    sample_pos = lax.iota(jnp.int32, length)
    cosine, sine_part = twiddle(sample_pos * phase_bin % total_len, total_len)
    real_part, imag_part = (
        real_part * cosine - imag_part * sine_part,
        real_part * sine_part + imag_part * cosine,
    )
    real_part = real_part.reshape(channel_count, inner_len, outer_len)
    imag_part = imag_part.reshape(channel_count, inner_len, outer_len)
    table_real, table_imag = dft_table(inner_len)
    real_part, imag_part = complex_einsum(
        "cab,ak->cbk", real_part, imag_part, table_real, table_imag
    )
    outer_ids = lax.iota(jnp.int32, outer_len)[:, None]
    inner_ids = lax.iota(jnp.int32, inner_len)[None, :]
    cosine, sine_part = twiddle(outer_ids * inner_ids, length)
    real_part, imag_part = (
        real_part * cosine - imag_part * sine_part,
        real_part * sine_part + imag_part * cosine,
    )
    table_real, table_imag = dft_table(outer_len)
    return complex_einsum("cbk,bm->mck", real_part, imag_part, table_real, table_imag)


def inverse_local(spec_real, spec_imag, phase_bin, total_len):
    outer_len, channel_count, inner_len = spec_real.shape
    length = outer_len * inner_len
    table_real, table_imag = dft_table(outer_len)
    real_part, imag_part = complex_einsum(
        "mck,mb->cbk", spec_real, spec_imag, table_real, -table_imag
    )
    outer_ids = lax.iota(jnp.int32, outer_len)[:, None]
    inner_ids = lax.iota(jnp.int32, inner_len)[None, :]
    cosine, sine_part = twiddle(outer_ids * inner_ids, length)
    sine_part = -sine_part
    real_part, imag_part = (
        real_part * cosine - imag_part * sine_part,
        real_part * sine_part + imag_part * cosine,
    )
    table_real, table_imag = dft_table(inner_len)
    real_part, imag_part = complex_einsum(
        "cbk,ka->cab", real_part, imag_part, table_real, -table_imag
    )
    real_part = real_part.reshape(channel_count, length)
    imag_part = imag_part.reshape(channel_count, length)
    sample_pos = lax.iota(jnp.int32, length)
    cosine, sine_part = twiddle(sample_pos * phase_bin % total_len, total_len)
    sine_part = -sine_part
    return (real_part * cosine - imag_part * sine_part, real_part * sine_part + imag_part * cosine)


LANES = 128


def cdot(left_real, left_imag, right_real, right_imag):
    def dot(a, b):
        return jnp.dot(a, b, precision=PRECISE, preferred_element_type=jnp.float32)

    return (
        dot(left_real, right_real) - dot(left_imag, right_imag),
        dot(left_real, right_imag) + dot(left_imag, right_real),
    )


def forward_kernel(xr_ref, xi_ref, twr_ref, twi_ref, kr_ref, ki_ref, t2r_ref, t2i_ref, wr_ref, wi_ref, yr_ref, yi_ref):
    own, outer, inner = xr_ref.shape
    xr = xr_ref[...]
    xi = xi_ref[...]
    position = lax.axis_index("tm")
    twr = twr_ref[position][None]
    twi = twi_ref[position][None]
    ur = (xr * twr - xi * twi).reshape(own * outer, inner)
    ui = (xr * twi + xi * twr).reshape(own * outer, inner)
    zr, zi = cdot(kr_ref[...], ki_ref[...], ur, ui)
    t2r = t2r_ref[...]
    t2i = t2i_ref[...]
    zr, zi = (zr * t2r - zi * t2i, zr * t2i + zi * t2r)
    yr, yi = cdot(zr, zi, wr_ref[...], wi_ref[...])
    yr_ref[...] = yr.reshape(own, outer, inner)
    yi_ref[...] = yi.reshape(own, outer, inner)


def inverse_kernel(win_ref, shift_ref, resp_ref, band_ref, twr_ref, twi_ref, kr_ref, ki_ref, t2r_ref, t2i_ref, wr_ref, wi_ref, xr_ref, xi_ref):
    own, outer, inner = xr_ref.shape
    band_width = resp_ref.shape[1]
    half_width = band_width // 2
    span = own + band_width - 1
    shift = shift_ref[...]
    masks = [shift == amount for amount in range(-half_width, half_width + 1)]
    moved = []
    for row in range(span):
        mr = jnp.zeros((outer, inner), jnp.float32)
        mi = jnp.zeros((outer, inner), jnp.float32)
        for index, amount in enumerate(range(-half_width, half_width + 1)):
            source = own + amount + row
            mr = jnp.where(masks[index], win_ref[0, source], mr)
            mi = jnp.where(masks[index], win_ref[1, source], mi)
        moved.append((mr, mi))
    rows_real = []
    rows_imag = []
    channel_all = band_ref.shape[0] // (2 * band_width)
    first = lax.axis_index("chan") * own
    for channel in range(own):
        acc_r = jnp.zeros((outer, inner), jnp.float32)
        acc_i = jnp.zeros((outer, inner), jnp.float32)
        for lag in range(band_width):
            br = band_ref[lag * channel_all + first + channel]
            bi = band_ref[(band_width + lag) * channel_all + first + channel]
            rr = resp_ref[0, lag]
            ri = resp_ref[1, lag]
            cr = br * rr - bi * ri
            ci = br * ri + bi * rr
            vr, vi = moved[channel + lag]
            acc_r = acc_r + cr * vr - ci * vi
            acc_i = acc_i + cr * vi + ci * vr
        rows_real.append(acc_r)
        rows_imag.append(acc_i)
    mr = jnp.concatenate(rows_real, axis=0)
    mi = jnp.concatenate(rows_imag, axis=0)
    yr, yi = cdot(mr, mi, wr_ref[...], -wi_ref[...])
    t2r = t2r_ref[...]
    t2i = -t2i_ref[...]
    yr, yi = (yr * t2r - yi * t2i, yr * t2i + yi * t2r)
    xr, xi = cdot(kr_ref[...], -ki_ref[...], yr, yi)
    xr = xr.reshape(own, outer, inner)
    xi = xi.reshape(own, outer, inner)
    position = lax.axis_index("tm")
    twr = twr_ref[position][None]
    twi = -twi_ref[position][None]
    xr_ref[...] = xr * twr - xi * twi
    xi_ref[...] = xr * twi + xi * twr


def dft_constant(length, numer):
    angle = -2.0 * np.pi / length * (numer % length)
    return (np.cos(angle).astype(np.float32), np.sin(angle).astype(np.float32))


def local_tables(own, outer, inner, blocks, levels):
    length = outer * inner
    total_len = length * blocks
    rows = np.arange(outer)[:, None]
    cols = np.arange(inner)[None, :]
    residues = [reverse_bits(position, levels) for position in range(blocks)]
    phase = np.stack([(rows * inner + cols) * residue for residue in residues])
    twr, twi = dft_constant(total_len, phase)
    small_r, small_i = dft_constant(outer, rows * np.arange(outer)[None, :])
    eye = np.eye(own, dtype=np.float32)
    kr = np.kron(eye, small_r)
    ki = np.kron(eye, small_i)
    t2r, t2i = dft_constant(length, rows * cols)
    t2r = np.tile(t2r, (own, 1))
    t2i = np.tile(t2i, (own, 1))
    wr, wi = dft_constant(inner, np.arange(inner)[:, None] * cols)
    return tuple(jnp.asarray(table) for table in (twr, twi, kr, ki, t2r, t2i, wr, wi))


def vmem_specs(count):
    return [pl.BlockSpec(memory_space=pltpu.VMEM)] * count


def forward_call(xr, xi, tables):
    shape = jax.ShapeDtypeStruct(xr.shape, jnp.float32)
    return pl.pallas_call(
        forward_kernel,
        out_shape=(shape, shape),
        in_specs=vmem_specs(2 + len(tables)),
        out_specs=tuple(vmem_specs(2)),
    )(xr, xi, *tables)


def inverse_call(window, shift, responses, band_flat, tables, own):
    shape = jax.ShapeDtypeStruct((own,) + window.shape[2:], jnp.float32)
    specs = vmem_specs(3) + [pl.BlockSpec(memory_space=pltpu.SMEM)] + vmem_specs(len(tables))
    return pl.pallas_call(
        inverse_kernel,
        out_shape=(shape, shape),
        in_specs=specs,
        out_specs=tuple(vmem_specs(2)),
    )(window, shift, responses, band_flat, *tables)


def from_offset(block, axis, delta):
    count = lax.axis_size(axis)
    return lax.ppermute(block, axis, [((i + delta) % count, i) for i in range(count)])


def digit_radices(count):
    radices = []
    for radix in (2, 4, 4):
        if count % radix == 0 and count > 1:
            radices.append(radix)
            count //= radix
    while count > 1:
        radices.append(2)
        count //= 2
    return radices


def gather_radix(block, axis):
    count = lax.axis_size(axis)
    me = lax.axis_index(axis)
    stride = 1
    for radix in digit_radices(count):
        digit = me // stride % radix
        pieces = [block]
        for delta in range(1, radix):
            route = []
            for index in range(count):
                own_digit = index // stride % radix
                source = index + ((own_digit + delta) % radix - own_digit) * stride
                route.append((source, index))
            pieces.append(lax.ppermute(block, axis, route))
        stacked = jnp.roll(jnp.stack(pieces), digit, axis=0)
        block = stacked.reshape((radix * block.shape[0],) + block.shape[1:])
        stride *= radix
    return block


def gather_doubling(block, axis):
    count = lax.axis_size(axis)
    me = lax.axis_index(axis)
    stride = 1
    while stride < count:
        partner = from_partner(block, axis, stride.bit_length() - 1)
        upper = me // stride % 2 == 1
        block = jnp.where(upper, jnp.concatenate([partner, block]), jnp.concatenate([block, partner]))
        stride *= 2
    return block


def per_device(signal, band, response, offsets):
    blocks = lax.axis_size("tm")
    levels = blocks.bit_length() - 1
    device_pos = lax.axis_index("tm")
    phase_bin = reverse_bits(device_pos, levels)
    channel_count, length = signal.shape
    total_len = length * blocks
    inner_len = math.gcd(128, length // lax.axis_size("chan"))
    real_part = signal
    imag_part = jnp.zeros_like(signal)
    for bit_index in range(levels - 1, -1, -1):
        half_span = 1 << bit_index
        upper_half = device_pos // half_span % 2 == 1
        cosine, sine_part = twiddle(device_pos % half_span, 2 * half_span)
        if bit_index == levels - 1:
            partner_real = from_partner(real_part, "tm", bit_index)
            diff_real = partner_real - real_part
            imag_part = jnp.where(upper_half, diff_real * sine_part, 0.0)
            real_part = jnp.where(upper_half, diff_real * cosine, real_part + partner_real)
            continue
        partner = from_partner(jnp.stack([real_part, imag_part]), "tm", bit_index)
        diff_real = partner[0] - real_part
        diff_imag = partner[1] - imag_part
        new_real = jnp.where(
            upper_half, diff_real * cosine - diff_imag * sine_part, real_part + partner[0]
        )
        new_imag = jnp.where(
            upper_half, diff_real * sine_part + diff_imag * cosine, imag_part + partner[1]
        )
        real_part, imag_part = (new_real, new_imag)
    inner = LANES
    outer = length // inner
    own = channel_count
    band_width = band.shape[1]
    half_width = band_width // 2
    channel_all = band.shape[2]
    tables = local_tables(own, outer, inner, blocks, levels)
    spec_real, spec_imag = forward_call(
        real_part.reshape(own, outer, inner), imag_part.reshape(own, outer, inner), tables
    )
    packed = jnp.concatenate(
        [response.reshape(2 * band_width, -1), offsets.reshape(1, -1).astype(jnp.float32)], axis=0
    )
    peers = lax.axis_size("chan")
    table = lax.all_to_all(jnp.broadcast_to(packed[None], (peers,) + packed.shape), "chan", 0, 0, tiled=True)
    entries = table.shape[1]
    table = table.transpose(1, 0, 2).reshape(entries, inner, outer).transpose(0, 2, 1)
    responses = table[: 2 * band_width].reshape(2, band_width, outer, inner)
    shift = (table[2 * band_width].astype(jnp.int32) + half_width) % channel_all - half_width
    spectra = jnp.stack([spec_real, spec_imag])
    neighbours = [from_offset(spectra, "chan", delta) for delta in (-1, 1, 2, 3)]
    window = jnp.concatenate([neighbours[0], spectra] + neighbours[1:], axis=1)
    real_part, imag_part = inverse_call(window, shift, responses, band.reshape(-1), tables, own)
    real_part = real_part.reshape(own, length)
    imag_part = imag_part.reshape(own, length)
    for bit_index in range(levels):
        half_span = 1 << bit_index
        upper_half = device_pos // half_span % 2 == 1
        cosine, sine_part = twiddle(device_pos % half_span, 2 * half_span)
        sine_part = -sine_part
        if bit_index == levels - 1:
            own_prod = real_part * cosine - imag_part * sine_part
            partner_real = from_partner(jnp.where(upper_half, own_prod, real_part), "tm", bit_index)
            real_part = jnp.where(upper_half, partner_real - own_prod, real_part + partner_real)
            break
        partner = from_partner(jnp.stack([real_part, imag_part]), "tm", bit_index)
        base_real = jnp.where(upper_half, partner[0], real_part)
        base_imag = jnp.where(upper_half, partner[1], imag_part)
        scaled_real = jnp.where(upper_half, real_part, partner[0])
        scaled_imag = jnp.where(upper_half, imag_part, partner[1])
        prod_real = scaled_real * cosine - scaled_imag * sine_part
        prod_imag = scaled_real * sine_part + scaled_imag * cosine
        real_part = jnp.where(upper_half, base_real - prod_real, base_real + prod_real)
        imag_part = jnp.where(upper_half, base_imag - prod_imag, base_imag + prod_imag)
    smoothed = real_part / total_len
    return smoothed


def solution(mesh):
    in_specs = (P("chan", "tm"), P(), P(None, "tm", None, "chan"), P("tm", "chan"))
    out_specs = P("chan", "tm")
    return jax.shard_map(
        per_device, mesh=mesh, in_specs=in_specs, out_specs=out_specs, check_vma=False
    )
```

```python
import math

import numpy as np

import jax
import jax.numpy as jnp
from jax import lax
from jax.experimental import pallas as pl
from jax.experimental.pallas import tpu as pltpu
from jax.sharding import PartitionSpec as P

PRECISE = lax.Precision.HIGHEST


def from_partner(block, axis, stride):
    count = lax.axis_size(axis)
    route = []
    for low in range(count):
        high = low | 1 << stride
        if high != low and high < count:
            route += [(low, high), (high, low)]
    return lax.ppermute(block, axis, route)


def twiddle(numer, length):
    angle = -2.0 * math.pi / length * numer.astype(jnp.float32)
    return (jnp.cos(angle), jnp.sin(angle))


def dft_table(length):
    steps = lax.iota(jnp.int32, length)
    return twiddle(steps[:, None] * steps[None, :] % length, length)


def reverse_bits(value, bit_count):
    result = value * 0
    for bit_index in range(bit_count):
        result = result + value // (1 << bit_index) % 2 * (1 << bit_count - 1 - bit_index)
    return result


def complex_einsum(form, left_real, left_imag, right_real, right_imag):
    out_real = jnp.einsum(form, left_real, right_real, precision=PRECISE) - jnp.einsum(
        form, left_imag, right_imag, precision=PRECISE
    )
    out_imag = jnp.einsum(form, left_real, right_imag, precision=PRECISE) + jnp.einsum(
        form, left_imag, right_real, precision=PRECISE
    )
    return (out_real, out_imag)


def forward_local(real_part, imag_part, phase_bin, total_len, inner_len):
    channel_count, length = real_part.shape
    outer_len = length // inner_len
    sample_pos = lax.iota(jnp.int32, length)
    cosine, sine_part = twiddle(sample_pos * phase_bin % total_len, total_len)
    real_part, imag_part = (
        real_part * cosine - imag_part * sine_part,
        real_part * sine_part + imag_part * cosine,
    )
    real_part = real_part.reshape(channel_count, inner_len, outer_len)
    imag_part = imag_part.reshape(channel_count, inner_len, outer_len)
    table_real, table_imag = dft_table(inner_len)
    real_part, imag_part = complex_einsum(
        "cab,ak->cbk", real_part, imag_part, table_real, table_imag
    )
    outer_ids = lax.iota(jnp.int32, outer_len)[:, None]
    inner_ids = lax.iota(jnp.int32, inner_len)[None, :]
    cosine, sine_part = twiddle(outer_ids * inner_ids, length)
    real_part, imag_part = (
        real_part * cosine - imag_part * sine_part,
        real_part * sine_part + imag_part * cosine,
    )
    table_real, table_imag = dft_table(outer_len)
    return complex_einsum("cbk,bm->mck", real_part, imag_part, table_real, table_imag)


def inverse_local(spec_real, spec_imag, phase_bin, total_len):
    outer_len, channel_count, inner_len = spec_real.shape
    length = outer_len * inner_len
    table_real, table_imag = dft_table(outer_len)
    real_part, imag_part = complex_einsum(
        "mck,mb->cbk", spec_real, spec_imag, table_real, -table_imag
    )
    outer_ids = lax.iota(jnp.int32, outer_len)[:, None]
    inner_ids = lax.iota(jnp.int32, inner_len)[None, :]
    cosine, sine_part = twiddle(outer_ids * inner_ids, length)
    sine_part = -sine_part
    real_part, imag_part = (
        real_part * cosine - imag_part * sine_part,
        real_part * sine_part + imag_part * cosine,
    )
    table_real, table_imag = dft_table(inner_len)
    real_part, imag_part = complex_einsum(
        "cbk,ka->cab", real_part, imag_part, table_real, -table_imag
    )
    real_part = real_part.reshape(channel_count, length)
    imag_part = imag_part.reshape(channel_count, length)
    sample_pos = lax.iota(jnp.int32, length)
    cosine, sine_part = twiddle(sample_pos * phase_bin % total_len, total_len)
    sine_part = -sine_part
    return (real_part * cosine - imag_part * sine_part, real_part * sine_part + imag_part * cosine)


LANES = 128


def cdot(left_real, left_imag, right_real, right_imag):
    def dot(a, b):
        return jnp.dot(a, b, precision=PRECISE, preferred_element_type=jnp.float32)

    return (
        dot(left_real, right_real) - dot(left_imag, right_imag),
        dot(left_real, right_imag) + dot(left_imag, right_real),
    )


def forward_kernel(xr_ref, xi_ref, twr_ref, twi_ref, kr_ref, ki_ref, t2r_ref, t2i_ref, wr_ref, wi_ref, yr_ref, yi_ref):
    own, outer, inner = xr_ref.shape
    xr = xr_ref[...]
    xi = xi_ref[...]
    position = lax.axis_index("tm")
    twr = twr_ref[position][None]
    twi = twi_ref[position][None]
    ur = (xr * twr - xi * twi).reshape(own * outer, inner)
    ui = (xr * twi + xi * twr).reshape(own * outer, inner)
    zr, zi = cdot(kr_ref[...], ki_ref[...], ur, ui)
    t2r = t2r_ref[...]
    t2i = t2i_ref[...]
    zr, zi = (zr * t2r - zi * t2i, zr * t2i + zi * t2r)
    yr, yi = cdot(zr, zi, wr_ref[...], wi_ref[...])
    yr_ref[...] = yr.reshape(own, outer, inner)
    yi_ref[...] = yi.reshape(own, outer, inner)


def inverse_kernel(win_ref, shift_ref, resp_ref, band_ref, twr_ref, twi_ref, kr_ref, ki_ref, t2r_ref, t2i_ref, wr_ref, wi_ref, xr_ref, xi_ref):
    own, outer, inner = xr_ref.shape
    band_width = resp_ref.shape[1]
    half_width = band_width // 2
    span = own + band_width - 1
    shift = shift_ref[...]
    masks = [shift == amount for amount in range(-half_width, half_width + 1)]
    moved = []
    for row in range(span):
        mr = jnp.zeros((outer, inner), jnp.float32)
        mi = jnp.zeros((outer, inner), jnp.float32)
        for index, amount in enumerate(range(-half_width, half_width + 1)):
            source = own + amount + row
            mr = jnp.where(masks[index], win_ref[0, source], mr)
            mi = jnp.where(masks[index], win_ref[1, source], mi)
        moved.append((mr, mi))
    rows_real = []
    rows_imag = []
    channel_all = band_ref.shape[0] // (2 * band_width)
    first = lax.axis_index("chan") * own
    for channel in range(own):
        acc_r = jnp.zeros((outer, inner), jnp.float32)
        acc_i = jnp.zeros((outer, inner), jnp.float32)
        for lag in range(band_width):
            br = band_ref[lag * channel_all + first + channel]
            bi = band_ref[(band_width + lag) * channel_all + first + channel]
            rr = resp_ref[0, lag]
            ri = resp_ref[1, lag]
            cr = br * rr - bi * ri
            ci = br * ri + bi * rr
            vr, vi = moved[channel + lag]
            acc_r = acc_r + cr * vr - ci * vi
            acc_i = acc_i + cr * vi + ci * vr
        rows_real.append(acc_r)
        rows_imag.append(acc_i)
    mr = jnp.concatenate(rows_real, axis=0)
    mi = jnp.concatenate(rows_imag, axis=0)
    yr, yi = cdot(mr, mi, wr_ref[...], -wi_ref[...])
    t2r = t2r_ref[...]
    t2i = -t2i_ref[...]
    yr, yi = (yr * t2r - yi * t2i, yr * t2i + yi * t2r)
    xr, xi = cdot(kr_ref[...], -ki_ref[...], yr, yi)
    xr = xr.reshape(own, outer, inner)
    xi = xi.reshape(own, outer, inner)
    position = lax.axis_index("tm")
    twr = twr_ref[position][None]
    twi = -twi_ref[position][None]
    xr_ref[...] = xr * twr - xi * twi
    xi_ref[...] = xr * twi + xi * twr


def dft_constant(length, numer):
    angle = -2.0 * np.pi / length * (numer % length)
    return (np.cos(angle).astype(np.float32), np.sin(angle).astype(np.float32))


def local_tables(own, outer, inner, blocks, levels):
    length = outer * inner
    total_len = length * blocks
    rows = np.arange(outer)[:, None]
    cols = np.arange(inner)[None, :]
    residues = [reverse_bits(position, levels) for position in range(blocks)]
    phase = np.stack([(rows * inner + cols) * residue for residue in residues])
    twr, twi = dft_constant(total_len, phase)
    small_r, small_i = dft_constant(outer, rows * np.arange(outer)[None, :])
    eye = np.eye(own, dtype=np.float32)
    kr = np.kron(eye, small_r)
    ki = np.kron(eye, small_i)
    t2r, t2i = dft_constant(length, rows * cols)
    t2r = np.tile(t2r, (own, 1))
    t2i = np.tile(t2i, (own, 1))
    wr, wi = dft_constant(inner, np.arange(inner)[:, None] * cols)
    return tuple(jnp.asarray(table) for table in (twr, twi, kr, ki, t2r, t2i, wr, wi))


def vmem_specs(count):
    return [pl.BlockSpec(memory_space=pltpu.VMEM)] * count


def forward_call(xr, xi, tables):
    shape = jax.ShapeDtypeStruct(xr.shape, jnp.float32)
    return pl.pallas_call(
        forward_kernel,
        out_shape=(shape, shape),
        in_specs=vmem_specs(2 + len(tables)),
        out_specs=tuple(vmem_specs(2)),
    )(xr, xi, *tables)


def inverse_call(window, shift, responses, band_flat, tables, own):
    shape = jax.ShapeDtypeStruct((own,) + window.shape[2:], jnp.float32)
    specs = vmem_specs(3) + [pl.BlockSpec(memory_space=pltpu.SMEM)] + vmem_specs(len(tables))
    return pl.pallas_call(
        inverse_kernel,
        out_shape=(shape, shape),
        in_specs=specs,
        out_specs=tuple(vmem_specs(2)),
    )(window, shift, responses, band_flat, *tables)


def from_offset(block, axis, delta):
    count = lax.axis_size(axis)
    return lax.ppermute(block, axis, [((i + delta) % count, i) for i in range(count)])


def digit_radices(count):
    radices = []
    for radix in (2, 4, 4):
        if count % radix == 0 and count > 1:
            radices.append(radix)
            count //= radix
    while count > 1:
        radices.append(2)
        count //= 2
    return radices


def gather_radix(block, axis):
    count = lax.axis_size(axis)
    me = lax.axis_index(axis)
    stride = 1
    for radix in digit_radices(count):
        digit = me // stride % radix
        pieces = [block]
        for delta in range(1, radix):
            route = []
            for index in range(count):
                own_digit = index // stride % radix
                source = index + ((own_digit + delta) % radix - own_digit) * stride
                route.append((source, index))
            pieces.append(lax.ppermute(block, axis, route))
        stacked = jnp.roll(jnp.stack(pieces), digit, axis=0)
        block = stacked.reshape((radix * block.shape[0],) + block.shape[1:])
        stride *= radix
    return block


def gather_doubling(block, axis):
    count = lax.axis_size(axis)
    me = lax.axis_index(axis)
    stride = 1
    while stride < count:
        partner = from_partner(block, axis, stride.bit_length() - 1)
        upper = me // stride % 2 == 1
        block = jnp.where(upper, jnp.concatenate([partner, block]), jnp.concatenate([block, partner]))
        stride *= 2
    return block


def per_device(signal, band, response, offsets):
    blocks = lax.axis_size("tm")
    levels = blocks.bit_length() - 1
    device_pos = lax.axis_index("tm")
    phase_bin = reverse_bits(device_pos, levels)
    channel_count, length = signal.shape
    total_len = length * blocks
    inner_len = math.gcd(128, length // lax.axis_size("chan"))
    real_part = signal
    imag_part = jnp.zeros_like(signal)
    for bit_index in range(levels - 1, -1, -1):
        half_span = 1 << bit_index
        upper_half = device_pos // half_span % 2 == 1
        cosine, sine_part = twiddle(device_pos % half_span, 2 * half_span)
        if bit_index == levels - 1:
            partner_real = from_partner(real_part, "tm", bit_index)
            diff_real = partner_real - real_part
            imag_part = jnp.where(upper_half, diff_real * sine_part, 0.0)
            real_part = jnp.where(upper_half, diff_real * cosine, real_part + partner_real)
            continue
        partner = from_partner(jnp.stack([real_part, imag_part]), "tm", bit_index)
        diff_real = partner[0] - real_part
        diff_imag = partner[1] - imag_part
        new_real = jnp.where(
            upper_half, diff_real * cosine - diff_imag * sine_part, real_part + partner[0]
        )
        new_imag = jnp.where(
            upper_half, diff_real * sine_part + diff_imag * cosine, imag_part + partner[1]
        )
        real_part, imag_part = (new_real, new_imag)
    inner = LANES
    outer = length // inner
    own = channel_count
    band_width = band.shape[1]
    half_width = band_width // 2
    channel_all = band.shape[2]
    tables = local_tables(own, outer, inner, blocks, levels)
    spec_real, spec_imag = forward_call(
        real_part.reshape(own, outer, inner), imag_part.reshape(own, outer, inner), tables
    )
    packed = jnp.concatenate(
        [response.reshape(2 * band_width, -1), offsets.reshape(1, -1).astype(jnp.float32)], axis=0
    )
    packed, _ = lax.optimization_barrier((packed, spec_real))
    peers = lax.axis_size("chan")
    table = lax.all_to_all(jnp.broadcast_to(packed[None], (peers,) + packed.shape), "chan", 0, 0, tiled=True)
    entries = table.shape[1]
    table = table.transpose(1, 0, 2).reshape(entries, inner, outer).transpose(0, 2, 1)
    responses = table[: 2 * band_width].reshape(2, band_width, outer, inner)
    shift = (table[2 * band_width].astype(jnp.int32) + half_width) % channel_all - half_width
    spectra = jnp.stack([spec_real, spec_imag])
    neighbours = [from_offset(spectra, "chan", delta) for delta in (-1, 1, 2, 3)]
    window = jnp.concatenate([neighbours[0], spectra] + neighbours[1:], axis=1)
    real_part, imag_part = inverse_call(window, shift, responses, band.reshape(-1), tables, own)
    real_part = real_part.reshape(own, length)
    imag_part = imag_part.reshape(own, length)
    for bit_index in range(levels):
        half_span = 1 << bit_index
        upper_half = device_pos // half_span % 2 == 1
        cosine, sine_part = twiddle(device_pos % half_span, 2 * half_span)
        sine_part = -sine_part
        if bit_index == levels - 1:
            own_prod = real_part * cosine - imag_part * sine_part
            partner_real = from_partner(jnp.where(upper_half, own_prod, real_part), "tm", bit_index)
            real_part = jnp.where(upper_half, partner_real - own_prod, real_part + partner_real)
            break
        partner = from_partner(jnp.stack([real_part, imag_part]), "tm", bit_index)
        base_real = jnp.where(upper_half, partner[0], real_part)
        base_imag = jnp.where(upper_half, partner[1], imag_part)
        scaled_real = jnp.where(upper_half, real_part, partner[0])
        scaled_imag = jnp.where(upper_half, imag_part, partner[1])
        prod_real = scaled_real * cosine - scaled_imag * sine_part
        prod_imag = scaled_real * sine_part + scaled_imag * cosine
        real_part = jnp.where(upper_half, base_real - prod_real, base_real + prod_real)
        imag_part = jnp.where(upper_half, base_imag - prod_imag, base_imag + prod_imag)
    smoothed = real_part / total_len
    return smoothed


def solution(mesh):
    in_specs = (P("chan", "tm"), P(), P(None, "tm", None, "chan"), P("tm", "chan"))
    out_specs = P("chan", "tm")
    return jax.shard_map(
        per_device, mesh=mesh, in_specs=in_specs, out_specs=out_specs, check_vma=False
    )
```

```python
import math

import numpy as np

import jax
import jax.numpy as jnp
from jax import lax
from jax.experimental import pallas as pl
from jax.experimental.pallas import tpu as pltpu
from jax.sharding import PartitionSpec as P

PRECISE = lax.Precision.HIGHEST


def from_partner(block, axis, stride):
    count = lax.axis_size(axis)
    route = []
    for low in range(count):
        high = low | 1 << stride
        if high != low and high < count:
            route += [(low, high), (high, low)]
    return lax.ppermute(block, axis, route)


def twiddle(numer, length):
    angle = -2.0 * math.pi / length * numer.astype(jnp.float32)
    return (jnp.cos(angle), jnp.sin(angle))


def dft_table(length):
    steps = lax.iota(jnp.int32, length)
    return twiddle(steps[:, None] * steps[None, :] % length, length)


def reverse_bits(value, bit_count):
    result = value * 0
    for bit_index in range(bit_count):
        result = result + value // (1 << bit_index) % 2 * (1 << bit_count - 1 - bit_index)
    return result


def complex_einsum(form, left_real, left_imag, right_real, right_imag):
    out_real = jnp.einsum(form, left_real, right_real, precision=PRECISE) - jnp.einsum(
        form, left_imag, right_imag, precision=PRECISE
    )
    out_imag = jnp.einsum(form, left_real, right_imag, precision=PRECISE) + jnp.einsum(
        form, left_imag, right_real, precision=PRECISE
    )
    return (out_real, out_imag)


def forward_local(real_part, imag_part, phase_bin, total_len, inner_len):
    channel_count, length = real_part.shape
    outer_len = length // inner_len
    sample_pos = lax.iota(jnp.int32, length)
    cosine, sine_part = twiddle(sample_pos * phase_bin % total_len, total_len)
    real_part, imag_part = (
        real_part * cosine - imag_part * sine_part,
        real_part * sine_part + imag_part * cosine,
    )
    real_part = real_part.reshape(channel_count, inner_len, outer_len)
    imag_part = imag_part.reshape(channel_count, inner_len, outer_len)
    table_real, table_imag = dft_table(inner_len)
    real_part, imag_part = complex_einsum(
        "cab,ak->cbk", real_part, imag_part, table_real, table_imag
    )
    outer_ids = lax.iota(jnp.int32, outer_len)[:, None]
    inner_ids = lax.iota(jnp.int32, inner_len)[None, :]
    cosine, sine_part = twiddle(outer_ids * inner_ids, length)
    real_part, imag_part = (
        real_part * cosine - imag_part * sine_part,
        real_part * sine_part + imag_part * cosine,
    )
    table_real, table_imag = dft_table(outer_len)
    return complex_einsum("cbk,bm->mck", real_part, imag_part, table_real, table_imag)


def inverse_local(spec_real, spec_imag, phase_bin, total_len):
    outer_len, channel_count, inner_len = spec_real.shape
    length = outer_len * inner_len
    table_real, table_imag = dft_table(outer_len)
    real_part, imag_part = complex_einsum(
        "mck,mb->cbk", spec_real, spec_imag, table_real, -table_imag
    )
    outer_ids = lax.iota(jnp.int32, outer_len)[:, None]
    inner_ids = lax.iota(jnp.int32, inner_len)[None, :]
    cosine, sine_part = twiddle(outer_ids * inner_ids, length)
    sine_part = -sine_part
    real_part, imag_part = (
        real_part * cosine - imag_part * sine_part,
        real_part * sine_part + imag_part * cosine,
    )
    table_real, table_imag = dft_table(inner_len)
    real_part, imag_part = complex_einsum(
        "cbk,ka->cab", real_part, imag_part, table_real, -table_imag
    )
    real_part = real_part.reshape(channel_count, length)
    imag_part = imag_part.reshape(channel_count, length)
    sample_pos = lax.iota(jnp.int32, length)
    cosine, sine_part = twiddle(sample_pos * phase_bin % total_len, total_len)
    sine_part = -sine_part
    return (real_part * cosine - imag_part * sine_part, real_part * sine_part + imag_part * cosine)


LANES = 128


def cdot(left_real, left_imag, right_real, right_imag):
    def dot(a, b):
        return jnp.dot(a, b, precision=PRECISE, preferred_element_type=jnp.float32)

    return (
        dot(left_real, right_real) - dot(left_imag, right_imag),
        dot(left_real, right_imag) + dot(left_imag, right_real),
    )


def forward_kernel(xr_ref, xi_ref, twr_ref, twi_ref, kr_ref, ki_ref, t2r_ref, t2i_ref, wr_ref, wi_ref, yr_ref, yi_ref):
    own, outer, inner = xr_ref.shape
    xr = xr_ref[...]
    xi = xi_ref[...]
    position = lax.axis_index("tm")
    twr = twr_ref[position][None]
    twi = twi_ref[position][None]
    ur = (xr * twr - xi * twi).reshape(own * outer, inner)
    ui = (xr * twi + xi * twr).reshape(own * outer, inner)
    zr, zi = cdot(kr_ref[...], ki_ref[...], ur, ui)
    t2r = t2r_ref[...]
    t2i = t2i_ref[...]
    zr, zi = (zr * t2r - zi * t2i, zr * t2i + zi * t2r)
    yr, yi = cdot(zr, zi, wr_ref[...], wi_ref[...])
    yr_ref[...] = yr.reshape(own, outer, inner)
    yi_ref[...] = yi.reshape(own, outer, inner)


def inverse_kernel(win_ref, shift_ref, resp_ref, band_ref, twr_ref, twi_ref, kr_ref, ki_ref, t2r_ref, t2i_ref, wr_ref, wi_ref, xr_ref, xi_ref):
    own, outer, inner = xr_ref.shape
    band_width = resp_ref.shape[1]
    half_width = band_width // 2
    span = own + band_width - 1
    shift = shift_ref[...]
    masks = [shift == amount for amount in range(-half_width, half_width + 1)]
    moved = []
    for row in range(span):
        mr = jnp.zeros((outer, inner), jnp.float32)
        mi = jnp.zeros((outer, inner), jnp.float32)
        for index, amount in enumerate(range(-half_width, half_width + 1)):
            source = own + amount + row
            mr = jnp.where(masks[index], win_ref[0, source], mr)
            mi = jnp.where(masks[index], win_ref[1, source], mi)
        moved.append((mr, mi))
    rows_real = []
    rows_imag = []
    channel_all = band_ref.shape[0] // (2 * band_width)
    first = lax.axis_index("chan") * own
    for channel in range(own):
        acc_r = jnp.zeros((outer, inner), jnp.float32)
        acc_i = jnp.zeros((outer, inner), jnp.float32)
        for lag in range(band_width):
            br = band_ref[lag * channel_all + first + channel]
            bi = band_ref[(band_width + lag) * channel_all + first + channel]
            rr = resp_ref[0, lag]
            ri = resp_ref[1, lag]
            cr = br * rr - bi * ri
            ci = br * ri + bi * rr
            vr, vi = moved[channel + lag]
            acc_r = acc_r + cr * vr - ci * vi
            acc_i = acc_i + cr * vi + ci * vr
        rows_real.append(acc_r)
        rows_imag.append(acc_i)
    mr = jnp.concatenate(rows_real, axis=0)
    mi = jnp.concatenate(rows_imag, axis=0)
    yr, yi = cdot(mr, mi, wr_ref[...], -wi_ref[...])
    t2r = t2r_ref[...]
    t2i = -t2i_ref[...]
    yr, yi = (yr * t2r - yi * t2i, yr * t2i + yi * t2r)
    xr, xi = cdot(kr_ref[...], -ki_ref[...], yr, yi)
    xr = xr.reshape(own, outer, inner)
    xi = xi.reshape(own, outer, inner)
    position = lax.axis_index("tm")
    twr = twr_ref[position][None]
    twi = -twi_ref[position][None]
    xr_ref[...] = xr * twr - xi * twi
    xi_ref[...] = xr * twi + xi * twr


def dft_constant(length, numer):
    angle = -2.0 * np.pi / length * (numer % length)
    return (np.cos(angle).astype(np.float32), np.sin(angle).astype(np.float32))


def local_tables(own, outer, inner, blocks, levels):
    length = outer * inner
    total_len = length * blocks
    rows = np.arange(outer)[:, None]
    cols = np.arange(inner)[None, :]
    residues = [reverse_bits(position, levels) for position in range(blocks)]
    phase = np.stack([(rows * inner + cols) * residue for residue in residues])
    twr, twi = dft_constant(total_len, phase)
    small_r, small_i = dft_constant(outer, rows * np.arange(outer)[None, :])
    eye = np.eye(own, dtype=np.float32)
    kr = np.kron(eye, small_r)
    ki = np.kron(eye, small_i)
    t2r, t2i = dft_constant(length, rows * cols)
    t2r = np.tile(t2r, (own, 1))
    t2i = np.tile(t2i, (own, 1))
    wr, wi = dft_constant(inner, np.arange(inner)[:, None] * cols)
    return tuple(jnp.asarray(table) for table in (twr, twi, kr, ki, t2r, t2i, wr, wi))


def vmem_specs(count):
    return [pl.BlockSpec(memory_space=pltpu.VMEM)] * count


def forward_call(xr, xi, tables):
    shape = jax.ShapeDtypeStruct(xr.shape, jnp.float32)
    return pl.pallas_call(
        forward_kernel,
        out_shape=(shape, shape),
        in_specs=vmem_specs(2 + len(tables)),
        out_specs=tuple(vmem_specs(2)),
    )(xr, xi, *tables)


def inverse_call(window, shift, responses, band_flat, tables, own):
    shape = jax.ShapeDtypeStruct((own,) + window.shape[2:], jnp.float32)
    specs = vmem_specs(3) + [pl.BlockSpec(memory_space=pltpu.SMEM)] + vmem_specs(len(tables))
    return pl.pallas_call(
        inverse_kernel,
        out_shape=(shape, shape),
        in_specs=specs,
        out_specs=tuple(vmem_specs(2)),
    )(window, shift, responses, band_flat, *tables)


def from_offset(block, axis, delta):
    count = lax.axis_size(axis)
    return lax.ppermute(block, axis, [((i + delta) % count, i) for i in range(count)])


def digit_radices(count):
    radices = []
    for radix in (2, 4, 4):
        if count % radix == 0 and count > 1:
            radices.append(radix)
            count //= radix
    while count > 1:
        radices.append(2)
        count //= 2
    return radices


def gather_radix(block, axis):
    count = lax.axis_size(axis)
    me = lax.axis_index(axis)
    stride = 1
    for radix in digit_radices(count):
        digit = me // stride % radix
        pieces = [block]
        for delta in range(1, radix):
            route = []
            for index in range(count):
                own_digit = index // stride % radix
                source = index + ((own_digit + delta) % radix - own_digit) * stride
                route.append((source, index))
            pieces.append(lax.ppermute(block, axis, route))
        stacked = jnp.roll(jnp.stack(pieces), digit, axis=0)
        block = stacked.reshape((radix * block.shape[0],) + block.shape[1:])
        stride *= radix
    return block


def gather_doubling(block, axis):
    count = lax.axis_size(axis)
    me = lax.axis_index(axis)
    stride = 1
    while stride < count:
        partner = from_partner(block, axis, stride.bit_length() - 1)
        upper = me // stride % 2 == 1
        block = jnp.where(upper, jnp.concatenate([partner, block]), jnp.concatenate([block, partner]))
        stride *= 2
    return block


def per_device(signal, band, response, offsets):
    blocks = lax.axis_size("tm")
    levels = blocks.bit_length() - 1
    device_pos = lax.axis_index("tm")
    phase_bin = reverse_bits(device_pos, levels)
    channel_count, length = signal.shape
    total_len = length * blocks
    inner_len = math.gcd(128, length // lax.axis_size("chan"))
    real_part = signal
    imag_part = jnp.zeros_like(signal)
    for bit_index in range(levels - 1, -1, -1):
        half_span = 1 << bit_index
        upper_half = device_pos // half_span % 2 == 1
        cosine, sine_part = twiddle(device_pos % half_span, 2 * half_span)
        if bit_index == levels - 1:
            partner_real = from_partner(real_part, "tm", bit_index)
            diff_real = partner_real - real_part
            imag_part = jnp.where(upper_half, diff_real * sine_part, 0.0)
            real_part = jnp.where(upper_half, diff_real * cosine, real_part + partner_real)
            continue
        partner = from_partner(jnp.stack([real_part, imag_part]), "tm", bit_index)
        diff_real = partner[0] - real_part
        diff_imag = partner[1] - imag_part
        new_real = jnp.where(
            upper_half, diff_real * cosine - diff_imag * sine_part, real_part + partner[0]
        )
        new_imag = jnp.where(
            upper_half, diff_real * sine_part + diff_imag * cosine, imag_part + partner[1]
        )
        real_part, imag_part = (new_real, new_imag)
    inner = LANES
    outer = length // inner
    own = channel_count
    band_width = band.shape[1]
    half_width = band_width // 2
    channel_all = band.shape[2]
    tables = local_tables(own, outer, inner, blocks, levels)
    spec_real, spec_imag = forward_call(
        real_part.reshape(own, outer, inner), imag_part.reshape(own, outer, inner), tables
    )
    packed = jnp.concatenate(
        [response.reshape(2 * band_width, -1), offsets.reshape(1, -1).astype(jnp.float32)], axis=0
    )
    peers = lax.axis_size("chan")
    entries, local_bins = packed.shape
    runs = local_bins // outer
    packed = packed.reshape(entries, runs, outer).transpose(0, 2, 1)
    spread = jnp.broadcast_to(packed[:, :, None], (entries, outer, peers, runs))
    table = lax.all_to_all(spread, "chan", 2, 2, tiled=True).reshape(entries, outer, inner)
    responses = table[: 2 * band_width].reshape(2, band_width, outer, inner)
    shift = (table[2 * band_width].astype(jnp.int32) + half_width) % channel_all - half_width
    spectra = jnp.stack([spec_real, spec_imag])
    neighbours = [from_offset(spectra, "chan", delta) for delta in (-1, 1, 2, 3)]
    window = jnp.concatenate([neighbours[0], spectra] + neighbours[1:], axis=1)
    real_part, imag_part = inverse_call(window, shift, responses, band.reshape(-1), tables, own)
    real_part = real_part.reshape(own, length)
    imag_part = imag_part.reshape(own, length)
    for bit_index in range(levels):
        half_span = 1 << bit_index
        upper_half = device_pos // half_span % 2 == 1
        cosine, sine_part = twiddle(device_pos % half_span, 2 * half_span)
        sine_part = -sine_part
        if bit_index == levels - 1:
            own_prod = real_part * cosine - imag_part * sine_part
            partner_real = from_partner(jnp.where(upper_half, own_prod, real_part), "tm", bit_index)
            real_part = jnp.where(upper_half, partner_real - own_prod, real_part + partner_real)
            break
        partner = from_partner(jnp.stack([real_part, imag_part]), "tm", bit_index)
        base_real = jnp.where(upper_half, partner[0], real_part)
        base_imag = jnp.where(upper_half, partner[1], imag_part)
        scaled_real = jnp.where(upper_half, real_part, partner[0])
        scaled_imag = jnp.where(upper_half, imag_part, partner[1])
        prod_real = scaled_real * cosine - scaled_imag * sine_part
        prod_imag = scaled_real * sine_part + scaled_imag * cosine
        real_part = jnp.where(upper_half, base_real - prod_real, base_real + prod_real)
        imag_part = jnp.where(upper_half, base_imag - prod_imag, base_imag + prod_imag)
    smoothed = real_part / total_len
    return smoothed


def solution(mesh):
    in_specs = (P("chan", "tm"), P(), P(None, "tm", None, "chan"), P("tm", "chan"))
    out_specs = P("chan", "tm")
    return jax.shard_map(
        per_device, mesh=mesh, in_specs=in_specs, out_specs=out_specs, check_vma=False
    )
```

```python
import math

import numpy as np

import jax
import jax.numpy as jnp
from jax import lax
from jax.experimental import pallas as pl
from jax.experimental.pallas import tpu as pltpu
from jax.sharding import PartitionSpec as P

PRECISE = lax.Precision.HIGHEST


def from_partner(block, axis, stride):
    count = lax.axis_size(axis)
    route = []
    for low in range(count):
        high = low | 1 << stride
        if high != low and high < count:
            route += [(low, high), (high, low)]
    return lax.ppermute(block, axis, route)


def twiddle(numer, length):
    angle = -2.0 * math.pi / length * numer.astype(jnp.float32)
    return (jnp.cos(angle), jnp.sin(angle))


def dft_table(length):
    steps = lax.iota(jnp.int32, length)
    return twiddle(steps[:, None] * steps[None, :] % length, length)


def reverse_bits(value, bit_count):
    result = value * 0
    for bit_index in range(bit_count):
        result = result + value // (1 << bit_index) % 2 * (1 << bit_count - 1 - bit_index)
    return result


def complex_einsum(form, left_real, left_imag, right_real, right_imag):
    out_real = jnp.einsum(form, left_real, right_real, precision=PRECISE) - jnp.einsum(
        form, left_imag, right_imag, precision=PRECISE
    )
    out_imag = jnp.einsum(form, left_real, right_imag, precision=PRECISE) + jnp.einsum(
        form, left_imag, right_real, precision=PRECISE
    )
    return (out_real, out_imag)


def forward_local(real_part, imag_part, phase_bin, total_len, inner_len):
    channel_count, length = real_part.shape
    outer_len = length // inner_len
    sample_pos = lax.iota(jnp.int32, length)
    cosine, sine_part = twiddle(sample_pos * phase_bin % total_len, total_len)
    real_part, imag_part = (
        real_part * cosine - imag_part * sine_part,
        real_part * sine_part + imag_part * cosine,
    )
    real_part = real_part.reshape(channel_count, inner_len, outer_len)
    imag_part = imag_part.reshape(channel_count, inner_len, outer_len)
    table_real, table_imag = dft_table(inner_len)
    real_part, imag_part = complex_einsum(
        "cab,ak->cbk", real_part, imag_part, table_real, table_imag
    )
    outer_ids = lax.iota(jnp.int32, outer_len)[:, None]
    inner_ids = lax.iota(jnp.int32, inner_len)[None, :]
    cosine, sine_part = twiddle(outer_ids * inner_ids, length)
    real_part, imag_part = (
        real_part * cosine - imag_part * sine_part,
        real_part * sine_part + imag_part * cosine,
    )
    table_real, table_imag = dft_table(outer_len)
    return complex_einsum("cbk,bm->mck", real_part, imag_part, table_real, table_imag)


def inverse_local(spec_real, spec_imag, phase_bin, total_len):
    outer_len, channel_count, inner_len = spec_real.shape
    length = outer_len * inner_len
    table_real, table_imag = dft_table(outer_len)
    real_part, imag_part = complex_einsum(
        "mck,mb->cbk", spec_real, spec_imag, table_real, -table_imag
    )
    outer_ids = lax.iota(jnp.int32, outer_len)[:, None]
    inner_ids = lax.iota(jnp.int32, inner_len)[None, :]
    cosine, sine_part = twiddle(outer_ids * inner_ids, length)
    sine_part = -sine_part
    real_part, imag_part = (
        real_part * cosine - imag_part * sine_part,
        real_part * sine_part + imag_part * cosine,
    )
    table_real, table_imag = dft_table(inner_len)
    real_part, imag_part = complex_einsum(
        "cbk,ka->cab", real_part, imag_part, table_real, -table_imag
    )
    real_part = real_part.reshape(channel_count, length)
    imag_part = imag_part.reshape(channel_count, length)
    sample_pos = lax.iota(jnp.int32, length)
    cosine, sine_part = twiddle(sample_pos * phase_bin % total_len, total_len)
    sine_part = -sine_part
    return (real_part * cosine - imag_part * sine_part, real_part * sine_part + imag_part * cosine)


LANES = 128


def cdot(left_real, left_imag, right_real, right_imag):
    def dot(a, b):
        return jnp.dot(a, b, precision=PRECISE, preferred_element_type=jnp.float32)

    return (
        dot(left_real, right_real) - dot(left_imag, right_imag),
        dot(left_real, right_imag) + dot(left_imag, right_real),
    )


def forward_kernel(xr_ref, xi_ref, twr_ref, twi_ref, kr_ref, ki_ref, t2r_ref, t2i_ref, wr_ref, wi_ref, yr_ref, yi_ref):
    own, outer, inner = xr_ref.shape
    xr = xr_ref[...]
    xi = xi_ref[...]
    position = lax.axis_index("tm")
    twr = twr_ref[position][None]
    twi = twi_ref[position][None]
    ur = (xr * twr - xi * twi).reshape(own * outer, inner)
    ui = (xr * twi + xi * twr).reshape(own * outer, inner)
    zr, zi = cdot(kr_ref[...], ki_ref[...], ur, ui)
    t2r = t2r_ref[...]
    t2i = t2i_ref[...]
    zr, zi = (zr * t2r - zi * t2i, zr * t2i + zi * t2r)
    yr, yi = cdot(zr, zi, wr_ref[...], wi_ref[...])
    yr_ref[...] = yr.reshape(own, outer, inner)
    yi_ref[...] = yi.reshape(own, outer, inner)


def inverse_kernel(win_ref, shift_ref, resp_ref, band_ref, twr_ref, twi_ref, kr_ref, ki_ref, t2r_ref, t2i_ref, wr_ref, wi_ref, xr_ref, xi_ref):
    own, outer, inner = xr_ref.shape
    band_width = resp_ref.shape[1]
    half_width = band_width // 2
    span = own + band_width - 1
    shift = shift_ref[...]
    masks = [shift == amount for amount in range(-half_width, half_width + 1)]
    moved = []
    for row in range(span):
        mr = jnp.zeros((outer, inner), jnp.float32)
        mi = jnp.zeros((outer, inner), jnp.float32)
        for index, amount in enumerate(range(-half_width, half_width + 1)):
            source = own + amount + row
            mr = jnp.where(masks[index], win_ref[0, source], mr)
            mi = jnp.where(masks[index], win_ref[1, source], mi)
        moved.append((mr, mi))
    rows_real = []
    rows_imag = []
    channel_all = band_ref.shape[0] // (2 * band_width)
    first = lax.axis_index("chan") * own
    for channel in range(own):
        acc_r = jnp.zeros((outer, inner), jnp.float32)
        acc_i = jnp.zeros((outer, inner), jnp.float32)
        for lag in range(band_width):
            br = band_ref[lag * channel_all + first + channel]
            bi = band_ref[(band_width + lag) * channel_all + first + channel]
            rr = resp_ref[0, lag]
            ri = resp_ref[1, lag]
            cr = br * rr - bi * ri
            ci = br * ri + bi * rr
            vr, vi = moved[channel + lag]
            acc_r = acc_r + cr * vr - ci * vi
            acc_i = acc_i + cr * vi + ci * vr
        rows_real.append(acc_r)
        rows_imag.append(acc_i)
    mr = jnp.concatenate(rows_real, axis=0)
    mi = jnp.concatenate(rows_imag, axis=0)
    yr, yi = cdot(mr, mi, wr_ref[...], -wi_ref[...])
    t2r = t2r_ref[...]
    t2i = -t2i_ref[...]
    yr, yi = (yr * t2r - yi * t2i, yr * t2i + yi * t2r)
    xr, xi = cdot(kr_ref[...], -ki_ref[...], yr, yi)
    xr = xr.reshape(own, outer, inner)
    xi = xi.reshape(own, outer, inner)
    position = lax.axis_index("tm")
    twr = twr_ref[position][None]
    twi = -twi_ref[position][None]
    xr_ref[...] = xr * twr - xi * twi
    xi_ref[...] = xr * twi + xi * twr


def dft_constant(length, numer):
    angle = -2.0 * np.pi / length * (numer % length)
    return (np.cos(angle).astype(np.float32), np.sin(angle).astype(np.float32))


def local_tables(own, outer, inner, blocks, levels):
    length = outer * inner
    total_len = length * blocks
    rows = np.arange(outer)[:, None]
    cols = np.arange(inner)[None, :]
    residues = [reverse_bits(position, levels) for position in range(blocks)]
    phase = np.stack([(rows * inner + cols) * residue for residue in residues])
    twr, twi = dft_constant(total_len, phase)
    small_r, small_i = dft_constant(outer, rows * np.arange(outer)[None, :])
    eye = np.eye(own, dtype=np.float32)
    kr = np.kron(eye, small_r)
    ki = np.kron(eye, small_i)
    t2r, t2i = dft_constant(length, rows * cols)
    t2r = np.tile(t2r, (own, 1))
    t2i = np.tile(t2i, (own, 1))
    wr, wi = dft_constant(inner, np.arange(inner)[:, None] * cols)
    return tuple(jnp.asarray(table) for table in (twr, twi, kr, ki, t2r, t2i, wr, wi))


def vmem_specs(count):
    return [pl.BlockSpec(memory_space=pltpu.VMEM)] * count


def forward_call(xr, xi, tables):
    shape = jax.ShapeDtypeStruct(xr.shape, jnp.float32)
    return pl.pallas_call(
        forward_kernel,
        out_shape=(shape, shape),
        in_specs=vmem_specs(2 + len(tables)),
        out_specs=tuple(vmem_specs(2)),
    )(xr, xi, *tables)


def inverse_call(window, shift, responses, band_flat, tables, own):
    shape = jax.ShapeDtypeStruct((own,) + window.shape[2:], jnp.float32)
    specs = vmem_specs(3) + [pl.BlockSpec(memory_space=pltpu.SMEM)] + vmem_specs(len(tables))
    return pl.pallas_call(
        inverse_kernel,
        out_shape=(shape, shape),
        in_specs=specs,
        out_specs=tuple(vmem_specs(2)),
    )(window, shift, responses, band_flat, *tables)


def from_offset(block, axis, delta):
    count = lax.axis_size(axis)
    return lax.ppermute(block, axis, [((i + delta) % count, i) for i in range(count)])


def digit_radices(count):
    radices = []
    for radix in (2, 4, 4):
        if count % radix == 0 and count > 1:
            radices.append(radix)
            count //= radix
    while count > 1:
        radices.append(2)
        count //= 2
    return radices


def gather_radix(block, axis):
    count = lax.axis_size(axis)
    me = lax.axis_index(axis)
    stride = 1
    for radix in digit_radices(count):
        digit = me // stride % radix
        pieces = [block]
        for delta in range(1, radix):
            route = []
            for index in range(count):
                own_digit = index // stride % radix
                source = index + ((own_digit + delta) % radix - own_digit) * stride
                route.append((source, index))
            pieces.append(lax.ppermute(block, axis, route))
        stacked = jnp.roll(jnp.stack(pieces), digit, axis=0)
        block = stacked.reshape((radix * block.shape[0],) + block.shape[1:])
        stride *= radix
    return block


def gather_doubling(block, axis):
    count = lax.axis_size(axis)
    me = lax.axis_index(axis)
    stride = 1
    while stride < count:
        partner = from_partner(block, axis, stride.bit_length() - 1)
        upper = me // stride % 2 == 1
        block = jnp.where(upper, jnp.concatenate([partner, block]), jnp.concatenate([block, partner]))
        stride *= 2
    return block


def per_device(signal, band, response, offsets):
    blocks = lax.axis_size("tm")
    levels = blocks.bit_length() - 1
    device_pos = lax.axis_index("tm")
    phase_bin = reverse_bits(device_pos, levels)
    channel_count, length = signal.shape
    total_len = length * blocks
    inner_len = math.gcd(128, length // lax.axis_size("chan"))
    real_part = signal
    imag_part = jnp.zeros_like(signal)
    for bit_index in range(levels - 1, -1, -1):
        half_span = 1 << bit_index
        upper_half = device_pos // half_span % 2 == 1
        cosine, sine_part = twiddle(device_pos % half_span, 2 * half_span)
        if bit_index == levels - 1:
            partner_real = from_partner(real_part, "tm", bit_index)
            diff_real = partner_real - real_part
            imag_part = jnp.where(upper_half, diff_real * sine_part, 0.0)
            real_part = jnp.where(upper_half, diff_real * cosine, real_part + partner_real)
            continue
        partner = from_partner(jnp.stack([real_part, imag_part]), "tm", bit_index)
        diff_real = partner[0] - real_part
        diff_imag = partner[1] - imag_part
        new_real = jnp.where(
            upper_half, diff_real * cosine - diff_imag * sine_part, real_part + partner[0]
        )
        new_imag = jnp.where(
            upper_half, diff_real * sine_part + diff_imag * cosine, imag_part + partner[1]
        )
        real_part, imag_part = (new_real, new_imag)
    inner = LANES
    outer = length // inner
    own = channel_count
    band_width = band.shape[1]
    half_width = band_width // 2
    channel_all = band.shape[2]
    tables = local_tables(own, outer, inner, blocks, levels)
    spec_real, spec_imag = forward_call(
        real_part.reshape(own, outer, inner), imag_part.reshape(own, outer, inner), tables
    )
    packed = jnp.concatenate(
        [response.reshape(2 * band_width, -1), offsets.reshape(1, -1).astype(jnp.float32)], axis=0
    )
    peers = lax.axis_size("chan")
    table = lax.all_to_all(jnp.broadcast_to(packed[None], (peers,) + packed.shape), "chan", 0, 0, tiled=True)
    entries = table.shape[1]
    table, _ = lax.optimization_barrier((table, spec_real))
    table = table.transpose(1, 0, 2).reshape(entries, inner, outer).transpose(0, 2, 1)
    responses = table[: 2 * band_width].reshape(2, band_width, outer, inner)
    shift = (table[2 * band_width].astype(jnp.int32) + half_width) % channel_all - half_width
    spectra = jnp.stack([spec_real, spec_imag])
    neighbours = [from_offset(spectra, "chan", delta) for delta in (-1, 1, 2, 3)]
    window = jnp.concatenate([neighbours[0], spectra] + neighbours[1:], axis=1)
    real_part, imag_part = inverse_call(window, shift, responses, band.reshape(-1), tables, own)
    real_part = real_part.reshape(own, length)
    imag_part = imag_part.reshape(own, length)
    for bit_index in range(levels):
        half_span = 1 << bit_index
        upper_half = device_pos // half_span % 2 == 1
        cosine, sine_part = twiddle(device_pos % half_span, 2 * half_span)
        sine_part = -sine_part
        if bit_index == levels - 1:
            own_prod = real_part * cosine - imag_part * sine_part
            partner_real = from_partner(jnp.where(upper_half, own_prod, real_part), "tm", bit_index)
            real_part = jnp.where(upper_half, partner_real - own_prod, real_part + partner_real)
            break
        partner = from_partner(jnp.stack([real_part, imag_part]), "tm", bit_index)
        base_real = jnp.where(upper_half, partner[0], real_part)
        base_imag = jnp.where(upper_half, partner[1], imag_part)
        scaled_real = jnp.where(upper_half, real_part, partner[0])
        scaled_imag = jnp.where(upper_half, imag_part, partner[1])
        prod_real = scaled_real * cosine - scaled_imag * sine_part
        prod_imag = scaled_real * sine_part + scaled_imag * cosine
        real_part = jnp.where(upper_half, base_real - prod_real, base_real + prod_real)
        imag_part = jnp.where(upper_half, base_imag - prod_imag, base_imag + prod_imag)
    smoothed = real_part / total_len
    return smoothed


def solution(mesh):
    in_specs = (P("chan", "tm"), P(), P(None, "tm", None, "chan"), P("tm", "chan"))
    out_specs = P("chan", "tm")
    return jax.shard_map(
        per_device, mesh=mesh, in_specs=in_specs, out_specs=out_specs, check_vma=False
    )
```

```python
import math

import numpy as np

import jax
import jax.numpy as jnp
from jax import lax
from jax.experimental import pallas as pl
from jax.experimental.pallas import tpu as pltpu
from jax.sharding import PartitionSpec as P

PRECISE = lax.Precision.HIGHEST


def from_partner(block, axis, stride):
    count = lax.axis_size(axis)
    route = []
    for low in range(count):
        high = low | 1 << stride
        if high != low and high < count:
            route += [(low, high), (high, low)]
    return lax.ppermute(block, axis, route)


def twiddle(numer, length):
    angle = -2.0 * math.pi / length * numer.astype(jnp.float32)
    return (jnp.cos(angle), jnp.sin(angle))


def dft_table(length):
    steps = lax.iota(jnp.int32, length)
    return twiddle(steps[:, None] * steps[None, :] % length, length)


def reverse_bits(value, bit_count):
    result = value * 0
    for bit_index in range(bit_count):
        result = result + value // (1 << bit_index) % 2 * (1 << bit_count - 1 - bit_index)
    return result


def complex_einsum(form, left_real, left_imag, right_real, right_imag):
    out_real = jnp.einsum(form, left_real, right_real, precision=PRECISE) - jnp.einsum(
        form, left_imag, right_imag, precision=PRECISE
    )
    out_imag = jnp.einsum(form, left_real, right_imag, precision=PRECISE) + jnp.einsum(
        form, left_imag, right_real, precision=PRECISE
    )
    return (out_real, out_imag)


def forward_local(real_part, imag_part, phase_bin, total_len, inner_len):
    channel_count, length = real_part.shape
    outer_len = length // inner_len
    sample_pos = lax.iota(jnp.int32, length)
    cosine, sine_part = twiddle(sample_pos * phase_bin % total_len, total_len)
    real_part, imag_part = (
        real_part * cosine - imag_part * sine_part,
        real_part * sine_part + imag_part * cosine,
    )
    real_part = real_part.reshape(channel_count, inner_len, outer_len)
    imag_part = imag_part.reshape(channel_count, inner_len, outer_len)
    table_real, table_imag = dft_table(inner_len)
    real_part, imag_part = complex_einsum(
        "cab,ak->cbk", real_part, imag_part, table_real, table_imag
    )
    outer_ids = lax.iota(jnp.int32, outer_len)[:, None]
    inner_ids = lax.iota(jnp.int32, inner_len)[None, :]
    cosine, sine_part = twiddle(outer_ids * inner_ids, length)
    real_part, imag_part = (
        real_part * cosine - imag_part * sine_part,
        real_part * sine_part + imag_part * cosine,
    )
    table_real, table_imag = dft_table(outer_len)
    return complex_einsum("cbk,bm->mck", real_part, imag_part, table_real, table_imag)


def inverse_local(spec_real, spec_imag, phase_bin, total_len):
    outer_len, channel_count, inner_len = spec_real.shape
    length = outer_len * inner_len
    table_real, table_imag = dft_table(outer_len)
    real_part, imag_part = complex_einsum(
        "mck,mb->cbk", spec_real, spec_imag, table_real, -table_imag
    )
    outer_ids = lax.iota(jnp.int32, outer_len)[:, None]
    inner_ids = lax.iota(jnp.int32, inner_len)[None, :]
    cosine, sine_part = twiddle(outer_ids * inner_ids, length)
    sine_part = -sine_part
    real_part, imag_part = (
        real_part * cosine - imag_part * sine_part,
        real_part * sine_part + imag_part * cosine,
    )
    table_real, table_imag = dft_table(inner_len)
    real_part, imag_part = complex_einsum(
        "cbk,ka->cab", real_part, imag_part, table_real, -table_imag
    )
    real_part = real_part.reshape(channel_count, length)
    imag_part = imag_part.reshape(channel_count, length)
    sample_pos = lax.iota(jnp.int32, length)
    cosine, sine_part = twiddle(sample_pos * phase_bin % total_len, total_len)
    sine_part = -sine_part
    return (real_part * cosine - imag_part * sine_part, real_part * sine_part + imag_part * cosine)


LANES = 128


def cdot(left_real, left_imag, right_real, right_imag):
    def dot(a, b):
        return jnp.dot(a, b, precision=PRECISE, preferred_element_type=jnp.float32)

    return (
        dot(left_real, right_real) - dot(left_imag, right_imag),
        dot(left_real, right_imag) + dot(left_imag, right_real),
    )


def forward_kernel(xr_ref, xi_ref, twr_ref, twi_ref, kr_ref, ki_ref, t2r_ref, t2i_ref, wr_ref, wi_ref, yr_ref, yi_ref):
    own, outer, inner = xr_ref.shape
    xr = xr_ref[...]
    xi = xi_ref[...]
    position = lax.axis_index("tm")
    twr = twr_ref[position][None]
    twi = twi_ref[position][None]
    ur = (xr * twr - xi * twi).reshape(own * outer, inner)
    ui = (xr * twi + xi * twr).reshape(own * outer, inner)
    zr, zi = cdot(kr_ref[...], ki_ref[...], ur, ui)
    t2r = t2r_ref[...]
    t2i = t2i_ref[...]
    zr, zi = (zr * t2r - zi * t2i, zr * t2i + zi * t2r)
    yr, yi = cdot(zr, zi, wr_ref[...], wi_ref[...])
    yr_ref[...] = yr.reshape(own, outer, inner)
    yi_ref[...] = yi.reshape(own, outer, inner)


def inverse_kernel(win_ref, shift_ref, resp_ref, band_ref, twr_ref, twi_ref, kr_ref, ki_ref, t2r_ref, t2i_ref, wr_ref, wi_ref, xr_ref, xi_ref):
    own, outer, inner = xr_ref.shape
    band_width = resp_ref.shape[1]
    half_width = band_width // 2
    span = own + band_width - 1
    shift = shift_ref[...]
    masks = [shift == amount for amount in range(-half_width, half_width + 1)]
    moved = []
    for row in range(span):
        mr = jnp.zeros((outer, inner), jnp.float32)
        mi = jnp.zeros((outer, inner), jnp.float32)
        for index, amount in enumerate(range(-half_width, half_width + 1)):
            source = own + amount + row
            mr = jnp.where(masks[index], win_ref[0, source], mr)
            mi = jnp.where(masks[index], win_ref[1, source], mi)
        moved.append((mr, mi))
    rows_real = []
    rows_imag = []
    channel_all = band_ref.shape[0] // (2 * band_width)
    first = lax.axis_index("chan") * own
    for channel in range(own):
        acc_r = jnp.zeros((outer, inner), jnp.float32)
        acc_i = jnp.zeros((outer, inner), jnp.float32)
        for lag in range(band_width):
            br = band_ref[lag * channel_all + first + channel]
            bi = band_ref[(band_width + lag) * channel_all + first + channel]
            rr = resp_ref[0, lag]
            ri = resp_ref[1, lag]
            cr = br * rr - bi * ri
            ci = br * ri + bi * rr
            vr, vi = moved[channel + lag]
            acc_r = acc_r + cr * vr - ci * vi
            acc_i = acc_i + cr * vi + ci * vr
        rows_real.append(acc_r)
        rows_imag.append(acc_i)
    mr = jnp.concatenate(rows_real, axis=0)
    mi = jnp.concatenate(rows_imag, axis=0)
    yr, yi = cdot(mr, mi, wr_ref[...], -wi_ref[...])
    t2r = t2r_ref[...]
    t2i = -t2i_ref[...]
    yr, yi = (yr * t2r - yi * t2i, yr * t2i + yi * t2r)
    xr, xi = cdot(kr_ref[...], -ki_ref[...], yr, yi)
    xr = xr.reshape(own, outer, inner)
    xi = xi.reshape(own, outer, inner)
    position = lax.axis_index("tm")
    twr = twr_ref[position][None]
    twi = -twi_ref[position][None]
    xr_ref[...] = xr * twr - xi * twi
    xi_ref[...] = xr * twi + xi * twr


def dft_constant(length, numer):
    angle = -2.0 * np.pi / length * (numer % length)
    return (np.cos(angle).astype(np.float32), np.sin(angle).astype(np.float32))


def local_tables(own, outer, inner, blocks, levels):
    length = outer * inner
    total_len = length * blocks
    rows = np.arange(outer)[:, None]
    cols = np.arange(inner)[None, :]
    residues = [reverse_bits(position, levels) for position in range(blocks)]
    phase = np.stack([(rows * inner + cols) * residue for residue in residues])
    twr, twi = dft_constant(total_len, phase)
    small_r, small_i = dft_constant(outer, rows * np.arange(outer)[None, :])
    eye = np.eye(own, dtype=np.float32)
    kr = np.kron(eye, small_r)
    ki = np.kron(eye, small_i)
    t2r, t2i = dft_constant(length, rows * cols)
    t2r = np.tile(t2r, (own, 1))
    t2i = np.tile(t2i, (own, 1))
    wr, wi = dft_constant(inner, np.arange(inner)[:, None] * cols)
    return tuple(jnp.asarray(table) for table in (twr, twi, kr, ki, t2r, t2i, wr, wi))


def vmem_specs(count):
    return [pl.BlockSpec(memory_space=pltpu.VMEM)] * count


def forward_call(xr, xi, tables):
    shape = jax.ShapeDtypeStruct(xr.shape, jnp.float32)
    return pl.pallas_call(
        forward_kernel,
        out_shape=(shape, shape),
        in_specs=vmem_specs(2 + len(tables)),
        out_specs=tuple(vmem_specs(2)),
    )(xr, xi, *tables)


def inverse_call(window, shift, responses, band_flat, tables, own):
    shape = jax.ShapeDtypeStruct((own,) + window.shape[2:], jnp.float32)
    specs = vmem_specs(3) + [pl.BlockSpec(memory_space=pltpu.SMEM)] + vmem_specs(len(tables))
    return pl.pallas_call(
        inverse_kernel,
        out_shape=(shape, shape),
        in_specs=specs,
        out_specs=tuple(vmem_specs(2)),
    )(window, shift, responses, band_flat, *tables)


def from_offset(block, axis, delta):
    count = lax.axis_size(axis)
    return lax.ppermute(block, axis, [((i + delta) % count, i) for i in range(count)])


def digit_radices(count):
    radices = []
    for radix in (2, 4, 4):
        if count % radix == 0 and count > 1:
            radices.append(radix)
            count //= radix
    while count > 1:
        radices.append(2)
        count //= 2
    return radices


def gather_radix(block, axis):
    count = lax.axis_size(axis)
    me = lax.axis_index(axis)
    stride = 1
    for radix in digit_radices(count):
        digit = me // stride % radix
        pieces = [block]
        for delta in range(1, radix):
            route = []
            for index in range(count):
                own_digit = index // stride % radix
                source = index + ((own_digit + delta) % radix - own_digit) * stride
                route.append((source, index))
            pieces.append(lax.ppermute(block, axis, route))
        stacked = jnp.roll(jnp.stack(pieces), digit, axis=0)
        block = stacked.reshape((radix * block.shape[0],) + block.shape[1:])
        stride *= radix
    return block


def gather_doubling(block, axis):
    count = lax.axis_size(axis)
    me = lax.axis_index(axis)
    stride = 1
    while stride < count:
        partner = from_partner(block, axis, stride.bit_length() - 1)
        upper = me // stride % 2 == 1
        block = jnp.where(upper, jnp.concatenate([partner, block]), jnp.concatenate([block, partner]))
        stride *= 2
    return block


def per_device(signal, band, response, offsets):
    blocks = lax.axis_size("tm")
    levels = blocks.bit_length() - 1
    device_pos = lax.axis_index("tm")
    phase_bin = reverse_bits(device_pos, levels)
    channel_count, length = signal.shape
    total_len = length * blocks
    inner_len = math.gcd(128, length // lax.axis_size("chan"))
    real_part = signal.reshape(channel_count, length // LANES, LANES)
    imag_part = jnp.zeros_like(real_part)
    for bit_index in range(levels - 1, -1, -1):
        half_span = 1 << bit_index
        upper_half = device_pos // half_span % 2 == 1
        cosine, sine_part = twiddle(device_pos % half_span, 2 * half_span)
        if bit_index == levels - 1:
            partner_real = from_partner(real_part, "tm", bit_index)
            diff_real = partner_real - real_part
            imag_part = jnp.where(upper_half, diff_real * sine_part, 0.0)
            real_part = jnp.where(upper_half, diff_real * cosine, real_part + partner_real)
            continue
        partner = from_partner(jnp.stack([real_part, imag_part]), "tm", bit_index)
        diff_real = partner[0] - real_part
        diff_imag = partner[1] - imag_part
        new_real = jnp.where(
            upper_half, diff_real * cosine - diff_imag * sine_part, real_part + partner[0]
        )
        new_imag = jnp.where(
            upper_half, diff_real * sine_part + diff_imag * cosine, imag_part + partner[1]
        )
        real_part, imag_part = (new_real, new_imag)
    inner = LANES
    outer = length // inner
    own = channel_count
    band_width = band.shape[1]
    half_width = band_width // 2
    channel_all = band.shape[2]
    tables = local_tables(own, outer, inner, blocks, levels)
    spec_real, spec_imag = forward_call(
        real_part, imag_part, tables
    )
    packed = jnp.concatenate(
        [response.reshape(2 * band_width, -1), offsets.reshape(1, -1).astype(jnp.float32)], axis=0
    )
    peers = lax.axis_size("chan")
    table = lax.all_to_all(jnp.broadcast_to(packed[None], (peers,) + packed.shape), "chan", 0, 0, tiled=True)
    entries = table.shape[1]
    table, _ = lax.optimization_barrier((table, spec_real))
    table = table.transpose(1, 0, 2).reshape(entries, inner, outer).transpose(0, 2, 1)
    responses = table[: 2 * band_width].reshape(2, band_width, outer, inner)
    shift = (table[2 * band_width].astype(jnp.int32) + half_width) % channel_all - half_width
    spectra = jnp.stack([spec_real, spec_imag])
    neighbours = [from_offset(spectra, "chan", delta) for delta in (-1, 1, 2, 3)]
    window = jnp.concatenate([neighbours[0], spectra] + neighbours[1:], axis=1)
    real_part, imag_part = inverse_call(window, shift, responses, band.reshape(-1), tables, own)
    for bit_index in range(levels):
        half_span = 1 << bit_index
        upper_half = device_pos // half_span % 2 == 1
        cosine, sine_part = twiddle(device_pos % half_span, 2 * half_span)
        sine_part = -sine_part
        if bit_index == levels - 1:
            own_prod = real_part * cosine - imag_part * sine_part
            partner_real = from_partner(jnp.where(upper_half, own_prod, real_part), "tm", bit_index)
            real_part = jnp.where(upper_half, partner_real - own_prod, real_part + partner_real)
            break
        partner = from_partner(jnp.stack([real_part, imag_part]), "tm", bit_index)
        base_real = jnp.where(upper_half, partner[0], real_part)
        base_imag = jnp.where(upper_half, partner[1], imag_part)
        scaled_real = jnp.where(upper_half, real_part, partner[0])
        scaled_imag = jnp.where(upper_half, imag_part, partner[1])
        prod_real = scaled_real * cosine - scaled_imag * sine_part
        prod_imag = scaled_real * sine_part + scaled_imag * cosine
        real_part = jnp.where(upper_half, base_real - prod_real, base_real + prod_real)
        imag_part = jnp.where(upper_half, base_imag - prod_imag, base_imag + prod_imag)
    smoothed = (real_part / total_len).reshape(channel_count, length)
    return smoothed


def solution(mesh):
    in_specs = (P("chan", "tm"), P(), P(None, "tm", None, "chan"), P("tm", "chan"))
    out_specs = P("chan", "tm")
    return jax.shard_map(
        per_device, mesh=mesh, in_specs=in_specs, out_specs=out_specs, check_vma=False
    )
```

```python
import math

import numpy as np

import jax
import jax.numpy as jnp
from jax import lax
from jax.experimental import pallas as pl
from jax.experimental.pallas import tpu as pltpu
from jax.sharding import PartitionSpec as P


def from_partner(block, axis, stride):
    count = lax.axis_size(axis)
    route = []
    for low in range(count):
        high = low | 1 << stride
        if high != low and high < count:
            route += [(low, high), (high, low)]
    return lax.ppermute(block, axis, route)


def twiddle(numer, length):
    angle = -2.0 * math.pi / length * numer.astype(jnp.float32)
    return (jnp.cos(angle), jnp.sin(angle))


def reverse_bits(value, bit_count):
    result = value * 0
    for bit_index in range(bit_count):
        result = result + value // (1 << bit_index) % 2 * (1 << bit_count - 1 - bit_index)
    return result


LANES = 128


def split_bf16(value):
    high = value.astype(jnp.bfloat16)
    return (high, (value - high.astype(jnp.float32)).astype(jnp.bfloat16))


def cdot(left_real, left_imag, right_real, right_imag):
    def dot(a, b):
        a_high, a_low = split_bf16(a)
        b_high, b_low = split_bf16(b)
        total = jnp.dot(a_high, b_low, preferred_element_type=jnp.float32)
        total = total + jnp.dot(a_low, b_high, preferred_element_type=jnp.float32)
        return total + jnp.dot(a_high, b_high, preferred_element_type=jnp.float32)

    return (
        dot(left_real, right_real) - dot(left_imag, right_imag),
        dot(left_real, right_imag) + dot(left_imag, right_real),
    )


def forward_kernel(xr_ref, xi_ref, twr_ref, twi_ref, kr_ref, ki_ref, t2r_ref, t2i_ref, wr_ref, wi_ref, yr_ref, yi_ref):
    own, outer, inner = xr_ref.shape
    xr = xr_ref[...]
    xi = xi_ref[...]
    position = lax.axis_index("tm")
    twr = twr_ref[position][None]
    twi = twi_ref[position][None]
    ur = (xr * twr - xi * twi).reshape(own * outer, inner)
    ui = (xr * twi + xi * twr).reshape(own * outer, inner)
    zr, zi = cdot(kr_ref[...], ki_ref[...], ur, ui)
    t2r = t2r_ref[...]
    t2i = t2i_ref[...]
    zr, zi = (zr * t2r - zi * t2i, zr * t2i + zi * t2r)
    yr, yi = cdot(zr, zi, wr_ref[...], wi_ref[...])
    yr_ref[...] = yr.reshape(own, outer, inner)
    yi_ref[...] = yi.reshape(own, outer, inner)


def inverse_kernel(win_ref, shift_ref, resp_ref, band_ref, twr_ref, twi_ref, kr_ref, ki_ref, t2r_ref, t2i_ref, wr_ref, wi_ref, xr_ref, xi_ref):
    own, outer, inner = xr_ref.shape
    band_width = resp_ref.shape[1]
    half_width = band_width // 2
    span = own + band_width - 1
    shift = shift_ref[...]
    masks = [shift == amount for amount in range(-half_width, half_width + 1)]
    moved = []
    for row in range(span):
        mr = jnp.zeros((outer, inner), jnp.float32)
        mi = jnp.zeros((outer, inner), jnp.float32)
        for index, amount in enumerate(range(-half_width, half_width + 1)):
            source = own + amount + row
            mr = jnp.where(masks[index], win_ref[0, source], mr)
            mi = jnp.where(masks[index], win_ref[1, source], mi)
        moved.append((mr, mi))
    rows_real = []
    rows_imag = []
    channel_all = band_ref.shape[0] // (2 * band_width)
    first = lax.axis_index("chan") * own
    for channel in range(own):
        acc_r = jnp.zeros((outer, inner), jnp.float32)
        acc_i = jnp.zeros((outer, inner), jnp.float32)
        for lag in range(band_width):
            br = band_ref[lag * channel_all + first + channel]
            bi = band_ref[(band_width + lag) * channel_all + first + channel]
            rr = resp_ref[0, lag]
            ri = resp_ref[1, lag]
            cr = br * rr - bi * ri
            ci = br * ri + bi * rr
            vr, vi = moved[channel + lag]
            acc_r = acc_r + cr * vr - ci * vi
            acc_i = acc_i + cr * vi + ci * vr
        rows_real.append(acc_r)
        rows_imag.append(acc_i)
    mr = jnp.concatenate(rows_real, axis=0)
    mi = jnp.concatenate(rows_imag, axis=0)
    yr, yi = cdot(mr, mi, wr_ref[...], -wi_ref[...])
    t2r = t2r_ref[...]
    t2i = -t2i_ref[...]
    yr, yi = (yr * t2r - yi * t2i, yr * t2i + yi * t2r)
    xr, xi = cdot(kr_ref[...], -ki_ref[...], yr, yi)
    xr = xr.reshape(own, outer, inner)
    xi = xi.reshape(own, outer, inner)
    position = lax.axis_index("tm")
    twr = twr_ref[position][None]
    twi = -twi_ref[position][None]
    xr_ref[...] = xr * twr - xi * twi
    xi_ref[...] = xr * twi + xi * twr


def dft_constant(length, numer):
    angle = -2.0 * np.pi / length * (numer % length)
    return (np.cos(angle).astype(np.float32), np.sin(angle).astype(np.float32))


def local_tables(own, outer, inner, blocks, levels):
    length = outer * inner
    total_len = length * blocks
    rows = np.arange(outer)[:, None]
    cols = np.arange(inner)[None, :]
    residues = [reverse_bits(position, levels) for position in range(blocks)]
    phase = np.stack([(rows * inner + cols) * residue for residue in residues])
    twr, twi = dft_constant(total_len, phase)
    small_r, small_i = dft_constant(outer, rows * np.arange(outer)[None, :])
    eye = np.eye(own, dtype=np.float32)
    kr = np.kron(eye, small_r)
    ki = np.kron(eye, small_i)
    t2r, t2i = dft_constant(length, rows * cols)
    t2r = np.tile(t2r, (own, 1))
    t2i = np.tile(t2i, (own, 1))
    wr, wi = dft_constant(inner, np.arange(inner)[:, None] * cols)
    return tuple(jnp.asarray(table) for table in (twr, twi, kr, ki, t2r, t2i, wr, wi))


def vmem_specs(count):
    return [pl.BlockSpec(memory_space=pltpu.VMEM)] * count


def forward_call(xr, xi, tables):
    shape = jax.ShapeDtypeStruct(xr.shape, jnp.float32)
    return pl.pallas_call(
        forward_kernel,
        out_shape=(shape, shape),
        in_specs=vmem_specs(2 + len(tables)),
        out_specs=tuple(vmem_specs(2)),
    )(xr, xi, *tables)


def inverse_call(window, shift, responses, band_flat, tables, own):
    shape = jax.ShapeDtypeStruct((own,) + window.shape[2:], jnp.float32)
    specs = vmem_specs(3) + [pl.BlockSpec(memory_space=pltpu.SMEM)] + vmem_specs(len(tables))
    return pl.pallas_call(
        inverse_kernel,
        out_shape=(shape, shape),
        in_specs=specs,
        out_specs=tuple(vmem_specs(2)),
    )(window, shift, responses, band_flat, *tables)


def from_offset(block, axis, delta):
    count = lax.axis_size(axis)
    return lax.ppermute(block, axis, [((i + delta) % count, i) for i in range(count)])


def per_device_body(signal, band, response, offsets):
    blocks = lax.axis_size("tm")
    levels = blocks.bit_length() - 1
    device_pos = lax.axis_index("tm")
    channel_count, length = signal.shape
    total_len = length * blocks
    real_part = signal
    imag_part = jnp.zeros_like(signal)
    for bit_index in range(levels - 1, -1, -1):
        half_span = 1 << bit_index
        upper_half = device_pos // half_span % 2 == 1
        cosine, sine_part = twiddle(device_pos % half_span, 2 * half_span)
        if bit_index == levels - 1:
            partner_real = from_partner(real_part, "tm", bit_index)
            diff_real = partner_real - real_part
            imag_part = jnp.where(upper_half, diff_real * sine_part, 0.0)
            real_part = jnp.where(upper_half, diff_real * cosine, real_part + partner_real)
            continue
        partner = from_partner(jnp.stack([real_part, imag_part]), "tm", bit_index)
        diff_real = partner[0] - real_part
        diff_imag = partner[1] - imag_part
        new_real = jnp.where(
            upper_half, diff_real * cosine - diff_imag * sine_part, real_part + partner[0]
        )
        new_imag = jnp.where(
            upper_half, diff_real * sine_part + diff_imag * cosine, imag_part + partner[1]
        )
        real_part, imag_part = (new_real, new_imag)
    inner = LANES
    outer = length // inner
    own = channel_count
    band_width = band.shape[1]
    half_width = band_width // 2
    channel_all = band.shape[2]
    tables = local_tables(own, outer, inner, blocks, levels)
    spec_real, spec_imag = forward_call(
        real_part.reshape(own, outer, inner), imag_part.reshape(own, outer, inner), tables
    )
    packed = jnp.concatenate(
        [response.reshape(2 * band_width, -1), offsets.reshape(1, -1).astype(jnp.float32)], axis=0
    )
    peers = lax.axis_size("chan")
    table = lax.all_to_all(
        jnp.broadcast_to(packed[None], (peers,) + packed.shape), "chan", 0, 0, tiled=True
    )
    entries = table.shape[1]
    table, _ = lax.optimization_barrier((table, spec_real))
    table = table.transpose(1, 0, 2).reshape(entries, inner, outer).transpose(0, 2, 1)
    responses = table[: 2 * band_width].reshape(2, band_width, outer, inner)
    shift = (table[2 * band_width].astype(jnp.int32) + half_width) % channel_all - half_width
    spectra = jnp.stack([spec_real, spec_imag])
    neighbours = [from_offset(spectra, "chan", delta) for delta in (-1, 1, 2, 3)]
    window = jnp.concatenate([neighbours[0], spectra] + neighbours[1:], axis=1)
    real_part, imag_part = inverse_call(window, shift, responses, band.reshape(-1), tables, own)
    real_part = real_part.reshape(own, length)
    imag_part = imag_part.reshape(own, length)
    for bit_index in range(levels):
        half_span = 1 << bit_index
        upper_half = device_pos // half_span % 2 == 1
        cosine, sine_part = twiddle(device_pos % half_span, 2 * half_span)
        sine_part = -sine_part
        if bit_index == levels - 1:
            own_prod = real_part * cosine - imag_part * sine_part
            partner_real = from_partner(jnp.where(upper_half, own_prod, real_part), "tm", bit_index)
            real_part = jnp.where(upper_half, partner_real - own_prod, real_part + partner_real)
            break
        partner = from_partner(jnp.stack([real_part, imag_part]), "tm", bit_index)
        base_real = jnp.where(upper_half, partner[0], real_part)
        base_imag = jnp.where(upper_half, partner[1], imag_part)
        scaled_real = jnp.where(upper_half, real_part, partner[0])
        scaled_imag = jnp.where(upper_half, imag_part, partner[1])
        prod_real = scaled_real * cosine - scaled_imag * sine_part
        prod_imag = scaled_real * sine_part + scaled_imag * cosine
        real_part = jnp.where(upper_half, base_real - prod_real, base_real + prod_real)
        imag_part = jnp.where(upper_half, base_imag - prod_imag, base_imag + prod_imag)
    smoothed = real_part / total_len
    return smoothed


def solution(mesh):
    in_specs = (P("chan", "tm"), P(), P(None, "tm", None, "chan"), P("tm", "chan"))
    out_specs = P("chan", "tm")
    return jax.shard_map(
        per_device_body, mesh=mesh, in_specs=in_specs, out_specs=out_specs, check_vma=False
    )
```

```python
import math

import numpy as np

import jax
import jax.numpy as jnp
from jax import lax
from jax.experimental import pallas as pl
from jax.experimental.pallas import tpu as pltpu
from jax.sharding import PartitionSpec as P


PRECISE = lax.Precision.HIGHEST


def from_partner(block, axis, stride):
    count = lax.axis_size(axis)
    route = []
    for low in range(count):
        high = low | 1 << stride
        if high != low and high < count:
            route += [(low, high), (high, low)]
    return lax.ppermute(block, axis, route)


def twiddle(numer, length):
    angle = -2.0 * math.pi / length * numer.astype(jnp.float32)
    return (jnp.cos(angle), jnp.sin(angle))


def reverse_bits(value, bit_count):
    result = value * 0
    for bit_index in range(bit_count):
        result = result + value // (1 << bit_index) % 2 * (1 << bit_count - 1 - bit_index)
    return result


LANES = 128


def cdot(left_real, left_imag, right_real, right_imag):
    def dot(a, b):
        return jnp.dot(a, b, precision=PRECISE, preferred_element_type=jnp.float32)

    return (
        dot(left_real, right_real) - dot(left_imag, right_imag),
        dot(left_real, right_imag) + dot(left_imag, right_real),
    )


def forward_kernel(xr_ref, xi_ref, twr_ref, twi_ref, kr_ref, ki_ref, t2r_ref, t2i_ref, wr_ref, wi_ref, yr_ref, yi_ref):
    own, outer, inner = xr_ref.shape
    xr = xr_ref[...]
    xi = xi_ref[...]
    position = lax.axis_index("tm")
    twr = twr_ref[position][None]
    twi = twi_ref[position][None]
    ur = (xr * twr - xi * twi).reshape(own * outer, inner)
    ui = (xr * twi + xi * twr).reshape(own * outer, inner)
    zr, zi = cdot(kr_ref[...], ki_ref[...], ur, ui)
    t2r = t2r_ref[...]
    t2i = t2i_ref[...]
    zr, zi = (zr * t2r - zi * t2i, zr * t2i + zi * t2r)
    yr, yi = cdot(zr, zi, wr_ref[...], wi_ref[...])
    yr_ref[...] = yr.reshape(own, outer, inner)
    yi_ref[...] = yi.reshape(own, outer, inner)


def inverse_kernel(win_ref, shift_ref, resp_ref, band_ref, twr_ref, twi_ref, kr_ref, ki_ref, t2r_ref, t2i_ref, wr_ref, wi_ref, xr_ref, xi_ref):
    own, outer, inner = xr_ref.shape
    band_width = resp_ref.shape[1]
    half_width = band_width // 2
    span = own + band_width - 1
    shift = shift_ref[...]
    masks = [shift == amount for amount in range(-half_width, half_width + 1)]
    moved = []
    for row in range(span):
        mr = jnp.zeros((outer, inner), jnp.float32)
        mi = jnp.zeros((outer, inner), jnp.float32)
        for index, amount in enumerate(range(-half_width, half_width + 1)):
            source = own + amount + row
            mr = jnp.where(masks[index], win_ref[0, source], mr)
            mi = jnp.where(masks[index], win_ref[1, source], mi)
        moved.append((mr, mi))
    rows_real = []
    rows_imag = []
    channel_all = band_ref.shape[0] // (2 * band_width)
    first = lax.axis_index("chan") * own
    for channel in range(own):
        acc_r = jnp.zeros((outer, inner), jnp.float32)
        acc_i = jnp.zeros((outer, inner), jnp.float32)
        for lag in range(band_width):
            br = band_ref[lag * channel_all + first + channel]
            bi = band_ref[(band_width + lag) * channel_all + first + channel]
            rr = resp_ref[0, lag]
            ri = resp_ref[1, lag]
            cr = br * rr - bi * ri
            ci = br * ri + bi * rr
            vr, vi = moved[channel + lag]
            acc_r = acc_r + cr * vr - ci * vi
            acc_i = acc_i + cr * vi + ci * vr
        rows_real.append(acc_r)
        rows_imag.append(acc_i)
    mr = jnp.concatenate(rows_real, axis=0)
    mi = jnp.concatenate(rows_imag, axis=0)
    yr, yi = cdot(mr, mi, wr_ref[...], -wi_ref[...])
    t2r = t2r_ref[...]
    t2i = -t2i_ref[...]
    yr, yi = (yr * t2r - yi * t2i, yr * t2i + yi * t2r)
    xr, xi = cdot(kr_ref[...], -ki_ref[...], yr, yi)
    xr = xr.reshape(own, outer, inner)
    xi = xi.reshape(own, outer, inner)
    position = lax.axis_index("tm")
    twr = twr_ref[position][None]
    twi = -twi_ref[position][None]
    xr_ref[...] = xr * twr - xi * twi
    xi_ref[...] = xr * twi + xi * twr


def dft_constant(length, numer):
    angle = -2.0 * np.pi / length * (numer % length)
    return (np.cos(angle).astype(np.float32), np.sin(angle).astype(np.float32))


def local_tables(own, outer, inner, blocks, levels):
    length = outer * inner
    total_len = length * blocks
    rows = np.arange(outer)[:, None]
    cols = np.arange(inner)[None, :]
    residues = [reverse_bits(position, levels) for position in range(blocks)]
    phase = np.stack([(rows * inner + cols) * residue for residue in residues])
    twr, twi = dft_constant(total_len, phase)
    small_r, small_i = dft_constant(outer, rows * np.arange(outer)[None, :])
    eye = np.eye(own, dtype=np.float32)
    kr = np.kron(eye, small_r)
    ki = np.kron(eye, small_i)
    t2r, t2i = dft_constant(length, rows * cols)
    t2r = np.tile(t2r, (own, 1))
    t2i = np.tile(t2i, (own, 1))
    wr, wi = dft_constant(inner, np.arange(inner)[:, None] * cols)
    return tuple(jnp.asarray(table) for table in (twr, twi, kr, ki, t2r, t2i, wr, wi))


def vmem_specs(count):
    return [pl.BlockSpec(memory_space=pltpu.VMEM)] * count


def forward_call(xr, xi, tables):
    shape = jax.ShapeDtypeStruct(xr.shape, jnp.float32)
    return pl.pallas_call(
        forward_kernel,
        out_shape=(shape, shape),
        in_specs=vmem_specs(2 + len(tables)),
        out_specs=tuple(vmem_specs(2)),
    )(xr, xi, *tables)


def inverse_call(window, shift, responses, band_flat, tables, own):
    shape = jax.ShapeDtypeStruct((own,) + window.shape[2:], jnp.float32)
    specs = vmem_specs(3) + [pl.BlockSpec(memory_space=pltpu.SMEM)] + vmem_specs(len(tables))
    return pl.pallas_call(
        inverse_kernel,
        out_shape=(shape, shape),
        in_specs=specs,
        out_specs=tuple(vmem_specs(2)),
    )(window, shift, responses, band_flat, *tables)


def from_offset(block, axis, delta):
    count = lax.axis_size(axis)
    return lax.ppermute(block, axis, [((i + delta) % count, i) for i in range(count)])


def per_device_body(signal, band, response, offsets):
    blocks = lax.axis_size("tm")
    levels = blocks.bit_length() - 1
    device_pos = lax.axis_index("tm")
    channel_count, length = signal.shape
    total_len = length * blocks
    real_part = signal
    imag_part = jnp.zeros_like(signal)
    for bit_index in range(levels - 1, -1, -1):
        half_span = 1 << bit_index
        upper_half = device_pos // half_span % 2 == 1
        cosine, sine_part = twiddle(device_pos % half_span, 2 * half_span)
        if bit_index == levels - 1:
            partner_real = from_partner(real_part, "tm", bit_index)
            diff_real = partner_real - real_part
            imag_part = jnp.where(upper_half, diff_real * sine_part, 0.0)
            real_part = jnp.where(upper_half, diff_real * cosine, real_part + partner_real)
            continue
        partner = from_partner(jnp.stack([real_part, imag_part]), "tm", bit_index)
        diff_real = partner[0] - real_part
        diff_imag = partner[1] - imag_part
        new_real = jnp.where(
            upper_half, diff_real * cosine - diff_imag * sine_part, real_part + partner[0]
        )
        new_imag = jnp.where(
            upper_half, diff_real * sine_part + diff_imag * cosine, imag_part + partner[1]
        )
        real_part, imag_part = (new_real, new_imag)
    inner = LANES
    outer = length // inner
    own = channel_count
    band_width = band.shape[1]
    half_width = band_width // 2
    channel_all = band.shape[2]
    tables = local_tables(own, outer, inner, blocks, levels)
    spec_real, spec_imag = forward_call(
        real_part.reshape(own, outer, inner), imag_part.reshape(own, outer, inner), tables
    )
    packed = jnp.concatenate(
        [response.reshape(2 * band_width, -1), offsets.reshape(1, -1).astype(jnp.float32)], axis=0
    )
    peers = lax.axis_size("chan")
    table = lax.all_to_all(
        jnp.broadcast_to(packed[None], (peers,) + packed.shape), "chan", 0, 0, tiled=True
    )
    entries = table.shape[1]
    table, _ = lax.optimization_barrier((table, spec_real))
    table = table.transpose(1, 0, 2).reshape(entries, inner, outer).transpose(0, 2, 1)
    responses = table[: 2 * band_width].reshape(2, band_width, outer, inner)
    shift = (table[2 * band_width].astype(jnp.int32) + half_width) % channel_all - half_width
    spectra = jnp.stack([spec_real, spec_imag])
    neighbours = [from_offset(spectra, "chan", delta) for delta in (-1, 1, 2, 3)]
    window = jnp.concatenate([neighbours[0], spectra] + neighbours[1:], axis=1)
    real_part, imag_part = inverse_call(window, shift, responses, band.reshape(-1), tables, own)
    real_part = real_part.reshape(own, length)
    imag_part = imag_part.reshape(own, length)
    for bit_index in range(levels):
        half_span = 1 << bit_index
        upper_half = device_pos // half_span % 2 == 1
        cosine, sine_part = twiddle(device_pos % half_span, 2 * half_span)
        sine_part = -sine_part
        if bit_index == levels - 1:
            own_prod = real_part * cosine - imag_part * sine_part
            partner_real = from_partner(jnp.where(upper_half, own_prod, real_part), "tm", bit_index)
            real_part = jnp.where(upper_half, partner_real - own_prod, real_part + partner_real)
            break
        partner = from_partner(jnp.stack([real_part, imag_part]), "tm", bit_index)
        base_real = jnp.where(upper_half, partner[0], real_part)
        base_imag = jnp.where(upper_half, partner[1], imag_part)
        scaled_real = jnp.where(upper_half, real_part, partner[0])
        scaled_imag = jnp.where(upper_half, imag_part, partner[1])
        prod_real = scaled_real * cosine - scaled_imag * sine_part
        prod_imag = scaled_real * sine_part + scaled_imag * cosine
        real_part = jnp.where(upper_half, base_real - prod_real, base_real + prod_real)
        imag_part = jnp.where(upper_half, base_imag - prod_imag, base_imag + prod_imag)
    smoothed = real_part / total_len
    return smoothed


def solution(mesh):
    in_specs = (P("chan", "tm"), P(), P(None, "tm", None, "chan"), P("tm", "chan"))
    out_specs = P("chan", "tm")
    return jax.shard_map(
        per_device_body, mesh=mesh, in_specs=in_specs, out_specs=out_specs, check_vma=False
    )
```

```python
import math

import numpy as np

import jax
import jax.numpy as jnp
from jax import lax
from jax.experimental import pallas as pl
from jax.experimental.pallas import tpu as pltpu
from jax.sharding import PartitionSpec as P


PRECISE = lax.Precision.HIGHEST


def from_partner(block, axis, stride):
    count = lax.axis_size(axis)
    route = []
    for low in range(count):
        high = low | 1 << stride
        if high != low and high < count:
            route += [(low, high), (high, low)]
    return lax.ppermute(block, axis, route)


def twiddle(numer, length):
    angle = -2.0 * math.pi / length * numer.astype(jnp.float32)
    return (jnp.cos(angle), jnp.sin(angle))


def reverse_bits(value, bit_count):
    result = value * 0
    for bit_index in range(bit_count):
        result = result + value // (1 << bit_index) % 2 * (1 << bit_count - 1 - bit_index)
    return result


LANES = 128


def cdot(left_real, left_imag, right_real, right_imag):
    def dot(a, b):
        return jnp.dot(a, b, precision=PRECISE, preferred_element_type=jnp.float32)

    return (
        dot(left_real, right_real) - dot(left_imag, right_imag),
        dot(left_real, right_imag) + dot(left_imag, right_real),
    )


def forward_kernel(xr_ref, xi_ref, twr_ref, twi_ref, kr_ref, ki_ref, t2r_ref, t2i_ref, wr_ref, wi_ref, y_ref):
    own, outer, inner = xr_ref.shape
    xr = xr_ref[...]
    xi = xi_ref[...]
    position = lax.axis_index("tm")
    twr = twr_ref[position][None]
    twi = twi_ref[position][None]
    ur = (xr * twr - xi * twi).reshape(own * outer, inner)
    ui = (xr * twi + xi * twr).reshape(own * outer, inner)
    zr, zi = cdot(kr_ref[...], ki_ref[...], ur, ui)
    t2r = t2r_ref[...]
    t2i = t2i_ref[...]
    zr, zi = (zr * t2r - zi * t2i, zr * t2i + zi * t2r)
    yr, yi = cdot(zr, zi, wr_ref[...], wi_ref[...])
    y_ref[0] = yr.reshape(own, outer, inner)
    y_ref[1] = yi.reshape(own, outer, inner)


def inverse_kernel(win_ref, shift_ref, resp_ref, band_ref, twr_ref, twi_ref, kr_ref, ki_ref, t2r_ref, t2i_ref, wr_ref, wi_ref, xr_ref, xi_ref):
    own, outer, inner = xr_ref.shape
    band_width = resp_ref.shape[1]
    half_width = band_width // 2
    span = own + band_width - 1
    shift = shift_ref[...]
    masks = [shift == amount for amount in range(-half_width, half_width + 1)]
    moved = []
    for row in range(span):
        mr = jnp.zeros((outer, inner), jnp.float32)
        mi = jnp.zeros((outer, inner), jnp.float32)
        for index, amount in enumerate(range(-half_width, half_width + 1)):
            source = own + amount + row
            mr = jnp.where(masks[index], win_ref[0, source], mr)
            mi = jnp.where(masks[index], win_ref[1, source], mi)
        moved.append((mr, mi))
    rows_real = []
    rows_imag = []
    channel_all = band_ref.shape[0] // (2 * band_width)
    first = lax.axis_index("chan") * own
    for channel in range(own):
        acc_r = jnp.zeros((outer, inner), jnp.float32)
        acc_i = jnp.zeros((outer, inner), jnp.float32)
        for lag in range(band_width):
            br = band_ref[lag * channel_all + first + channel]
            bi = band_ref[(band_width + lag) * channel_all + first + channel]
            rr = resp_ref[0, lag]
            ri = resp_ref[1, lag]
            cr = br * rr - bi * ri
            ci = br * ri + bi * rr
            vr, vi = moved[channel + lag]
            acc_r = acc_r + cr * vr - ci * vi
            acc_i = acc_i + cr * vi + ci * vr
        rows_real.append(acc_r)
        rows_imag.append(acc_i)
    mr = jnp.concatenate(rows_real, axis=0)
    mi = jnp.concatenate(rows_imag, axis=0)
    yr, yi = cdot(mr, mi, wr_ref[...], -wi_ref[...])
    t2r = t2r_ref[...]
    t2i = -t2i_ref[...]
    yr, yi = (yr * t2r - yi * t2i, yr * t2i + yi * t2r)
    xr, xi = cdot(kr_ref[...], -ki_ref[...], yr, yi)
    xr = xr.reshape(own, outer, inner)
    xi = xi.reshape(own, outer, inner)
    position = lax.axis_index("tm")
    twr = twr_ref[position][None]
    twi = -twi_ref[position][None]
    xr_ref[...] = xr * twr - xi * twi
    xi_ref[...] = xr * twi + xi * twr


def dft_constant(length, numer):
    angle = -2.0 * np.pi / length * (numer % length)
    return (np.cos(angle).astype(np.float32), np.sin(angle).astype(np.float32))


def local_tables(own, outer, inner, blocks, levels):
    length = outer * inner
    total_len = length * blocks
    rows = np.arange(outer)[:, None]
    cols = np.arange(inner)[None, :]
    residues = [reverse_bits(position, levels) for position in range(blocks)]
    phase = np.stack([(rows * inner + cols) * residue for residue in residues])
    twr, twi = dft_constant(total_len, phase)
    small_r, small_i = dft_constant(outer, rows * np.arange(outer)[None, :])
    eye = np.eye(own, dtype=np.float32)
    kr = np.kron(eye, small_r)
    ki = np.kron(eye, small_i)
    t2r, t2i = dft_constant(length, rows * cols)
    t2r = np.tile(t2r, (own, 1))
    t2i = np.tile(t2i, (own, 1))
    wr, wi = dft_constant(inner, np.arange(inner)[:, None] * cols)
    return tuple(jnp.asarray(table) for table in (twr, twi, kr, ki, t2r, t2i, wr, wi))


def vmem_specs(count):
    return [pl.BlockSpec(memory_space=pltpu.VMEM)] * count


def forward_call(xr, xi, tables):
    shape = jax.ShapeDtypeStruct((2,) + xr.shape, jnp.float32)
    return pl.pallas_call(
        forward_kernel,
        out_shape=shape,
        in_specs=vmem_specs(2 + len(tables)),
        out_specs=pl.BlockSpec(memory_space=pltpu.VMEM),
        compiler_params=pltpu.CompilerParams(allow_input_fusion=[True, True] + [False] * len(tables)),
    )(xr, xi, *tables)


def inverse_call(window, shift, responses, band_flat, tables, own):
    shape = jax.ShapeDtypeStruct((own,) + window.shape[2:], jnp.float32)
    specs = vmem_specs(3) + [pl.BlockSpec(memory_space=pltpu.SMEM)] + vmem_specs(len(tables))
    return pl.pallas_call(
        inverse_kernel,
        out_shape=(shape, shape),
        in_specs=specs,
        out_specs=tuple(vmem_specs(2)),
    )(window, shift, responses, band_flat, *tables)


def from_offset(block, axis, delta):
    count = lax.axis_size(axis)
    return lax.ppermute(block, axis, [((i + delta) % count, i) for i in range(count)])


def per_device_body(signal, band, response, offsets):
    blocks = lax.axis_size("tm")
    levels = blocks.bit_length() - 1
    device_pos = lax.axis_index("tm")
    channel_count, length = signal.shape
    total_len = length * blocks
    real_part = signal
    imag_part = jnp.zeros_like(signal)
    for bit_index in range(levels - 1, -1, -1):
        half_span = 1 << bit_index
        upper_half = device_pos // half_span % 2 == 1
        cosine, sine_part = twiddle(device_pos % half_span, 2 * half_span)
        if bit_index == levels - 1:
            partner_real = from_partner(real_part, "tm", bit_index)
            diff_real = partner_real - real_part
            imag_part = jnp.where(upper_half, diff_real * sine_part, 0.0)
            real_part = jnp.where(upper_half, diff_real * cosine, real_part + partner_real)
            continue
        partner = from_partner(jnp.stack([real_part, imag_part]), "tm", bit_index)
        diff_real = partner[0] - real_part
        diff_imag = partner[1] - imag_part
        new_real = jnp.where(
            upper_half, diff_real * cosine - diff_imag * sine_part, real_part + partner[0]
        )
        new_imag = jnp.where(
            upper_half, diff_real * sine_part + diff_imag * cosine, imag_part + partner[1]
        )
        real_part, imag_part = (new_real, new_imag)
    inner = LANES
    outer = length // inner
    own = channel_count
    band_width = band.shape[1]
    half_width = band_width // 2
    channel_all = band.shape[2]
    tables = local_tables(own, outer, inner, blocks, levels)
    spectra = forward_call(
        real_part.reshape(own, outer, inner), imag_part.reshape(own, outer, inner), tables
    )
    packed = jnp.concatenate(
        [response.reshape(2 * band_width, -1), offsets.reshape(1, -1).astype(jnp.float32)], axis=0
    )
    peers = lax.axis_size("chan")
    table = lax.all_to_all(
        jnp.broadcast_to(packed[None], (peers,) + packed.shape), "chan", 0, 0, tiled=True
    )
    entries = table.shape[1]
    table, _ = lax.optimization_barrier((table, spectra))
    table = table.transpose(1, 0, 2).reshape(entries, inner, outer).transpose(0, 2, 1)
    responses = table[: 2 * band_width].reshape(2, band_width, outer, inner)
    shift = (table[2 * band_width].astype(jnp.int32) + half_width) % channel_all - half_width
    neighbours = [from_offset(spectra, "chan", delta) for delta in (-1, 1, 2, 3)]
    window = jnp.concatenate([neighbours[0], spectra] + neighbours[1:], axis=1)
    real_part, imag_part = inverse_call(window, shift, responses, band.reshape(-1), tables, own)
    real_part = real_part.reshape(own, length)
    imag_part = imag_part.reshape(own, length)
    for bit_index in range(levels):
        half_span = 1 << bit_index
        upper_half = device_pos // half_span % 2 == 1
        cosine, sine_part = twiddle(device_pos % half_span, 2 * half_span)
        sine_part = -sine_part
        if bit_index == levels - 1:
            own_prod = real_part * cosine - imag_part * sine_part
            partner_real = from_partner(jnp.where(upper_half, own_prod, real_part), "tm", bit_index)
            real_part = jnp.where(upper_half, partner_real - own_prod, real_part + partner_real)
            break
        partner = from_partner(jnp.stack([real_part, imag_part]), "tm", bit_index)
        base_real = jnp.where(upper_half, partner[0], real_part)
        base_imag = jnp.where(upper_half, partner[1], imag_part)
        scaled_real = jnp.where(upper_half, real_part, partner[0])
        scaled_imag = jnp.where(upper_half, imag_part, partner[1])
        prod_real = scaled_real * cosine - scaled_imag * sine_part
        prod_imag = scaled_real * sine_part + scaled_imag * cosine
        real_part = jnp.where(upper_half, base_real - prod_real, base_real + prod_real)
        imag_part = jnp.where(upper_half, base_imag - prod_imag, base_imag + prod_imag)
    smoothed = real_part / total_len
    return smoothed


def solution(mesh):
    in_specs = (P("chan", "tm"), P(), P(None, "tm", None, "chan"), P("tm", "chan"))
    out_specs = P("chan", "tm")
    return jax.shard_map(
        per_device_body, mesh=mesh, in_specs=in_specs, out_specs=out_specs, check_vma=False
    )
```
